128 devices in a mesh: phase: 16 (over x_lo, y, core), space: 8 (over z, x_hi).
Axes of the slice: x: 4 (x_hi: 2, x_lo: 2; x = x_hi * 2 + x_lo), y: 4, z: 4, core: 2. Of those that a mesh axis runs over, the one named last changes fastest.
Arguments:
- volume: bfloat16 [16, 32, 4, 32, 256], P('phase', 'space'), may hold values from -6 to 6
- gain_first: float32 [256], replicated, may hold values from 0.25 to 1.75
- phase_qkv: bfloat16 [256, 768], replicated, may hold values from -0.375 to 0.375
- phase_out: bfloat16 [256, 256], replicated, may hold values from -0.375 to 0.375
- bin_phase: int32 [16], replicated, may hold values from 0 to 15, each once
- phase_bias: float32 [8, 16], replicated, may hold values from -4 to 304
- gain_second: float32 [256], replicated, may hold values from 0.25 to 1.75
- window_qkv: bfloat16 [256, 768], replicated, may hold values from -0.375 to 0.375
- window_out: bfloat16 [256, 256], replicated, may hold values from -0.375 to 0.375
- window_corner: int32 [8, 3], replicated, may hold values from -3 to 0
- window_bias: float32 [8, 64], replicated, may hold values from -4 to 304
- gain_third: float32 [256], replicated, may hold values from 0.25 to 1.75
- mlp_up: bfloat16 [256, 1024], replicated, may hold values from -0.375 to 0.375
- mlp_down: bfloat16 [1024, 256], replicated, may hold values from -0.1875 to 0.1875
Outputs:
- layer_out: bfloat16 [16, 32, 4, 32, 256], P('phase', 'space')
The draws below stay inside these ranges and needn't reach their ends.
Inputs may be any that keep to these rules, and one draw needn't show every extreme that they name: `bin_phase`: each phase 0 to 15 is held by exactly one bin. `window_corner`: head h's window covers corner to corner + 3 along each dimension.
All inputs are finite; a program needn't handle non-finite values.
Results may differ from the reference program's by a relative error of at most 0.012.
Values may be sent and summed in bfloat16 or wider, within the bound.
A program may use at most 128 MiB of HBM per device.

```python
import math
import jax
import jax.numpy as jnp
from jax import lax

D = 256
HEADS = 8
FF = 1024
GX = 4
GY = 32
BINS = 16
NZ = 32


def bias_table(key, row_count, col_count):
    fourth = jax.random.fold_in(key, 3)
    return jnp.clip(jax.random.normal(fourth, (row_count, col_count)), -4.0, 4.0)


def draw_phase_bias(key, part):
    return bias_table(jax.random.fold_in(key, 11), HEADS, BINS).astype(jnp.float32)


def draw_window_bias(key, part):
    return bias_table(jax.random.fold_in(key, 23), HEADS, 64).astype(jnp.float32)


def with_ends(array, key, least, largest):
    place = [jax.random.randint(jax.random.fold_in(key, axis), (), 0, length) for axis, length in enumerate(array.shape)]
    longest = array.shape.index(max(array.shape))
    beside = place[:longest] + [(place[longest] + 1) % array.shape[longest]] + place[longest + 1:]
    return array.at[tuple(place)].set(least).at[tuple(beside)].set(largest)


def block_scale(rng, extent, cuts, low, high):
    level, own = 1.0, jax.random.fold_in(rng, 6)
    for axis_at, blocks in cuts:
        heights = jnp.exp(jax.random.uniform(jax.random.fold_in(own, axis_at), (blocks,), jnp.float32, low / len(cuts), high / len(cuts)))
        level = level * jnp.repeat(heights, extent[axis_at] // blocks).reshape([-1 if axis == axis_at else 1 for axis in range(len(extent))])
    return level


def gaussian(stream_key, dims, scale, reach, shards=(), kind=jnp.bfloat16):
    loudness = block_scale(stream_key, dims, shards, -0.22, 0.18) if shards else 1.0
    entries = jax.random.normal(stream_key, dims, jnp.float32) * scale * loudness
    return jnp.minimum(jnp.maximum(entries, -reach), reach).astype(kind)


def setup_inputs(seed: int = 0) -> dict:
    splits = jax.random.split(jax.random.key(seed), 15)
    volume = gaussian(splits[0], (BINS, NZ, GX, GY, D), 1.0, 6.0, ((0, 16), (1, 8)))
    gain_first = jnp.clip(1.0 + 0.15 * jax.random.normal(splits[1], (D,), jnp.float32), 0.25, 1.75)
    phase_qkv = gaussian(splits[2], (D, 3 * D), D ** -0.5, 0.375)
    phase_out = gaussian(splits[3], (D, D), D ** -0.5, 0.375)
    bin_phase = jax.random.permutation(splits[4], BINS).astype(jnp.int32)
    phase_bias = draw_phase_bias(jax.random.fold_in(splits[14], 71), 0)
    gain_second = jnp.clip(1.0 + 0.15 * jax.random.normal(splits[6], (D,), jnp.float32), 0.25, 1.75)
    window_qkv = gaussian(splits[7], (D, 3 * D), D ** -0.5, 0.375)
    window_out = gaussian(splits[8], (D, D), D ** -0.5, 0.375)
    window_corner = with_ends(jax.random.randint(splits[9], (HEADS, 3), -3, 1), jax.random.fold_in(splits[9], 1), -3, 0).astype(jnp.int32)
    window_bias = draw_window_bias(jax.random.fold_in(splits[14], 71), 0)
    gain_third = jnp.clip(1.0 + 0.15 * jax.random.normal(splits[11], (D,), jnp.float32), 0.25, 1.75)
    mlp_up = gaussian(splits[12], (D, FF), D ** -0.5, 0.375)
    mlp_down = gaussian(splits[13], (FF, D), FF ** -0.5, 0.1875)
    return {"volume": volume, "gain_first": gain_first, "phase_qkv": phase_qkv, "phase_out": phase_out, "bin_phase": bin_phase, "phase_bias": phase_bias, "gain_second": gain_second, "window_qkv": window_qkv, "window_out": window_out, "window_corner": window_corner, "window_bias": window_bias, "gain_third": gain_third, "mlp_up": mlp_up, "mlp_down": mlp_down}


EPSILON = 1e-06

def rms_norm(values, gain):
    mean_sq = lax.optimization_barrier(jnp.mean(values * values, axis=-1, keepdims=True))
    return values * lax.rsqrt(mean_sq + EPSILON) * gain

def head_matrix(model_width, head_count):
    column = lax.broadcasted_iota(jnp.int32, (model_width, head_count), 0) // (model_width // head_count)
    target = lax.broadcasted_iota(jnp.int32, (model_width, head_count), 1)
    return (column == target).astype(jnp.float32)

def window_attend(queries, keys_ext, window_corner, window_bias, z_first, depth):
    planes, extent_x, extent_y, model_width = queries.shape
    head_count = window_corner.shape[0]
    head_dim = model_width // head_count
    score_scale = 1.0 / math.sqrt(head_dim)
    padded = jnp.pad(keys_ext, ((0, 0), (3, 3), (3, 3), (0, 0)))
    corner = window_corner.astype(jnp.int32)
    key_parts = []
    value_parts = []
    for member in range(head_count):
        anchor = ((corner[member, 0] + 3).astype(jnp.int32), (corner[member, 1] + 3).astype(jnp.int32), (corner[member, 2] + 3).astype(jnp.int32))
        key_start = jnp.asarray(member * head_dim, dtype=jnp.int32)
        value_start = jnp.asarray(model_width + member * head_dim, dtype=jnp.int32)
        sizes_here = (planes + 3, extent_x + 3, extent_y + 3, head_dim)
        key_parts.append(lax.dynamic_slice(padded, anchor + (key_start,), sizes_here))
        value_parts.append(lax.dynamic_slice(padded, anchor + (value_start,), sizes_here))
    key_shift = jnp.concatenate(key_parts, axis=3)
    value_shift = jnp.concatenate(value_parts, axis=3)
    summer = head_matrix(model_width, head_count)
    z_index = z_first + lax.broadcasted_iota(jnp.int32, (planes, 1, 1, 1), 0) + corner[:, 0]
    x_index = lax.broadcasted_iota(jnp.int32, (1, extent_x, 1, 1), 1) + corner[:, 1]
    y_index = lax.broadcasted_iota(jnp.int32, (1, 1, extent_y, 1), 2) + corner[:, 2]
    query_float = queries.astype(jnp.float32)
    score_list = []
    for neighbor in range(64):
        step_z, step_x, step_y = (neighbor // 16, neighbor // 4 % 4, neighbor % 4)
        keys_here = key_shift[step_z:step_z + planes, step_x:step_x + extent_x, step_y:step_y + extent_y]
        raw_score = jnp.dot(query_float * keys_here.astype(jnp.float32), summer, precision=lax.Precision.HIGHEST) * score_scale + window_bias[:, neighbor]
        inside = (z_index + step_z >= 0) & (z_index + step_z < depth) & (x_index + step_x >= 0) & (x_index + step_x < extent_x) & (y_index + step_y >= 0) & (y_index + step_y < extent_y)
        score_list.append(jnp.where(inside, raw_score, -1e+30))
    weights = jax.nn.softmax(jnp.stack(score_list), axis=0).astype(jnp.bfloat16)
    accumulated = jnp.zeros(queries.shape, jnp.float32)
    for neighbor in range(64):
        step_z, step_x, step_y = (neighbor // 16, neighbor // 4 % 4, neighbor % 4)
        values_here = value_shift[step_z:step_z + planes, step_x:step_x + extent_x, step_y:step_y + extent_y]
        spread = jnp.dot(weights[neighbor].astype(jnp.float32), summer.T, precision=lax.Precision.HIGHEST)
        accumulated = accumulated + spread * values_here.astype(jnp.float32)
    return accumulated.astype(jnp.bfloat16)

def reference(volume, gain_first, phase_qkv, phase_out, bin_phase, phase_bias, gain_second, window_qkv, window_out, window_corner, window_bias, gain_third, mlp_up, mlp_down):
    bin_count, depth, extent_x, extent_y, model_width = volume.shape
    head_count = window_corner.shape[0]
    head_dim = model_width // head_count
    score_scale = 1.0 / math.sqrt(head_dim)
    stream = volume.astype(jnp.float32).reshape(-1, model_width)
    normed_one = rms_norm(stream, gain_first).astype(jnp.bfloat16)
    triple = jnp.dot(normed_one, phase_qkv, preferred_element_type=jnp.float32).astype(jnp.bfloat16)
    triple = triple.reshape(bin_count, -1, 3 * model_width)
    token_count = triple.shape[1]
    queries = triple[..., :model_width].astype(jnp.float32).reshape(bin_count, token_count, head_count, head_dim)
    key_all = triple[..., model_width:2 * model_width].astype(jnp.float32).reshape(bin_count, token_count, head_count, head_dim)
    value_all = triple[..., 2 * model_width:].astype(jnp.float32).reshape(bin_count, token_count, head_count, head_dim)
    phase_gap = (bin_phase[None, :] - bin_phase[:, None]) % bin_count
    onehot = (phase_gap[:, :, None] == jnp.arange(bin_count, dtype=jnp.int32)[None, None, :]).astype(jnp.float32)
    bias_all = jnp.einsum('bck,hk->bch', onehot, phase_bias.astype(jnp.float32), precision=lax.Precision.HIGHEST)

    def per_bin(member):
        query_bin, bias_bin = member
        scores = jnp.einsum('phd,cphd->chp', query_bin, key_all) * score_scale + bias_bin[:, :, None]
        rounded = jax.nn.softmax(scores, axis=0).astype(jnp.bfloat16)
        rounded = lax.optimization_barrier(rounded)
        return jnp.einsum('chp,cphd->phd', rounded.astype(jnp.float32), value_all).astype(jnp.bfloat16)
    phase_mixed = lax.map(per_bin, (queries, bias_all)).reshape(-1, model_width)
    residual_one = stream + jnp.dot(phase_mixed, phase_out, preferred_element_type=jnp.float32)
    normed_two = rms_norm(residual_one, gain_second).astype(jnp.bfloat16)
    triple_two = jnp.dot(normed_two, window_qkv, preferred_element_type=jnp.float32).astype(jnp.bfloat16)
    triple_two = triple_two.reshape(bin_count, depth, extent_x, extent_y, 3 * model_width)

    def per_volume(block):
        keys_ext = jnp.pad(block[..., model_width:], ((3, 3), (0, 0), (0, 0), (0, 0)))
        return window_attend(block[..., :model_width], keys_ext, window_corner, window_bias, 0, depth)
    windowed = lax.map(per_volume, triple_two).reshape(-1, model_width)
    residual_two = residual_one + jnp.dot(windowed, window_out, preferred_element_type=jnp.float32)
    normed_three = rms_norm(residual_two, gain_third).astype(jnp.bfloat16)
    hidden = jax.nn.gelu(jnp.dot(normed_three, mlp_up, preferred_element_type=jnp.float32), approximate=True).astype(jnp.bfloat16)
    layer_out = residual_two + jnp.dot(hidden, mlp_down, preferred_element_type=jnp.float32)
    return layer_out.astype(jnp.bfloat16).reshape(volume.shape)
```

```python
import functools
import math

import jax
import jax.numpy as jnp
from jax import lax
from jax.experimental import pallas as pl
from jax.experimental.pallas import tpu as pltpu
from jax.sharding import PartitionSpec as P

MESH = pl.DeviceIdType.MESH
EPSILON = 1e-06
MASKED = -1e30
F32 = jnp.float32
BF16 = jnp.bfloat16


def normed(values, gain):
    mean_sq = jnp.mean(values * values, axis=-1, keepdims=True)
    return (values * lax.rsqrt(mean_sq + EPSILON) * gain).astype(BF16)


def dot(a, b):
    return jnp.dot(a, b, preferred_element_type=F32)


def dot_t(a, b):
    return lax.dot_general(a, b, (((1,), (1,)), ((), ())), preferred_element_type=F32)


def kernel(
    bins,
    slabs,
    bin_phase,
    phase_bias,
    corner,
    window_bias,
    gain1,
    gain2,
    gain3,
    vol,
    w_qkv1_hbm,
    w_out1_hbm,
    w_qkv2_hbm,
    w_out2_hbm,
    w_up_hbm,
    w_down_hbm,
    out,
    w_qkv1,
    w_out1,
    w_qkv2,
    w_out2,
    w_up,
    w_down,
    got,
    sent,
    ext,
    queries,
    keys,
    values,
    phase_table,
    window_table,
    weight_sem,
    local_sem,
    send_sem,
    recv_sem,
):
    me = lax.axis_index("phase")
    slab = lax.axis_index("space")
    planes, blocks = vol.shape[0], vol.shape[1]
    heads = 8
    scale = 1.0 / math.sqrt(32)
    unscale = math.sqrt(32)
    rate = scale * math.log2(math.e)
    reach = planes - 1
    not_first = slab > 0
    not_last = slab < slabs - 1

    weight_copies = [
        pltpu.make_async_copy(source, target, weight_sem.at[i])
        for i, (source, target) in enumerate(
            [
                (w_qkv1_hbm, w_qkv1),
                (w_out1_hbm, w_out1),
                (w_qkv2_hbm, w_qkv2),
                (w_out2_hbm, w_out2),
                (w_up_hbm, w_up),
                (w_down_hbm, w_down),
            ]
        )
    ]
    for copy in weight_copies:
        copy.start()
    own_in = pltpu.make_async_copy(vol.at[:, me], got.at[:, me], local_sem.at[0])
    own_in.start()

    barrier = pltpu.get_barrier_semaphore()

    @pl.loop(1, bins)
    def _(i):
        pl.semaphore_signal(
            barrier, inc=1, device_id={"phase": lax.rem(me + i, bins)}, device_id_type=MESH
        )

    @pl.when(not_first)
    def _():
        @pl.loop(0, bins)
        def _(i):
            pl.semaphore_signal(
                barrier,
                inc=1,
                device_id={"phase": lax.rem(me + i, bins), "space": slab - 1},
                device_id_type=MESH,
            )

    @pl.when(not_last)
    def _():
        @pl.loop(0, bins)
        def _(i):
            pl.semaphore_signal(
                barrier,
                inc=1,
                device_id={"phase": lax.rem(me + i, bins), "space": slab + 1},
                device_id_type=MESH,
            )

    lane = lax.broadcasted_iota(jnp.int32, (1, 128), 1)

    lane_bin = lax.broadcasted_iota(jnp.int32, (bins, 128), 1) // 8
    row_bin = lax.broadcasted_iota(jnp.int32, (bins, 128), 0)
    there = jnp.zeros((bins, 128), jnp.int32)
    here = jnp.zeros((bins, 128), jnp.int32)
    for c in range(bins):
        there = jnp.where(lane_bin == c, bin_phase[c], there)
        here = jnp.where(row_bin == c, bin_phase[c], here)
    gap = there - here
    gap = jnp.where(gap < 0, gap + bins, gap)
    same = (
        lax.broadcasted_iota(jnp.int32, (bins, 8, 128), 1)
        == lax.broadcasted_iota(jnp.int32, (bins, 8, 128), 2) % 8
    )
    for h in range(heads):
        level = jnp.zeros((bins, 128), F32)
        for k in range(bins):
            level = jnp.where(gap == k, phase_bias[h, k] * unscale, level)
        table = jnp.where(same, jnp.broadcast_to(level[:, None, :], (bins, 8, 128)), MASKED)
        phase_table[h] = table.reshape(128, 128)

    row = lax.broadcasted_iota(jnp.int32, (128, 128), 0)
    column = lax.broadcasted_iota(jnp.int32, (128, 128), 1)
    step_x = column // 32 - row // 32
    step_y = column % 32 - row % 32
    window_table[4 * heads] = jnp.full((128, 128), MASKED, F32)

    @pl.loop(0, heads)
    def _(h):
        b = step_x - corner[h, 1]
        c = step_y - corner[h, 2]
        inside = (b >= 0) & (b < 4) & (c >= 0) & (c < 4)
        code = jnp.where(inside, 4 * b + c, 16)
        for a in range(4):
            table = jnp.full((128, 128), MASKED, F32)
            for j in range(16):
                table = jnp.where(code == j, window_bias[h, 16 * a + j] * unscale, table)
            window_table[4 * h + a] = table

    @pl.when(jnp.logical_not(not_first))
    def _():
        ext[0:reach] = jnp.zeros((reach, blocks, 8, 256), BF16)

    @pl.when(jnp.logical_not(not_last))
    def _():
        ext[reach + planes :] = jnp.zeros((reach, blocks, 8, 256), BF16)

    sides = not_first.astype(jnp.int32) + not_last.astype(jnp.int32)
    pl.semaphore_wait(barrier, bins - 1 + bins * sides)

    @pl.loop(1, bins)
    def _(i):
        peer = lax.rem(me + i, bins)
        pltpu.make_async_remote_copy(
            src_ref=vol.at[:, peer],
            dst_ref=got.at[:, me],
            send_sem=send_sem.at[0],
            recv_sem=recv_sem.at[0],
            device_id={"phase": peer},
            device_id_type=MESH,
        ).start()

    own_in.wait()
    weight_copies[0].wait()
    weight_copies[1].wait()
    others = got.at[:, pl.ds(0, bins - 1)]
    pltpu.make_async_copy(others, others, recv_sem.at[0]).wait()

    ones = jnp.ones((128, 128), BF16)
    head_lanes = [(lane // 32) == i for i in range(4)]
    head_keep = [m.astype(F32).astype(BF16) for m in head_lanes]

    @pl.loop(0, planes)
    def _(g):
        stream = got[g].astype(F32).reshape(128, 256)
        triple = dot(normed(stream, gain1[...]), w_qkv1[...]).astype(BF16)
        tiles = []
        for t in range(2):
            q = triple[:, 128 * t : 128 * t + 128]
            k = triple[:, 256 + 128 * t : 384 + 128 * t]
            v = triple[:, 512 + 128 * t : 640 + 128 * t]
            both = jnp.concatenate([v, ones], axis=1)
            top = jnp.zeros((128, 128), F32)
            low = jnp.ones((128, 128), F32)
            for i in range(4):
                z = dot_t(q * head_keep[i], k) + phase_table[4 * t + i]
                peak = jnp.max(z, axis=1, keepdims=True)
                weight = jnp.exp2((z - peak) * rate).astype(BF16)
                summed = dot(weight, both)
                top = jnp.where(head_lanes[i], summed[:, :128], top)
                low = jnp.where(head_lanes[i], summed[:, 128:], low)
            tiles.append((top / low).astype(BF16))
        mixed = jnp.concatenate(tiles, axis=1)
        residual = stream + dot(mixed, w_out1[...])
        sent[g] = residual.astype(BF16).reshape(blocks, 8, 256)

    own_out = pltpu.make_async_copy(
        sent.at[:, me], ext.at[pl.ds(reach, planes), me], local_sem.at[1]
    )
    own_out.start()

    @pl.loop(1, bins)
    def _(i):
        peer = lax.rem(me + i, bins)
        pltpu.make_async_remote_copy(
            src_ref=sent.at[:, peer],
            dst_ref=ext.at[pl.ds(reach, planes), me],
            send_sem=send_sem.at[1],
            recv_sem=recv_sem.at[1],
            device_id={"phase": peer},
            device_id_type=MESH,
        ).start()

    @pl.when(not_last)
    def _():
        @pl.loop(0, bins)
        def _(i):
            peer = lax.rem(me + i, bins)
            pltpu.make_async_remote_copy(
                src_ref=sent.at[pl.ds(planes - reach, reach), peer],
                dst_ref=ext.at[pl.ds(0, reach), me],
                send_sem=send_sem.at[2],
                recv_sem=recv_sem.at[2],
                device_id={"phase": peer, "space": slab + 1},
                device_id_type=MESH,
            ).start()

    @pl.when(not_first)
    def _():
        @pl.loop(0, bins)
        def _(i):
            peer = lax.rem(me + i, bins)
            pltpu.make_async_remote_copy(
                src_ref=sent.at[pl.ds(0, reach), peer],
                dst_ref=ext.at[pl.ds(reach + planes, reach), me],
                send_sem=send_sem.at[3],
                recv_sem=recv_sem.at[3],
                device_id={"phase": peer, "space": slab - 1},
                device_id_type=MESH,
            ).start()

    weight_copies[2].wait()
    own_out.wait()
    others = ext.at[pl.ds(reach, planes), pl.ds(0, bins - 1)]
    pltpu.make_async_copy(others, others, recv_sem.at[1]).wait()

    @pl.loop(0, planes)
    def _(g):
        stream = ext[reach + g].astype(F32).reshape(128, 256)
        triple = dot(normed(stream, gain2[...]), w_qkv2[...]).astype(BF16)
        queries[g] = triple[:, :256]
        keys[reach + g] = triple[:, 256:512]
        values[reach + g] = triple[:, 512:]

    below = ext.at[pl.ds(0, reach)]
    above = ext.at[pl.ds(reach + planes, reach)]

    @pl.when(not_first)
    def _():
        pltpu.make_async_copy(below, below, recv_sem.at[2]).wait()

    @pl.when(not_last)
    def _():
        pltpu.make_async_copy(above, above, recv_sem.at[3]).wait()

    @pl.loop(0, reach)
    def _(g):
        for plane in (g, reach + planes + g):
            stream = ext[plane].astype(F32).reshape(128, 256)
            pair = dot(normed(stream, gain2[...]), w_qkv2[:, 256:]).astype(BF16)
            keys[plane] = pair[:, :256]
            values[plane] = pair[:, 256:]

    for copy in weight_copies[3:]:
        copy.wait()

    depth = planes * slabs

    @pl.loop(0, planes)
    def _(g):
        tiles = []
        for t in range(2):
            lanes = slice(128 * t, 128 * t + 128)
            q = queries[g, :, lanes]
            top = jnp.zeros((128, 128), F32)
            low = jnp.ones((128, 128), F32)
            for i in range(4):
                h = 4 * t + i
                low_z = g + corner[h, 0]
                first = low_z + reach
                k = keys[pl.ds(first, 4), :, lanes].reshape(512, 128)
                v = values[pl.ds(first, 4), :, lanes].reshape(512, 128)
                parts = []
                for a in range(4):
                    z_key = slab * planes + low_z + a
                    outside = (z_key < 0) | (z_key >= depth)
                    parts.append(window_table[jnp.where(outside, 4 * heads, 4 * h + a)])
                z = dot_t(q * head_keep[i], k) + jnp.concatenate(parts, axis=1)
                peak = jnp.max(z, axis=1, keepdims=True)
                weight = jnp.exp2((z - peak) * rate).astype(BF16)
                both = jnp.concatenate([v, jnp.ones((512, 128), BF16)], axis=1)
                summed = dot(weight, both)
                top = jnp.where(head_lanes[i], summed[:, :128], top)
                low = jnp.where(head_lanes[i], summed[:, 128:], low)
            tiles.append((top / low).astype(BF16))
        mixed = jnp.concatenate(tiles, axis=1)
        residual = ext[reach + g].astype(F32).reshape(128, 256) + dot(mixed, w_out2[...])
        hidden = jax.nn.gelu(dot(normed(residual, gain3[...]), w_up[...]), approximate=True)
        final = residual + dot(hidden.astype(BF16), w_down[...])
        out[g] = final.astype(BF16)

    others = got.at[:, pl.ds(0, bins - 1)]
    pltpu.make_async_copy(others, others, send_sem.at[0]).wait()
    pltpu.make_async_copy(others, others, send_sem.at[1]).wait()

    @pl.when(not_last)
    def _():
        pltpu.make_async_copy(below, below, send_sem.at[2]).wait()

    @pl.when(not_first)
    def _():
        pltpu.make_async_copy(above, above, send_sem.at[3]).wait()


def solution(mesh):
    bins, slabs = mesh.shape["phase"], mesh.shape["space"]

    def local(
        volume,
        gain_first,
        phase_qkv,
        phase_out,
        bin_phase,
        phase_bias,
        gain_second,
        window_qkv,
        window_out,
        window_corner,
        window_bias,
        gain_third,
        mlp_up,
        mlp_down,
    ):
        _, planes, extent_x, extent_y, width = volume.shape
        tokens = extent_x * extent_y
        blocks = tokens // 8
        reach = planes - 1
        deep = planes + 2 * reach
        smem = pl.BlockSpec(memory_space=pltpu.SMEM)
        vmem = pl.BlockSpec(memory_space=pltpu.VMEM)
        hbm = pl.BlockSpec(memory_space=pl.ANY)
        weights = (phase_qkv, phase_out, window_qkv, window_out, mlp_up, mlp_down)
        result = pl.pallas_call(
            functools.partial(kernel, bins, slabs),
            out_shape=jax.ShapeDtypeStruct((planes, tokens, width), BF16),
            in_specs=[smem] * 4 + [vmem] * 3 + [hbm] * 7,
            out_specs=vmem,
            scratch_shapes=[pltpu.VMEM(w.shape, BF16) for w in weights]
            + [
                pltpu.VMEM((planes, blocks, 8, width), BF16),
                pltpu.VMEM((planes, blocks, 8, width), BF16),
                pltpu.VMEM((deep, blocks, 8, width), BF16),
                pltpu.VMEM((planes, tokens, width), BF16),
                pltpu.VMEM((deep, tokens, width), BF16),
                pltpu.VMEM((deep, tokens, width), BF16),
                pltpu.VMEM((8, 128, 128), F32),
                pltpu.VMEM((33, 128, 128), F32),
                pltpu.SemaphoreType.DMA((6,)),
                pltpu.SemaphoreType.DMA((2,)),
                pltpu.SemaphoreType.DMA((4,)),
                pltpu.SemaphoreType.DMA((4,)),
            ],
            compiler_params=pltpu.CompilerParams(collective_id=0, has_side_effects=True),
        )(
            bin_phase,
            phase_bias,
            window_corner,
            window_bias,
            gain_first.reshape(1, width),
            gain_second.reshape(1, width),
            gain_third.reshape(1, width),
            volume.reshape(planes, blocks, 8, width),
            *weights,
        )
        return result.reshape(volume.shape)

    split = P("phase", "space", None, None, None)
    return jax.shard_map(
        local,
        mesh=mesh,
        in_specs=(split,) + (P(),) * 13,
        out_specs=split,
        check_vma=False,
    )
```

```python
import functools
import math

import jax
import jax.numpy as jnp
from jax import lax
from jax.experimental import pallas as pl
from jax.experimental.pallas import tpu as pltpu
from jax.sharding import PartitionSpec as P

MESH = pl.DeviceIdType.MESH
EPSILON = 1e-06
MASKED = -1e30
F32 = jnp.float32
BF16 = jnp.bfloat16


def normed(values, gain):
    mean_sq = jnp.mean(values * values, axis=-1, keepdims=True)
    return (values * lax.rsqrt(mean_sq + EPSILON) * gain).astype(BF16)


def dot(a, b):
    return jnp.dot(a, b, preferred_element_type=F32)


def dot_t(a, b):
    return lax.dot_general(a, b, (((1,), (1,)), ((), ())), preferred_element_type=F32)


def kernel(
    bins,
    slabs,
    bin_phase,
    phase_bias,
    corner,
    window_bias,
    gain1_hbm,
    gain2_hbm,
    gain3_hbm,
    vol,
    w_qkv1_hbm,
    w_out1_hbm,
    w_qkv2_hbm,
    w_out2_hbm,
    w_up_hbm,
    w_down_hbm,
    out,
    gain1,
    gain2,
    gain3,
    w_qkv1,
    w_out1,
    w_qkv2,
    w_out2,
    w_up,
    w_down,
    got,
    sent,
    ext,
    queries,
    keys,
    values,
    phase_table,
    window_table,
    weight_sem,
    local_sem,
    send_sem,
    recv_sem,
):
    me = lax.axis_index("phase")
    slab = lax.axis_index("space")
    planes, blocks = vol.shape[0], vol.shape[1]
    heads = 8
    scale = 1.0 / math.sqrt(32)
    unscale = math.sqrt(32)
    rate = scale * math.log2(math.e)
    reach = planes - 1
    not_first = slab > 0
    not_last = slab < slabs - 1

    barrier = pltpu.get_barrier_semaphore()

    @pl.loop(1, bins)
    def _(i):
        pl.semaphore_signal(
            barrier, inc=1, device_id={"phase": lax.rem(me + i, bins)}, device_id_type=MESH
        )

    @pl.when(not_first)
    def _():
        @pl.loop(0, bins)
        def _(i):
            pl.semaphore_signal(
                barrier,
                inc=1,
                device_id={"phase": lax.rem(me + i, bins), "space": slab - 1},
                device_id_type=MESH,
            )

    @pl.when(not_last)
    def _():
        @pl.loop(0, bins)
        def _(i):
            pl.semaphore_signal(
                barrier,
                inc=1,
                device_id={"phase": lax.rem(me + i, bins), "space": slab + 1},
                device_id_type=MESH,
            )

    weight_copies = [
        pltpu.make_async_copy(source, target, weight_sem.at[i])
        for i, (source, target) in enumerate(
            [
                (gain1_hbm, gain1),
                (w_qkv1_hbm, w_qkv1),
                (w_out1_hbm, w_out1),
                (gain2_hbm, gain2),
                (w_qkv2_hbm, w_qkv2),
                (w_out2_hbm, w_out2),
                (gain3_hbm, gain3),
                (w_up_hbm, w_up),
                (w_down_hbm, w_down),
            ]
        )
    ]
    for copy in weight_copies:
        copy.start()
    own_in = pltpu.make_async_copy(vol.at[:, me], got.at[:, me], local_sem.at[0])
    own_in.start()

    lane = lax.broadcasted_iota(jnp.int32, (1, 128), 1)

    lane_bin = lax.broadcasted_iota(jnp.int32, (bins, 128), 1) // 8
    row_bin = lax.broadcasted_iota(jnp.int32, (bins, 128), 0)
    there = jnp.zeros((bins, 128), jnp.int32)
    here = jnp.zeros((bins, 128), jnp.int32)
    for c in range(bins):
        there = jnp.where(lane_bin == c, bin_phase[c], there)
        here = jnp.where(row_bin == c, bin_phase[c], here)
    gap = there - here
    gap = jnp.where(gap < 0, gap + bins, gap)
    same = (
        lax.broadcasted_iota(jnp.int32, (bins, 8, 128), 1)
        == lax.broadcasted_iota(jnp.int32, (bins, 8, 128), 2) % 8
    )
    for h in range(heads):
        level = jnp.zeros((bins, 128), F32)
        for k in range(bins):
            level = jnp.where(gap == k, phase_bias[h, k] * unscale, level)
        table = jnp.where(same, jnp.broadcast_to(level[:, None, :], (bins, 8, 128)), MASKED)
        phase_table[h] = table.reshape(128, 128)

    @pl.when(jnp.logical_not(not_first))
    def _():
        ext[0:reach] = jnp.zeros((reach, blocks, 8, 256), BF16)

    @pl.when(jnp.logical_not(not_last))
    def _():
        ext[reach + planes :] = jnp.zeros((reach, blocks, 8, 256), BF16)

    sides = not_first.astype(jnp.int32) + not_last.astype(jnp.int32)
    pl.semaphore_wait(barrier, bins - 1 + bins * sides)

    half = planes // 2
    for part in range(2):

        @pl.loop(1, bins)
        def _(i):
            peer = lax.rem(me + i, bins)
            pltpu.make_async_remote_copy(
                src_ref=vol.at[pl.ds(half * part, half), peer],
                dst_ref=got.at[pl.ds(half * part, half), me],
                send_sem=send_sem.at[part],
                recv_sem=recv_sem.at[part],
                device_id={"phase": peer},
                device_id_type=MESH,
            ).start()

    row = lax.broadcasted_iota(jnp.int32, (128, 128), 0)
    column = lax.broadcasted_iota(jnp.int32, (128, 128), 1)
    step_x = column // 32 - row // 32
    step_y = column % 32 - row % 32
    window_table[4 * heads] = jnp.full((128, 128), MASKED, F32)

    @pl.loop(0, heads)
    def _(h):
        b = step_x - corner[1, h]
        c = step_y - corner[2, h]
        inside = (b >= 0) & (b < 4) & (c >= 0) & (c < 4)
        code = jnp.where(inside, 4 * b + c, 16)
        for a in range(4):
            table = jnp.full((128, 128), MASKED, F32)
            for j in range(16):
                table = jnp.where(code == j, window_bias[h, 16 * a + j] * unscale, table)
            window_table[4 * h + a] = table

    head_lanes = [(lane // 32) == i for i in range(4)]
    head_keep = [m.astype(F32).astype(BF16) for m in head_lanes]

    def attend(part):
        rows = 128 * half
        stream = got[half * part : half * part + half].astype(F32).reshape(rows, 256)
        triple = dot(normed(stream, gain1[...]), w_qkv1[...]).astype(BF16)
        mixed = []
        for p in range(half):
            tiles = []
            for t in range(2):
                q = triple[128 * p : 128 * p + 128, 128 * t : 128 * t + 128]
                k = triple[128 * p : 128 * p + 128, 256 + 128 * t : 384 + 128 * t]
                v = triple[128 * p : 128 * p + 128, 512 + 128 * t : 640 + 128 * t]
                both = jnp.concatenate([v, jnp.ones((128, 128), BF16)], axis=1)
                stacked = jnp.concatenate([q * keep for keep in head_keep], axis=0)
                z = dot_t(stacked, k) + phase_table[4 * t : 4 * t + 4].reshape(512, 128)
                peak = jnp.max(z, axis=1, keepdims=True)
                weight = jnp.exp2((z - peak) * rate).astype(BF16)
                summed = dot(weight, both)
                top = summed[:128, :128]
                low = summed[:128, 128:]
                for i in range(1, 4):
                    top = jnp.where(head_lanes[i], summed[128 * i : 128 * i + 128, :128], top)
                    low = jnp.where(head_lanes[i], summed[128 * i : 128 * i + 128, 128:], low)
                tiles.append((top / low).astype(BF16))
            mixed.append(jnp.concatenate(tiles, axis=1))
        residual = stream + dot(jnp.concatenate(mixed, axis=0), w_out1[...])
        sent[half * part : half * part + half] = residual.astype(BF16).reshape(half, blocks, 8, 256)

    def hand_on(part):
        here = half * part
        up = max(here, planes - reach)
        up_count = here + half - up
        down_count = min(here + half, reach) - here
        pltpu.make_async_copy(
            sent.at[pl.ds(here, half), me], ext.at[pl.ds(reach + here, half), me], local_sem.at[1 + part]
        ).start()

        @pl.when(not_last)
        def _():
            @pl.loop(0, bins)
            def _(i):
                peer = lax.rem(me + i, bins)
                pltpu.make_async_remote_copy(
                    src_ref=sent.at[pl.ds(up, up_count), peer],
                    dst_ref=ext.at[pl.ds(up - (planes - reach), up_count), me],
                    send_sem=send_sem.at[4 + part],
                    recv_sem=recv_sem.at[4 + part],
                    device_id={"phase": peer, "space": slab + 1},
                    device_id_type=MESH,
                ).start()

        @pl.when(not_first)
        def _():
            @pl.loop(0, bins)
            def _(i):
                peer = lax.rem(me + i, bins)
                pltpu.make_async_remote_copy(
                    src_ref=sent.at[pl.ds(here, down_count), peer],
                    dst_ref=ext.at[pl.ds(reach + planes + here, down_count), me],
                    send_sem=send_sem.at[6 + part],
                    recv_sem=recv_sem.at[6 + part],
                    device_id={"phase": peer, "space": slab - 1},
                    device_id_type=MESH,
                ).start()

        @pl.loop(1, bins)
        def _(i):
            peer = lax.rem(me + i, bins)
            pltpu.make_async_remote_copy(
                src_ref=sent.at[pl.ds(here, half), peer],
                dst_ref=ext.at[pl.ds(reach + here, half), me],
                send_sem=send_sem.at[2 + part],
                recv_sem=recv_sem.at[2 + part],
                device_id={"phase": peer},
                device_id_type=MESH,
            ).start()

    def arrived(ref, sem):
        pltpu.make_async_copy(ref, ref, sem).wait()

    own_in.wait()
    for copy in weight_copies[:3]:
        copy.wait()
    for part in range(2):
        arrived(got.at[pl.ds(0, half), pl.ds(0, bins - 1)], recv_sem.at[part])
        attend(part)
        hand_on(part)

    for copy in weight_copies[3:5]:
        copy.wait()

    def project(plane, inner):
        stream = ext[plane].astype(F32).reshape(128, 256)
        if inner is None:
            pair = dot(normed(stream, gain2[...]), w_qkv2[:, 256:]).astype(BF16)
            keys[plane] = pair[:, :256]
            values[plane] = pair[:, 256:]
        else:
            triple = dot(normed(stream, gain2[...]), w_qkv2[...]).astype(BF16)
            queries[inner] = triple[:, :256]
            keys[plane] = triple[:, 256:512]
            values[plane] = triple[:, 512:]

    for part in range(2):
        pltpu.make_async_copy(
            sent.at[pl.ds(0, half), me], ext.at[pl.ds(reach, half), me], local_sem.at[1 + part]
        ).wait()
        arrived(got.at[pl.ds(0, half), pl.ds(0, bins - 1)], recv_sem.at[2 + part])

        @pl.loop(half * part, half * part + half)
        def _(g):
            project(reach + g, g)

    for part in range(2):
        here = half * part
        up = max(here, planes - reach)
        up_count = here + half - up
        down_count = min(here + half, reach) - here

        @pl.when(not_first)
        def _():
            arrived(ext.at[pl.ds(0, up_count)], recv_sem.at[4 + part])

        @pl.when(not_last)
        def _():
            arrived(ext.at[pl.ds(0, down_count)], recv_sem.at[6 + part])

        first = up - (planes - reach)

        @pl.loop(first, first + up_count)
        def _(g):
            project(g, None)

        @pl.loop(reach + planes + here, reach + planes + here + down_count)
        def _(g):
            project(g, None)

    for copy in weight_copies[5:]:
        copy.wait()

    depth = planes * slabs

    @pl.loop(0, planes)
    def _(g):
        tiles = []
        for t in range(2):
            lanes = slice(128 * t, 128 * t + 128)
            q = queries[g, :, lanes]
            top = jnp.zeros((128, 128), F32)
            low = jnp.ones((128, 128), F32)
            for i in range(4):
                h = 4 * t + i
                low_z = g + corner[0, h]
                first = low_z + reach
                k = keys[pl.ds(first, 4), :, lanes].reshape(512, 128)
                v = values[pl.ds(first, 4), :, lanes].reshape(512, 128)
                parts = []
                for a in range(4):
                    z_key = slab * planes + low_z + a
                    outside = (z_key < 0) | (z_key >= depth)
                    parts.append(window_table[jnp.where(outside, 4 * heads, 4 * h + a)])
                z = dot_t(q * head_keep[i], k) + jnp.concatenate(parts, axis=1)
                peak = jnp.max(z, axis=1, keepdims=True)
                weight = jnp.exp2((z - peak) * rate).astype(BF16)
                both = jnp.concatenate([v, jnp.ones((512, 128), BF16)], axis=1)
                summed = dot(weight, both)
                top = jnp.where(head_lanes[i], summed[:, :128], top)
                low = jnp.where(head_lanes[i], summed[:, 128:], low)
            tiles.append((top / low).astype(BF16))
        mixed = jnp.concatenate(tiles, axis=1)
        residual = ext[reach + g].astype(F32).reshape(128, 256) + dot(mixed, w_out2[...])
        hidden = jax.nn.gelu(dot(normed(residual, gain3[...]), w_up[...]), approximate=True)
        final = residual + dot(hidden.astype(BF16), w_down[...])
        out[g] = final

    for part in range(2):
        here = half * part
        up_count = here + half - max(here, planes - reach)
        down_count = min(here + half, reach) - here
        arrived(got.at[pl.ds(0, half), pl.ds(0, bins - 1)], send_sem.at[part])
        arrived(got.at[pl.ds(0, half), pl.ds(0, bins - 1)], send_sem.at[2 + part])

        @pl.when(not_last)
        def _():
            arrived(ext.at[pl.ds(0, up_count)], send_sem.at[4 + part])

        @pl.when(not_first)
        def _():
            arrived(ext.at[pl.ds(0, down_count)], send_sem.at[6 + part])


def solution(mesh):
    bins, slabs = mesh.shape["phase"], mesh.shape["space"]

    def local(
        volume,
        gain_first,
        phase_qkv,
        phase_out,
        bin_phase,
        phase_bias,
        gain_second,
        window_qkv,
        window_out,
        window_corner,
        window_bias,
        gain_third,
        mlp_up,
        mlp_down,
    ):
        _, planes, extent_x, extent_y, width = volume.shape
        tokens = extent_x * extent_y
        blocks = tokens // 8
        reach = planes - 1
        deep = planes + 2 * reach
        smem = pl.BlockSpec(memory_space=pltpu.SMEM)
        vmem = pl.BlockSpec(memory_space=pltpu.VMEM)
        hbm = pl.BlockSpec(memory_space=pl.ANY)
        weights = (phase_qkv, phase_out, window_qkv, window_out, mlp_up, mlp_down)
        result = pl.pallas_call(
            functools.partial(kernel, bins, slabs),
            out_shape=jax.ShapeDtypeStruct((planes, tokens, width), F32),
            in_specs=[smem] * 4 + [hbm] * 10,
            out_specs=vmem,
            scratch_shapes=[pltpu.VMEM((1, width), F32)] * 3
            + [pltpu.VMEM(w.shape, BF16) for w in weights]
            + [
                pltpu.VMEM((planes, blocks, 8, width), BF16),
                pltpu.VMEM((planes, blocks, 8, width), BF16),
                pltpu.VMEM((deep, blocks, 8, width), BF16),
                pltpu.VMEM((planes, tokens, width), BF16),
                pltpu.VMEM((deep, tokens, width), BF16),
                pltpu.VMEM((deep, tokens, width), BF16),
                pltpu.VMEM((8, 128, 128), F32),
                pltpu.VMEM((33, 128, 128), F32),
                pltpu.SemaphoreType.DMA((9,)),
                pltpu.SemaphoreType.DMA((3,)),
                pltpu.SemaphoreType.DMA((8,)),
                pltpu.SemaphoreType.DMA((8,)),
            ],
            compiler_params=pltpu.CompilerParams(collective_id=0, has_side_effects=True),
        )(
            bin_phase,
            phase_bias,
            window_corner.T,
            window_bias,
            gain_first.reshape(1, width),
            gain_second.reshape(1, width),
            gain_third.reshape(1, width),
            volume.reshape(planes, blocks, 8, width),
            *weights,
        )
        return result.astype(BF16).reshape(volume.shape)

    split = P("phase", "space", None, None, None)
    return jax.shard_map(
        local,
        mesh=mesh,
        in_specs=(split,) + (P(),) * 13,
        out_specs=split,
        check_vma=False,
    )
```

```python
import functools
import math

import jax
import jax.numpy as jnp
from jax import lax
from jax.experimental import pallas as pl
from jax.experimental.pallas import tpu as pltpu
from jax.sharding import PartitionSpec as P

MESH = pl.DeviceIdType.MESH
EPSILON = 1e-06
MASKED = -1e30
F32 = jnp.float32
BF16 = jnp.bfloat16


def normed(values, gain):
    mean_sq = jnp.mean(values * values, axis=-1, keepdims=True)
    return (values * lax.rsqrt(mean_sq + EPSILON) * gain).astype(BF16)


def dot(a, b):
    return jnp.dot(a, b, preferred_element_type=F32)


def dot_t(a, b):
    return lax.dot_general(a, b, (((1,), (1,)), ((), ())), preferred_element_type=F32)


def kernel(
    bins,
    slabs,
    bin_phase,
    phase_bias,
    corner,
    window_bias,
    gain1_hbm,
    gain2_hbm,
    gain3_hbm,
    vol,
    w_qkv1_hbm,
    w_out1_hbm,
    w_qkv2_hbm,
    w_out2_hbm,
    w_up_hbm,
    w_down_hbm,
    out,
    gain1,
    gain2,
    gain3,
    w_qkv1,
    w_out1,
    w_qkv2,
    w_out2,
    w_up,
    w_down,
    got,
    sent,
    ext,
    queries,
    keys,
    values,
    phase_table,
    window_table,
    weight_sem,
    local_sem,
    send_sem,
    recv_sem,
):
    me = lax.axis_index("phase")
    slab = lax.axis_index("space")
    planes, blocks = vol.shape[0], vol.shape[1]
    heads = 8
    scale = 1.0 / math.sqrt(32)
    unscale = math.sqrt(32)
    rate = scale * math.log2(math.e)
    reach = planes - 1
    not_first = slab > 0
    not_last = slab < slabs - 1

    barrier = pltpu.get_barrier_semaphore()

    @pl.loop(1, bins)
    def _(i):
        pl.semaphore_signal(
            barrier, inc=1, device_id={"phase": lax.rem(me + i, bins)}, device_id_type=MESH
        )

    @pl.when(not_first)
    def _():
        pl.semaphore_signal(barrier, inc=1, device_id={"space": slab - 1}, device_id_type=MESH)

    @pl.when(not_last)
    def _():
        pl.semaphore_signal(barrier, inc=1, device_id={"space": slab + 1}, device_id_type=MESH)

    weight_copies = [
        pltpu.make_async_copy(source, target, weight_sem.at[i])
        for i, (source, target) in enumerate(
            [
                (gain1_hbm, gain1),
                (w_qkv1_hbm, w_qkv1),
                (w_out1_hbm, w_out1),
                (gain2_hbm, gain2),
                (w_qkv2_hbm, w_qkv2),
                (w_out2_hbm, w_out2),
                (gain3_hbm, gain3),
                (w_up_hbm, w_up),
                (w_down_hbm, w_down),
            ]
        )
    ]
    for copy in weight_copies:
        copy.start()
    own_in = pltpu.make_async_copy(vol.at[:, me], got.at[:, me], local_sem.at[0])
    own_in.start()

    lane = lax.broadcasted_iota(jnp.int32, (1, 128), 1)

    lane_bin = lax.broadcasted_iota(jnp.int32, (bins, 128), 1) // 8
    row_bin = lax.broadcasted_iota(jnp.int32, (bins, 128), 0)
    there = jnp.zeros((bins, 128), jnp.int32)
    here = jnp.zeros((bins, 128), jnp.int32)
    for c in range(bins):
        there = jnp.where(lane_bin == c, bin_phase[c], there)
        here = jnp.where(row_bin == c, bin_phase[c], here)
    gap = there - here
    gap = jnp.where(gap < 0, gap + bins, gap)
    same = (
        lax.broadcasted_iota(jnp.int32, (bins, 8, 128), 1)
        == lax.broadcasted_iota(jnp.int32, (bins, 8, 128), 2) % 8
    )
    for h in range(heads):
        level = jnp.zeros((bins, 128), F32)
        for k in range(bins):
            level = jnp.where(gap == k, phase_bias[h, k] * unscale, level)
        table = jnp.where(same, jnp.broadcast_to(level[:, None, :], (bins, 8, 128)), MASKED)
        phase_table[h] = table.reshape(128, 128)

    @pl.when(jnp.logical_not(not_first))
    def _():
        ext[0:reach] = jnp.zeros((reach, blocks, 8, 256), BF16)

    @pl.when(jnp.logical_not(not_last))
    def _():
        ext[reach + planes :] = jnp.zeros((reach, blocks, 8, 256), BF16)

    sides = not_first.astype(jnp.int32) + not_last.astype(jnp.int32)
    pl.semaphore_wait(barrier, bins - 1 + sides)

    half = planes // 2
    for part in range(2):

        @pl.loop(1, bins)
        def _(i):
            peer = lax.rem(me + i, bins)
            pltpu.make_async_remote_copy(
                src_ref=vol.at[pl.ds(half * part, half), peer],
                dst_ref=got.at[pl.ds(half * part, half), me],
                send_sem=send_sem.at[part],
                recv_sem=recv_sem.at[part],
                device_id={"phase": peer},
                device_id_type=MESH,
            ).start()

    row = lax.broadcasted_iota(jnp.int32, (128, 128), 0)
    column = lax.broadcasted_iota(jnp.int32, (128, 128), 1)
    step_x = column // 32 - row // 32
    step_y = column % 32 - row % 32
    window_table[4 * heads] = jnp.full((128, 128), MASKED, F32)

    @pl.loop(0, heads)
    def _(h):
        b = step_x - corner[1, h]
        c = step_y - corner[2, h]
        inside = (b >= 0) & (b < 4) & (c >= 0) & (c < 4)
        code = jnp.where(inside, 4 * b + c, 16)
        for a in range(4):
            table = jnp.full((128, 128), MASKED, F32)
            for j in range(16):
                table = jnp.where(code == j, window_bias[h, 16 * a + j] * unscale, table)
            window_table[4 * h + a] = table

    head_lanes = [(lane // 32) == i for i in range(4)]
    head_keep = [m.astype(F32).astype(BF16) for m in head_lanes]

    def attend(part):
        rows = 128 * half
        stream = got[half * part : half * part + half].astype(F32).reshape(rows, 256)
        triple = dot(normed(stream, gain1[...]), w_qkv1[...]).astype(BF16)
        mixed = []
        for p in range(half):
            tiles = []
            for t in range(2):
                q = triple[128 * p : 128 * p + 128, 128 * t : 128 * t + 128]
                k = triple[128 * p : 128 * p + 128, 256 + 128 * t : 384 + 128 * t]
                v = triple[128 * p : 128 * p + 128, 512 + 128 * t : 640 + 128 * t]
                both = jnp.concatenate([v, jnp.ones((128, 128), BF16)], axis=1)
                stacked = jnp.concatenate([q * keep for keep in head_keep], axis=0)
                z = dot_t(stacked, k) + phase_table[4 * t : 4 * t + 4].reshape(512, 128)
                peak = jnp.max(z, axis=1, keepdims=True)
                weight = jnp.exp2((z - peak) * rate).astype(BF16)
                summed = dot(weight, both)
                top = summed[:128, :128]
                low = summed[:128, 128:]
                for i in range(1, 4):
                    top = jnp.where(head_lanes[i], summed[128 * i : 128 * i + 128, :128], top)
                    low = jnp.where(head_lanes[i], summed[128 * i : 128 * i + 128, 128:], low)
                tiles.append((top / low).astype(BF16))
            mixed.append(jnp.concatenate(tiles, axis=1))
        residual = stream + dot(jnp.concatenate(mixed, axis=0), w_out1[...])
        sent[half * part : half * part + half] = residual.astype(BF16).reshape(half, blocks, 8, 256)

    def hand_on(part):
        here = half * part
        up = max(here, planes - reach)
        up_count = here + half - up
        down_count = min(here + half, reach) - here
        pltpu.make_async_copy(
            sent.at[pl.ds(here, half), me], ext.at[pl.ds(reach + here, half), me], local_sem.at[1 + part]
        ).start()

        @pl.when(not_last)
        def _():
            @pl.loop(0, bins)
            def _(i):
                peer = lax.rem(me + i, bins)
                pltpu.make_async_remote_copy(
                    src_ref=sent.at[pl.ds(up, up_count), peer],
                    dst_ref=ext.at[pl.ds(up - (planes - reach), up_count), me],
                    send_sem=send_sem.at[4 + part],
                    recv_sem=recv_sem.at[4 + part],
                    device_id={"phase": peer, "space": slab + 1},
                    device_id_type=MESH,
                ).start()

        @pl.when(not_first)
        def _():
            @pl.loop(0, bins)
            def _(i):
                peer = lax.rem(me + i, bins)
                pltpu.make_async_remote_copy(
                    src_ref=sent.at[pl.ds(here, down_count), peer],
                    dst_ref=ext.at[pl.ds(reach + planes + here, down_count), me],
                    send_sem=send_sem.at[6 + part],
                    recv_sem=recv_sem.at[6 + part],
                    device_id={"phase": peer, "space": slab - 1},
                    device_id_type=MESH,
                ).start()

        @pl.loop(1, bins)
        def _(i):
            peer = lax.rem(me + i, bins)
            pltpu.make_async_remote_copy(
                src_ref=sent.at[pl.ds(here, half), peer],
                dst_ref=ext.at[pl.ds(reach + here, half), me],
                send_sem=send_sem.at[2 + part],
                recv_sem=recv_sem.at[2 + part],
                device_id={"phase": peer},
                device_id_type=MESH,
            ).start()

    def arrived(ref, sem):
        pltpu.make_async_copy(ref, ref, sem).wait()

    own_in.wait()
    for copy in weight_copies[:3]:
        copy.wait()
    for part in range(2):
        arrived(got.at[pl.ds(0, half), pl.ds(0, bins - 1)], recv_sem.at[part])
        attend(part)
        hand_on(part)

    for copy in weight_copies[3:5]:
        copy.wait()

    def project(plane, inner):
        stream = ext[plane].astype(F32).reshape(128, 256)
        if inner is None:
            pair = dot(normed(stream, gain2[...]), w_qkv2[:, 256:]).astype(BF16)
            keys[plane] = pair[:, :256]
            values[plane] = pair[:, 256:]
        else:
            triple = dot(normed(stream, gain2[...]), w_qkv2[...]).astype(BF16)
            queries[inner] = triple[:, :256]
            keys[plane] = triple[:, 256:512]
            values[plane] = triple[:, 512:]

    for part in range(2):
        pltpu.make_async_copy(
            sent.at[pl.ds(0, half), me], ext.at[pl.ds(reach, half), me], local_sem.at[1 + part]
        ).wait()
        arrived(got.at[pl.ds(0, half), pl.ds(0, bins - 1)], recv_sem.at[2 + part])

        @pl.loop(half * part, half * part + half)
        def _(g):
            project(reach + g, g)

    for part in range(2):
        here = half * part
        up = max(here, planes - reach)
        up_count = here + half - up
        down_count = min(here + half, reach) - here

        @pl.when(not_first)
        def _():
            arrived(ext.at[pl.ds(0, up_count)], recv_sem.at[4 + part])

        @pl.when(not_last)
        def _():
            arrived(ext.at[pl.ds(0, down_count)], recv_sem.at[6 + part])

        first = up - (planes - reach)

        @pl.loop(first, first + up_count)
        def _(g):
            project(g, None)

        @pl.loop(reach + planes + here, reach + planes + here + down_count)
        def _(g):
            project(g, None)

    for copy in weight_copies[5:]:
        copy.wait()

    depth = planes * slabs

    @pl.loop(0, planes)
    def _(g):
        tiles = []
        for t in range(2):
            lanes = slice(128 * t, 128 * t + 128)
            q = queries[g, :, lanes]
            top = jnp.zeros((128, 128), F32)
            low = jnp.ones((128, 128), F32)
            for i in range(4):
                h = 4 * t + i
                low_z = g + corner[0, h]
                first = low_z + reach
                k = keys[pl.ds(first, 4), :, lanes].reshape(512, 128)
                v = values[pl.ds(first, 4), :, lanes].reshape(512, 128)
                parts = []
                for a in range(4):
                    z_key = slab * planes + low_z + a
                    outside = (z_key < 0) | (z_key >= depth)
                    parts.append(window_table[jnp.where(outside, 4 * heads, 4 * h + a)])
                z = dot_t(q * head_keep[i], k) + jnp.concatenate(parts, axis=1)
                peak = jnp.max(z, axis=1, keepdims=True)
                weight = jnp.exp2((z - peak) * rate).astype(BF16)
                both = jnp.concatenate([v, jnp.ones((512, 128), BF16)], axis=1)
                summed = dot(weight, both)
                top = jnp.where(head_lanes[i], summed[:, :128], top)
                low = jnp.where(head_lanes[i], summed[:, 128:], low)
            tiles.append((top / low).astype(BF16))
        mixed = jnp.concatenate(tiles, axis=1)
        residual = ext[reach + g].astype(F32).reshape(128, 256) + dot(mixed, w_out2[...])
        hidden = jax.nn.gelu(dot(normed(residual, gain3[...]), w_up[...]), approximate=True)
        final = residual + dot(hidden.astype(BF16), w_down[...])
        out[g] = final

    for part in range(2):
        here = half * part
        up_count = here + half - max(here, planes - reach)
        down_count = min(here + half, reach) - here
        arrived(got.at[pl.ds(0, half), pl.ds(0, bins - 1)], send_sem.at[part])
        arrived(got.at[pl.ds(0, half), pl.ds(0, bins - 1)], send_sem.at[2 + part])

        @pl.when(not_last)
        def _():
            arrived(ext.at[pl.ds(0, up_count)], send_sem.at[4 + part])

        @pl.when(not_first)
        def _():
            arrived(ext.at[pl.ds(0, down_count)], send_sem.at[6 + part])


def solution(mesh):
    bins, slabs = mesh.shape["phase"], mesh.shape["space"]

    def local(
        volume,
        gain_first,
        phase_qkv,
        phase_out,
        bin_phase,
        phase_bias,
        gain_second,
        window_qkv,
        window_out,
        window_corner,
        window_bias,
        gain_third,
        mlp_up,
        mlp_down,
    ):
        _, planes, extent_x, extent_y, width = volume.shape
        tokens = extent_x * extent_y
        blocks = tokens // 8
        reach = planes - 1
        deep = planes + 2 * reach
        smem = pl.BlockSpec(memory_space=pltpu.SMEM)
        vmem = pl.BlockSpec(memory_space=pltpu.VMEM)
        hbm = pl.BlockSpec(memory_space=pl.ANY)
        weights = (phase_qkv, phase_out, window_qkv, window_out, mlp_up, mlp_down)
        result = pl.pallas_call(
            functools.partial(kernel, bins, slabs),
            out_shape=jax.ShapeDtypeStruct((planes, tokens, width), F32),
            in_specs=[smem] * 4 + [hbm] * 10,
            out_specs=vmem,
            scratch_shapes=[pltpu.VMEM((1, width), F32)] * 3
            + [pltpu.VMEM(w.shape, BF16) for w in weights]
            + [
                pltpu.VMEM((planes, blocks, 8, width), BF16),
                pltpu.VMEM((planes, blocks, 8, width), BF16),
                pltpu.VMEM((deep, blocks, 8, width), BF16),
                pltpu.VMEM((planes, tokens, width), BF16),
                pltpu.VMEM((deep, tokens, width), BF16),
                pltpu.VMEM((deep, tokens, width), BF16),
                pltpu.VMEM((8, 128, 128), F32),
                pltpu.VMEM((33, 128, 128), F32),
                pltpu.SemaphoreType.DMA((9,)),
                pltpu.SemaphoreType.DMA((3,)),
                pltpu.SemaphoreType.DMA((8,)),
                pltpu.SemaphoreType.DMA((8,)),
            ],
            compiler_params=pltpu.CompilerParams(collective_id=0, has_side_effects=True),
        )(
            bin_phase,
            phase_bias,
            window_corner.T,
            window_bias,
            gain_first.reshape(1, width),
            gain_second.reshape(1, width),
            gain_third.reshape(1, width),
            volume.reshape(planes, blocks, 8, width),
            *weights,
        )
        return result.astype(BF16).reshape(volume.shape)

    split = P("phase", "space", None, None, None)
    return jax.shard_map(
        local,
        mesh=mesh,
        in_specs=(split,) + (P(),) * 13,
        out_specs=split,
        check_vma=False,
    )
```

```python
import functools
import math

import jax
import jax.numpy as jnp
from jax import lax
from jax.experimental import pallas as pl
from jax.experimental.pallas import tpu as pltpu
from jax.sharding import PartitionSpec as P

MESH = pl.DeviceIdType.MESH
EPSILON = 1e-06
MASKED = -1e30
F32 = jnp.float32
BF16 = jnp.bfloat16


def normed(values, gain):
    mean_sq = jnp.mean(values * values, axis=-1, keepdims=True)
    return (values * lax.rsqrt(mean_sq + EPSILON) * gain).astype(BF16)


def dot(a, b):
    return jnp.dot(a, b, preferred_element_type=F32)


def dot_t(a, b):
    return lax.dot_general(a, b, (((1,), (1,)), ((), ())), preferred_element_type=F32)


def kernel(
    bins,
    slabs,
    bin_phase_hbm,
    phase_bias_hbm,
    corner_hbm,
    window_bias_hbm,
    gain1_hbm,
    gain2_hbm,
    gain3_hbm,
    vol,
    w_qkv1_hbm,
    w_out1_hbm,
    w_qkv2_hbm,
    w_out2_hbm,
    w_up_hbm,
    w_down_hbm,
    out,
    bin_phase,
    phase_bias,
    corner,
    window_bias,
    gain1,
    gain2,
    gain3,
    w_qkv1,
    w_out1,
    w_qkv2,
    w_out2,
    w_up,
    w_down,
    got,
    sent,
    ext,
    queries,
    keys,
    values,
    phase_table,
    window_table,
    table_sem,
    weight_sem,
    local_sem,
    send_sem,
    recv_sem,
):
    me = lax.axis_index("phase")
    slab = lax.axis_index("space")
    planes, blocks = vol.shape[0], vol.shape[1]
    heads = 8
    scale = 1.0 / math.sqrt(32)
    unscale = math.sqrt(32)
    rate = scale * math.log2(math.e)
    reach = planes - 1
    not_first = slab > 0
    not_last = slab < slabs - 1

    barrier = pltpu.get_barrier_semaphore()

    @pl.loop(1, bins)
    def _(i):
        pl.semaphore_signal(
            barrier, inc=1, device_id={"phase": lax.rem(me + i, bins)}, device_id_type=MESH
        )

    @pl.when(not_first)
    def _():
        pl.semaphore_signal(barrier, inc=1, device_id={"space": slab - 1}, device_id_type=MESH)

    @pl.when(not_last)
    def _():
        pl.semaphore_signal(barrier, inc=1, device_id={"space": slab + 1}, device_id_type=MESH)

    table_copies = [
        pltpu.make_async_copy(source, target, table_sem.at[i])
        for i, (source, target) in enumerate(
            [
                (bin_phase_hbm, bin_phase),
                (phase_bias_hbm, phase_bias),
                (corner_hbm, corner),
                (window_bias_hbm, window_bias),
            ]
        )
    ]
    for copy in table_copies:
        copy.start()
    weight_copies = [
        pltpu.make_async_copy(source, target, weight_sem.at[i])
        for i, (source, target) in enumerate(
            [
                (gain1_hbm, gain1),
                (w_qkv1_hbm, w_qkv1),
                (w_out1_hbm, w_out1),
                (gain2_hbm, gain2),
                (w_qkv2_hbm, w_qkv2),
                (w_out2_hbm, w_out2),
                (gain3_hbm, gain3),
                (w_up_hbm, w_up),
                (w_down_hbm, w_down),
            ]
        )
    ]
    for copy in weight_copies:
        copy.start()
    own_in = pltpu.make_async_copy(vol.at[:, me], got.at[:, me], local_sem.at[0])
    own_in.start()

    for copy in table_copies:
        copy.wait()
    lane = lax.broadcasted_iota(jnp.int32, (1, 128), 1)

    lane_bin = lax.broadcasted_iota(jnp.int32, (bins, 128), 1) // 8
    row_bin = lax.broadcasted_iota(jnp.int32, (bins, 128), 0)
    there = jnp.zeros((bins, 128), jnp.int32)
    here = jnp.zeros((bins, 128), jnp.int32)
    for c in range(bins):
        there = jnp.where(lane_bin == c, bin_phase[c], there)
        here = jnp.where(row_bin == c, bin_phase[c], here)
    gap = there - here
    gap = jnp.where(gap < 0, gap + bins, gap)
    same = (
        lax.broadcasted_iota(jnp.int32, (bins, 8, 128), 1)
        == lax.broadcasted_iota(jnp.int32, (bins, 8, 128), 2) % 8
    )
    for h in range(heads):
        level = jnp.zeros((bins, 128), F32)
        for k in range(bins):
            level = jnp.where(gap == k, phase_bias[h, k] * unscale, level)
        table = jnp.where(same, jnp.broadcast_to(level[:, None, :], (bins, 8, 128)), MASKED)
        phase_table[h] = table.reshape(128, 128)

    @pl.when(jnp.logical_not(not_first))
    def _():
        ext[0:reach] = jnp.zeros((reach, blocks, 8, 256), BF16)

    @pl.when(jnp.logical_not(not_last))
    def _():
        ext[reach + planes :] = jnp.zeros((reach, blocks, 8, 256), BF16)

    sides = not_first.astype(jnp.int32) + not_last.astype(jnp.int32)
    pl.semaphore_wait(barrier, bins - 1 + sides)

    half = planes // 2
    for part in range(2):

        @pl.loop(1, bins)
        def _(i):
            peer = lax.rem(me + i, bins)
            pltpu.make_async_remote_copy(
                src_ref=vol.at[pl.ds(half * part, half), peer],
                dst_ref=got.at[pl.ds(half * part, half), me],
                send_sem=send_sem.at[part],
                recv_sem=recv_sem.at[part],
                device_id={"phase": peer},
                device_id_type=MESH,
            ).start()

    row = lax.broadcasted_iota(jnp.int32, (128, 128), 0)
    column = lax.broadcasted_iota(jnp.int32, (128, 128), 1)
    step_x = column // 32 - row // 32
    step_y = column % 32 - row % 32
    window_table[4 * heads] = jnp.full((128, 128), MASKED, F32)

    @pl.loop(0, heads)
    def _(h):
        b = step_x - corner[1, h]
        c = step_y - corner[2, h]
        inside = (b >= 0) & (b < 4) & (c >= 0) & (c < 4)
        code = jnp.where(inside, 4 * b + c, 16)
        for a in range(4):
            table = jnp.full((128, 128), MASKED, F32)
            for j in range(16):
                table = jnp.where(code == j, window_bias[h, 16 * a + j] * unscale, table)
            window_table[4 * h + a] = table

    head_lanes = [(lane // 32) == i for i in range(4)]
    head_keep = [m.astype(F32).astype(BF16) for m in head_lanes]

    def attend(part):
        rows = 128 * half
        stream = got[half * part : half * part + half].astype(F32).reshape(rows, 256)
        triple = dot(normed(stream, gain1[...]), w_qkv1[...]).astype(BF16)
        mixed = []
        for p in range(half):
            tiles = []
            for t in range(2):
                q = triple[128 * p : 128 * p + 128, 128 * t : 128 * t + 128]
                k = triple[128 * p : 128 * p + 128, 256 + 128 * t : 384 + 128 * t]
                v = triple[128 * p : 128 * p + 128, 512 + 128 * t : 640 + 128 * t]
                both = jnp.concatenate([v, jnp.ones((128, 128), BF16)], axis=1)
                stacked = jnp.concatenate([q * keep for keep in head_keep], axis=0)
                z = dot_t(stacked, k) + phase_table[4 * t : 4 * t + 4].reshape(512, 128)
                peak = jnp.max(z, axis=1, keepdims=True)
                weight = jnp.exp2((z - peak) * rate).astype(BF16)
                summed = dot(weight, both)
                top = summed[:128, :128]
                low = summed[:128, 128:]
                for i in range(1, 4):
                    top = jnp.where(head_lanes[i], summed[128 * i : 128 * i + 128, :128], top)
                    low = jnp.where(head_lanes[i], summed[128 * i : 128 * i + 128, 128:], low)
                tiles.append((top / low).astype(BF16))
            mixed.append(jnp.concatenate(tiles, axis=1))
        residual = stream + dot(jnp.concatenate(mixed, axis=0), w_out1[...])
        sent[half * part : half * part + half] = residual.astype(BF16).reshape(half, blocks, 8, 256)

    def hand_on(part):
        here = half * part
        up = max(here, planes - reach)
        up_count = here + half - up
        down_count = min(here + half, reach) - here
        pltpu.make_async_copy(
            sent.at[pl.ds(here, half), me], ext.at[pl.ds(reach + here, half), me], local_sem.at[1 + part]
        ).start()

        @pl.when(not_last)
        def _():
            @pl.loop(0, bins)
            def _(i):
                peer = lax.rem(me + i, bins)
                pltpu.make_async_remote_copy(
                    src_ref=sent.at[pl.ds(up, up_count), peer],
                    dst_ref=ext.at[pl.ds(up - (planes - reach), up_count), me],
                    send_sem=send_sem.at[4 + part],
                    recv_sem=recv_sem.at[4 + part],
                    device_id={"phase": peer, "space": slab + 1},
                    device_id_type=MESH,
                ).start()

        @pl.when(not_first)
        def _():
            @pl.loop(0, bins)
            def _(i):
                peer = lax.rem(me + i, bins)
                pltpu.make_async_remote_copy(
                    src_ref=sent.at[pl.ds(here, down_count), peer],
                    dst_ref=ext.at[pl.ds(reach + planes + here, down_count), me],
                    send_sem=send_sem.at[6 + part],
                    recv_sem=recv_sem.at[6 + part],
                    device_id={"phase": peer, "space": slab - 1},
                    device_id_type=MESH,
                ).start()

        @pl.loop(1, bins)
        def _(i):
            peer = lax.rem(me + i, bins)
            pltpu.make_async_remote_copy(
                src_ref=sent.at[pl.ds(here, half), peer],
                dst_ref=ext.at[pl.ds(reach + here, half), me],
                send_sem=send_sem.at[2 + part],
                recv_sem=recv_sem.at[2 + part],
                device_id={"phase": peer},
                device_id_type=MESH,
            ).start()

    def arrived(ref, sem):
        pltpu.make_async_copy(ref, ref, sem).wait()

    own_in.wait()
    for copy in weight_copies[:3]:
        copy.wait()
    for part in range(2):
        arrived(got.at[pl.ds(0, half), pl.ds(0, bins - 1)], recv_sem.at[part])
        attend(part)
        hand_on(part)

    for copy in weight_copies[3:5]:
        copy.wait()

    def project(plane, inner):
        stream = ext[plane].astype(F32).reshape(128, 256)
        if inner is None:
            pair = dot(normed(stream, gain2[...]), w_qkv2[:, 256:]).astype(BF16)
            keys[plane] = pair[:, :256]
            values[plane] = pair[:, 256:]
        else:
            triple = dot(normed(stream, gain2[...]), w_qkv2[...]).astype(BF16)
            queries[inner] = triple[:, :256]
            keys[plane] = triple[:, 256:512]
            values[plane] = triple[:, 512:]

    for part in range(2):
        pltpu.make_async_copy(
            sent.at[pl.ds(0, half), me], ext.at[pl.ds(reach, half), me], local_sem.at[1 + part]
        ).wait()
        arrived(got.at[pl.ds(0, half), pl.ds(0, bins - 1)], recv_sem.at[2 + part])

        @pl.loop(half * part, half * part + half)
        def _(g):
            project(reach + g, g)

    for part in range(2):
        here = half * part
        up = max(here, planes - reach)
        up_count = here + half - up
        down_count = min(here + half, reach) - here

        @pl.when(not_first)
        def _():
            arrived(ext.at[pl.ds(0, up_count)], recv_sem.at[4 + part])

        @pl.when(not_last)
        def _():
            arrived(ext.at[pl.ds(0, down_count)], recv_sem.at[6 + part])

        first = up - (planes - reach)

        @pl.loop(first, first + up_count)
        def _(g):
            project(g, None)

        @pl.loop(reach + planes + here, reach + planes + here + down_count)
        def _(g):
            project(g, None)

    for copy in weight_copies[5:]:
        copy.wait()

    depth = planes * slabs

    @pl.loop(0, planes)
    def _(g):
        tiles = []
        for t in range(2):
            lanes = slice(128 * t, 128 * t + 128)
            q = queries[g, :, lanes]
            top = jnp.zeros((128, 128), F32)
            low = jnp.ones((128, 128), F32)
            for i in range(4):
                h = 4 * t + i
                low_z = g + corner[0, h]
                first = low_z + reach
                k = keys[pl.ds(first, 4), :, lanes].reshape(512, 128)
                v = values[pl.ds(first, 4), :, lanes].reshape(512, 128)
                parts = []
                for a in range(4):
                    z_key = slab * planes + low_z + a
                    outside = (z_key < 0) | (z_key >= depth)
                    parts.append(window_table[jnp.where(outside, 4 * heads, 4 * h + a)])
                z = dot_t(q * head_keep[i], k) + jnp.concatenate(parts, axis=1)
                peak = jnp.max(z, axis=1, keepdims=True)
                weight = jnp.exp2((z - peak) * rate).astype(BF16)
                both = jnp.concatenate([v, jnp.ones((512, 128), BF16)], axis=1)
                summed = dot(weight, both)
                top = jnp.where(head_lanes[i], summed[:, :128], top)
                low = jnp.where(head_lanes[i], summed[:, 128:], low)
            tiles.append((top / low).astype(BF16))
        mixed = jnp.concatenate(tiles, axis=1)
        residual = ext[reach + g].astype(F32).reshape(128, 256) + dot(mixed, w_out2[...])
        hidden = jax.nn.gelu(dot(normed(residual, gain3[...]), w_up[...]), approximate=True)
        final = residual + dot(hidden.astype(BF16), w_down[...])
        out[g] = final

    for part in range(2):
        here = half * part
        up_count = here + half - max(here, planes - reach)
        down_count = min(here + half, reach) - here
        arrived(got.at[pl.ds(0, half), pl.ds(0, bins - 1)], send_sem.at[part])
        arrived(got.at[pl.ds(0, half), pl.ds(0, bins - 1)], send_sem.at[2 + part])

        @pl.when(not_last)
        def _():
            arrived(ext.at[pl.ds(0, up_count)], send_sem.at[4 + part])

        @pl.when(not_first)
        def _():
            arrived(ext.at[pl.ds(0, down_count)], send_sem.at[6 + part])


def solution(mesh):
    bins, slabs = mesh.shape["phase"], mesh.shape["space"]

    def local(
        volume,
        gain_first,
        phase_qkv,
        phase_out,
        bin_phase,
        phase_bias,
        gain_second,
        window_qkv,
        window_out,
        window_corner,
        window_bias,
        gain_third,
        mlp_up,
        mlp_down,
    ):
        _, planes, extent_x, extent_y, width = volume.shape
        tokens = extent_x * extent_y
        blocks = tokens // 8
        reach = planes - 1
        deep = planes + 2 * reach
        vmem = pl.BlockSpec(memory_space=pltpu.VMEM)
        hbm = pl.BlockSpec(memory_space=pl.ANY)
        weights = (phase_qkv, phase_out, window_qkv, window_out, mlp_up, mlp_down)
        result = pl.pallas_call(
            functools.partial(kernel, bins, slabs),
            out_shape=pltpu.VMEM((planes, tokens, width), F32),
            in_specs=[hbm] * 14,
            out_specs=vmem,
            scratch_shapes=[
                pltpu.SMEM(bin_phase.shape, jnp.int32),
                pltpu.SMEM(phase_bias.shape, F32),
                pltpu.SMEM(window_corner.shape[::-1], jnp.int32),
                pltpu.SMEM(window_bias.shape, F32),
            ]
            + [pltpu.VMEM((1, width), F32)] * 3
            + [pltpu.VMEM(w.shape, BF16) for w in weights]
            + [
                pltpu.VMEM((planes, blocks, 8, width), BF16),
                pltpu.VMEM((planes, blocks, 8, width), BF16),
                pltpu.VMEM((deep, blocks, 8, width), BF16),
                pltpu.VMEM((planes, tokens, width), BF16),
                pltpu.VMEM((deep, tokens, width), BF16),
                pltpu.VMEM((deep, tokens, width), BF16),
                pltpu.VMEM((8, 128, 128), F32),
                pltpu.VMEM((33, 128, 128), F32),
                pltpu.SemaphoreType.DMA((4,)),
                pltpu.SemaphoreType.DMA((9,)),
                pltpu.SemaphoreType.DMA((3,)),
                pltpu.SemaphoreType.DMA((8,)),
                pltpu.SemaphoreType.DMA((8,)),
            ],
            compiler_params=pltpu.CompilerParams(collective_id=0, has_side_effects=True),
        )(
            bin_phase,
            phase_bias,
            window_corner.T,
            window_bias,
            gain_first.reshape(1, width),
            gain_second.reshape(1, width),
            gain_third.reshape(1, width),
            volume.reshape(planes, blocks, 8, width),
            *weights,
        )
        return result.astype(BF16).reshape(volume.shape)

    split = P("phase", "space", None, None, None)
    return jax.shard_map(
        local,
        mesh=mesh,
        in_specs=(split,) + (P(),) * 13,
        out_specs=split,
        check_vma=False,
    )
```

```python
import functools
import math

import jax
import jax.numpy as jnp
from jax import lax
from jax.experimental import pallas as pl
from jax.experimental.pallas import tpu as pltpu
from jax.sharding import PartitionSpec as P

MESH = pl.DeviceIdType.MESH
EPSILON = 1e-06
MASKED = -1e30
F32 = jnp.float32
BF16 = jnp.bfloat16


def normed(values, gain):
    mean_sq = jnp.mean(values * values, axis=-1, keepdims=True)
    return (values * lax.rsqrt(mean_sq + EPSILON) * gain).astype(BF16)


def dot(a, b):
    return jnp.dot(a, b, preferred_element_type=F32)


def dot_t(a, b):
    return lax.dot_general(a, b, (((1,), (1,)), ((), ())), preferred_element_type=F32)


def kernel(
    bins,
    slabs,
    bin_phase_hbm,
    phase_bias_hbm,
    corner_hbm,
    window_bias_hbm,
    gain1_hbm,
    gain2_hbm,
    gain3_hbm,
    vol,
    w_qkv1_hbm,
    w_out1_hbm,
    w_qkv2_hbm,
    w_out2_hbm,
    w_up_hbm,
    w_down_hbm,
    out,
    bin_phase,
    phase_bias,
    corner,
    window_bias,
    gain1,
    gain2,
    gain3,
    w_qkv1,
    w_out1,
    w_qkv2,
    w_out2,
    w_up,
    w_down,
    got,
    sent,
    ext,
    queries,
    keys,
    values,
    attended,
    phase_table,
    window_table,
    table_sem,
    weight_sem,
    local_sem,
    send_sem,
    recv_sem,
):
    me = lax.axis_index("phase")
    slab = lax.axis_index("space")
    planes, blocks = vol.shape[0], vol.shape[1]
    heads = 8
    scale = 1.0 / math.sqrt(32)
    unscale = math.sqrt(32)
    rate = scale * math.log2(math.e)
    reach = planes - 1
    not_first = slab > 0
    not_last = slab < slabs - 1

    barrier = pltpu.get_barrier_semaphore()

    @pl.loop(1, bins)
    def _(i):
        pl.semaphore_signal(
            barrier, inc=1, device_id={"phase": lax.rem(me + i, bins)}, device_id_type=MESH
        )

    @pl.when(not_first)
    def _():
        pl.semaphore_signal(barrier, inc=1, device_id={"space": slab - 1}, device_id_type=MESH)

    @pl.when(not_last)
    def _():
        pl.semaphore_signal(barrier, inc=1, device_id={"space": slab + 1}, device_id_type=MESH)

    table_copies = [
        pltpu.make_async_copy(source, target, table_sem.at[i])
        for i, (source, target) in enumerate(
            [
                (bin_phase_hbm, bin_phase),
                (phase_bias_hbm, phase_bias),
                (corner_hbm, corner),
                (window_bias_hbm, window_bias),
            ]
        )
    ]
    for copy in table_copies:
        copy.start()
    weight_copies = [
        pltpu.make_async_copy(source, target, weight_sem.at[i])
        for i, (source, target) in enumerate(
            [
                (gain1_hbm, gain1),
                (w_qkv1_hbm, w_qkv1),
                (w_out1_hbm, w_out1),
                (gain2_hbm, gain2),
                (w_qkv2_hbm, w_qkv2),
                (w_out2_hbm, w_out2),
                (gain3_hbm, gain3),
                (w_up_hbm, w_up),
                (w_down_hbm, w_down),
            ]
        )
    ]
    for copy in weight_copies:
        copy.start()
    own_in = pltpu.make_async_copy(vol.at[:, me], got.at[:, me], local_sem.at[0])
    own_in.start()

    for copy in table_copies:
        copy.wait()
    lane = lax.broadcasted_iota(jnp.int32, (1, 128), 1)

    lane_bin = lax.broadcasted_iota(jnp.int32, (bins, 128), 1) // 8
    row_bin = lax.broadcasted_iota(jnp.int32, (bins, 128), 0)
    there = jnp.zeros((bins, 128), jnp.int32)
    here = jnp.zeros((bins, 128), jnp.int32)
    for c in range(bins):
        there = jnp.where(lane_bin == c, bin_phase[c], there)
        here = jnp.where(row_bin == c, bin_phase[c], here)
    gap = there - here
    gap = jnp.where(gap < 0, gap + bins, gap)
    same = (
        lax.broadcasted_iota(jnp.int32, (bins, 8, 128), 1)
        == lax.broadcasted_iota(jnp.int32, (bins, 8, 128), 2) % 8
    )
    for h in range(heads):
        level = jnp.zeros((bins, 128), F32)
        for k in range(bins):
            level = jnp.where(gap == k, phase_bias[h, k] * unscale, level)
        table = jnp.where(same, jnp.broadcast_to(level[:, None, :], (bins, 8, 128)), MASKED)
        phase_table[h] = table.reshape(128, 128)

    @pl.when(jnp.logical_not(not_first))
    def _():
        ext[0:reach] = jnp.zeros((reach, blocks, 8, 256), BF16)

    @pl.when(jnp.logical_not(not_last))
    def _():
        ext[reach + planes :] = jnp.zeros((reach, blocks, 8, 256), BF16)

    sides = not_first.astype(jnp.int32) + not_last.astype(jnp.int32)
    pl.semaphore_wait(barrier, bins - 1 + sides)

    half = planes // 2
    for part in range(2):

        @pl.loop(1, bins)
        def _(i):
            peer = lax.rem(me + i, bins)
            pltpu.make_async_remote_copy(
                src_ref=vol.at[pl.ds(half * part, half), peer],
                dst_ref=got.at[pl.ds(half * part, half), me],
                send_sem=send_sem.at[part],
                recv_sem=recv_sem.at[part],
                device_id={"phase": peer},
                device_id_type=MESH,
            ).start()

    row = lax.broadcasted_iota(jnp.int32, (128, 128), 0)
    column = lax.broadcasted_iota(jnp.int32, (128, 128), 1)
    step_x = column // 32 - row // 32
    step_y = column % 32 - row % 32
    window_table[4 * heads] = jnp.full((128, 128), MASKED, F32)

    @pl.loop(0, heads)
    def _(h):
        b = step_x - corner[1, h]
        c = step_y - corner[2, h]
        inside = (b >= 0) & (b < 4) & (c >= 0) & (c < 4)
        code = jnp.where(inside, 4 * b + c, 16)
        for a in range(4):
            table = jnp.full((128, 128), MASKED, F32)
            for j in range(16):
                table = jnp.where(code == j, window_bias[h, 16 * a + j] * unscale, table)
            window_table[4 * h + a] = table

    head_lanes = [(lane // 32) == i for i in range(4)]
    head_keep = [m.astype(F32).astype(BF16) for m in head_lanes]

    def attend(part):
        rows = 128 * half
        stream = got[half * part : half * part + half].astype(F32).reshape(rows, 256)
        triple = dot(normed(stream, gain1[...]), w_qkv1[...]).astype(BF16)
        mixed = []
        for p in range(half):
            tiles = []
            for t in range(2):
                q = triple[128 * p : 128 * p + 128, 128 * t : 128 * t + 128]
                k = triple[128 * p : 128 * p + 128, 256 + 128 * t : 384 + 128 * t]
                v = triple[128 * p : 128 * p + 128, 512 + 128 * t : 640 + 128 * t]
                both = jnp.concatenate([v, jnp.ones((128, 128), BF16)], axis=1)
                stacked = jnp.concatenate([q * keep for keep in head_keep], axis=0)
                z = dot_t(stacked, k) + phase_table[4 * t : 4 * t + 4].reshape(512, 128)
                peak = jnp.max(z, axis=1, keepdims=True)
                weight = jnp.exp2((z - peak) * rate).astype(BF16)
                summed = dot(weight, both)
                top = summed[:128, :128]
                low = summed[:128, 128:]
                for i in range(1, 4):
                    top = jnp.where(head_lanes[i], summed[128 * i : 128 * i + 128, :128], top)
                    low = jnp.where(head_lanes[i], summed[128 * i : 128 * i + 128, 128:], low)
                tiles.append((top / low).astype(BF16))
            mixed.append(jnp.concatenate(tiles, axis=1))
        residual = stream + dot(jnp.concatenate(mixed, axis=0), w_out1[...])
        sent[half * part : half * part + half] = residual.astype(BF16).reshape(half, blocks, 8, 256)

    def hand_on(part):
        here = half * part
        up = max(here, planes - reach)
        up_count = here + half - up
        down_count = min(here + half, reach) - here
        pltpu.make_async_copy(
            sent.at[pl.ds(here, half), me], ext.at[pl.ds(reach + here, half), me], local_sem.at[1 + part]
        ).start()

        @pl.loop(1, bins)
        def _(i):
            peer = lax.rem(me + i, bins)
            pltpu.make_async_remote_copy(
                src_ref=sent.at[pl.ds(here, half), peer],
                dst_ref=ext.at[pl.ds(reach + here, half), me],
                send_sem=send_sem.at[2 + part],
                recv_sem=recv_sem.at[2 + part],
                device_id={"phase": peer},
                device_id_type=MESH,
            ).start()

        @pl.when(not_last)
        def _():
            @pl.loop(0, bins)
            def _(i):
                peer = lax.rem(me + i, bins)
                pltpu.make_async_remote_copy(
                    src_ref=sent.at[pl.ds(up, up_count), peer],
                    dst_ref=ext.at[pl.ds(up - (planes - reach), up_count), me],
                    send_sem=send_sem.at[4 + part],
                    recv_sem=recv_sem.at[4 + part],
                    device_id={"phase": peer, "space": slab + 1},
                    device_id_type=MESH,
                ).start()

        @pl.when(not_first)
        def _():
            @pl.loop(0, bins)
            def _(i):
                peer = lax.rem(me + i, bins)
                pltpu.make_async_remote_copy(
                    src_ref=sent.at[pl.ds(here, down_count), peer],
                    dst_ref=ext.at[pl.ds(reach + planes + here, down_count), me],
                    send_sem=send_sem.at[6 + part],
                    recv_sem=recv_sem.at[6 + part],
                    device_id={"phase": peer, "space": slab - 1},
                    device_id_type=MESH,
                ).start()

    def arrived(ref, sem):
        pltpu.make_async_copy(ref, ref, sem).wait()

    own_in.wait()
    for copy in weight_copies[:3]:
        copy.wait()
    for part in range(2):
        arrived(got.at[pl.ds(0, half), pl.ds(0, bins - 1)], recv_sem.at[part])
        attend(part)
        hand_on(part)

    for copy in weight_copies[3:5]:
        copy.wait()

    def project(plane, inner):
        stream = ext[plane].astype(F32).reshape(128, 256)
        if inner is None:
            pair = dot(normed(stream, gain2[...]), w_qkv2[:, 256:]).astype(BF16)
            keys[plane] = pair[:, :256]
            values[plane] = pair[:, 256:]
        else:
            triple = dot(normed(stream, gain2[...]), w_qkv2[...]).astype(BF16)
            queries[inner] = triple[:, :256]
            keys[plane] = triple[:, 256:512]
            values[plane] = triple[:, 512:]

    for part in range(2):
        pltpu.make_async_copy(
            sent.at[pl.ds(0, half), me], ext.at[pl.ds(reach, half), me], local_sem.at[1 + part]
        ).wait()
        arrived(got.at[pl.ds(0, half), pl.ds(0, bins - 1)], recv_sem.at[2 + part])

        @pl.loop(half * part, half * part + half)
        def _(g):
            project(reach + g, g)

    for part in range(2):
        here = half * part
        up = max(here, planes - reach)
        up_count = here + half - up
        down_count = min(here + half, reach) - here

        @pl.when(not_first)
        def _():
            arrived(ext.at[pl.ds(0, up_count)], recv_sem.at[4 + part])

        @pl.when(not_last)
        def _():
            arrived(ext.at[pl.ds(0, down_count)], recv_sem.at[6 + part])

        first = up - (planes - reach)

        @pl.loop(first, first + up_count)
        def _(g):
            project(g, None)

        @pl.loop(reach + planes + here, reach + planes + here + down_count)
        def _(g):
            project(g, None)

    for copy in weight_copies[5:]:
        copy.wait()

    depth = planes * slabs

    def look(g):
        tiles = []
        for t in range(2):
            lanes = slice(128 * t, 128 * t + 128)
            q = queries[g, :, lanes]
            top = jnp.zeros((128, 128), F32)
            low = jnp.ones((128, 128), F32)
            for i in range(4):
                h = 4 * t + i
                low_z = g + corner[0, h]
                first = low_z + reach
                k = keys[pl.ds(first, 4), :, lanes].reshape(512, 128)
                v = values[pl.ds(first, 4), :, lanes].reshape(512, 128)
                parts = []
                for a in range(4):
                    z_key = slab * planes + low_z + a
                    outside = (z_key < 0) | (z_key >= depth)
                    parts.append(window_table[jnp.where(outside, 4 * heads, 4 * h + a)])
                z = dot_t(q * head_keep[i], k) + jnp.concatenate(parts, axis=1)
                peak = jnp.max(z, axis=1, keepdims=True)
                weight = jnp.exp2((z - peak) * rate).astype(BF16)
                both = jnp.concatenate([v, jnp.ones((512, 128), BF16)], axis=1)
                summed = dot(weight, both)
                top = jnp.where(head_lanes[i], summed[:, :128], top)
                low = jnp.where(head_lanes[i], summed[:, 128:], low)
            tiles.append((top / low).astype(BF16))
        attended[g] = jnp.concatenate(tiles, axis=1)

    for g in range(planes):
        look(g)
    for part in range(2):
        here = half * part
        rows = 128 * half
        mixed = attended[here : here + half].reshape(rows, 256)
        residual = ext[reach + here : reach + here + half].astype(F32).reshape(rows, 256) + dot(mixed, w_out2[...])
        hidden = jax.nn.gelu(dot(normed(residual, gain3[...]), w_up[...]), approximate=True)
        final = residual + dot(hidden.astype(BF16), w_down[...])
        out[here : here + half] = final.reshape(half, 128, 256)

    for part in range(2):
        here = half * part
        up_count = here + half - max(here, planes - reach)
        down_count = min(here + half, reach) - here
        arrived(got.at[pl.ds(0, half), pl.ds(0, bins - 1)], send_sem.at[part])
        arrived(got.at[pl.ds(0, half), pl.ds(0, bins - 1)], send_sem.at[2 + part])

        @pl.when(not_last)
        def _():
            arrived(ext.at[pl.ds(0, up_count)], send_sem.at[4 + part])

        @pl.when(not_first)
        def _():
            arrived(ext.at[pl.ds(0, down_count)], send_sem.at[6 + part])


def solution(mesh):
    bins, slabs = mesh.shape["phase"], mesh.shape["space"]

    def local(
        volume,
        gain_first,
        phase_qkv,
        phase_out,
        bin_phase,
        phase_bias,
        gain_second,
        window_qkv,
        window_out,
        window_corner,
        window_bias,
        gain_third,
        mlp_up,
        mlp_down,
    ):
        _, planes, extent_x, extent_y, width = volume.shape
        tokens = extent_x * extent_y
        blocks = tokens // 8
        reach = planes - 1
        deep = planes + 2 * reach
        vmem = pl.BlockSpec(memory_space=pltpu.VMEM)
        hbm = pl.BlockSpec(memory_space=pl.ANY)
        weights = (phase_qkv, phase_out, window_qkv, window_out, mlp_up, mlp_down)
        result = pl.pallas_call(
            functools.partial(kernel, bins, slabs),
            out_shape=pltpu.VMEM((planes, tokens, width), F32),
            in_specs=[hbm] * 14,
            out_specs=vmem,
            scratch_shapes=[
                pltpu.SMEM(bin_phase.shape, jnp.int32),
                pltpu.SMEM(phase_bias.shape, F32),
                pltpu.SMEM(window_corner.shape[::-1], jnp.int32),
                pltpu.SMEM(window_bias.shape, F32),
            ]
            + [pltpu.VMEM((1, width), F32)] * 3
            + [pltpu.VMEM(w.shape, BF16) for w in weights]
            + [
                pltpu.VMEM((planes, blocks, 8, width), BF16),
                pltpu.VMEM((planes, blocks, 8, width), BF16),
                pltpu.VMEM((deep, blocks, 8, width), BF16),
                pltpu.VMEM((planes, tokens, width), BF16),
                pltpu.VMEM((deep, tokens, width), BF16),
                pltpu.VMEM((deep, tokens, width), BF16),
                pltpu.VMEM((planes, tokens, width), BF16),
                pltpu.VMEM((8, 128, 128), F32),
                pltpu.VMEM((33, 128, 128), F32),
                pltpu.SemaphoreType.DMA((4,)),
                pltpu.SemaphoreType.DMA((9,)),
                pltpu.SemaphoreType.DMA((3,)),
                pltpu.SemaphoreType.DMA((8,)),
                pltpu.SemaphoreType.DMA((8,)),
            ],
            compiler_params=pltpu.CompilerParams(collective_id=0, has_side_effects=True),
        )(
            bin_phase,
            phase_bias,
            window_corner.T,
            window_bias,
            gain_first.reshape(1, width),
            gain_second.reshape(1, width),
            gain_third.reshape(1, width),
            volume.reshape(planes, blocks, 8, width),
            *weights,
        )
        return result.astype(BF16).reshape(volume.shape)

    split = P("phase", "space", None, None, None)
    return jax.shard_map(
        local,
        mesh=mesh,
        in_specs=(split,) + (P(),) * 13,
        out_specs=split,
        check_vma=False,
    )
```

```python
import functools
import math

import jax
import jax.numpy as jnp
from jax import lax
from jax.experimental import pallas as pl
from jax.experimental.pallas import tpu as pltpu
from jax.sharding import PartitionSpec as P

MESH = pl.DeviceIdType.MESH
EPSILON = 1e-06
MASKED = -1e30
F32 = jnp.float32
BF16 = jnp.bfloat16


def normed(values, gain):
    mean_sq = jnp.mean(values * values, axis=-1, keepdims=True)
    return (values * lax.rsqrt(mean_sq + EPSILON) * gain).astype(BF16)


def dot(a, b):
    return jnp.dot(a, b, preferred_element_type=F32)


def dot_t(a, b):
    return lax.dot_general(a, b, (((1,), (1,)), ((), ())), preferred_element_type=F32)


def kernel(
    bins,
    slabs,
    bin_phase_hbm,
    phase_bias_hbm,
    corner_hbm,
    window_bias_hbm,
    gain1_hbm,
    gain2_hbm,
    gain3_hbm,
    vol,
    w_qkv1_hbm,
    w_out1_hbm,
    w_qkv2_hbm,
    w_out2_hbm,
    w_up_hbm,
    w_down_hbm,
    out,
    bin_phase,
    phase_bias,
    corner,
    window_bias,
    gain1,
    gain2,
    gain3,
    w_qkv1,
    w_out1,
    w_qkv2,
    w_out2,
    w_up,
    w_down,
    got,
    sent,
    ext,
    queries,
    keys,
    values,
    attended,
    phase_table,
    window_table,
    table_sem,
    weight_sem,
    local_sem,
    send_sem,
    recv_sem,
):
    me = lax.axis_index("phase")
    slab = lax.axis_index("space")
    planes, blocks = vol.shape[0], vol.shape[1]
    heads = 8
    scale = 1.0 / math.sqrt(32)
    unscale = math.sqrt(32)
    rate = scale * math.log2(math.e)
    reach = planes - 1
    assert planes == 4
    not_first = slab > 0
    not_last = slab < slabs - 1

    barrier = pltpu.get_barrier_semaphore()

    @pl.loop(1, bins)
    def _(i):
        pl.semaphore_signal(
            barrier, inc=1, device_id={"phase": lax.rem(me + i, bins)}, device_id_type=MESH
        )

    @pl.when(not_first)
    def _():
        pl.semaphore_signal(barrier, inc=1, device_id={"space": slab - 1}, device_id_type=MESH)

    @pl.when(not_last)
    def _():
        pl.semaphore_signal(barrier, inc=1, device_id={"space": slab + 1}, device_id_type=MESH)

    table_copies = [
        pltpu.make_async_copy(source, target, table_sem.at[i])
        for i, (source, target) in enumerate(
            [
                (bin_phase_hbm, bin_phase),
                (phase_bias_hbm, phase_bias),
                (corner_hbm, corner),
                (window_bias_hbm, window_bias),
            ]
        )
    ]
    for copy in table_copies:
        copy.start()
    weight_copies = [
        pltpu.make_async_copy(source, target, weight_sem.at[i])
        for i, (source, target) in enumerate(
            [
                (gain1_hbm, gain1),
                (w_qkv1_hbm, w_qkv1),
                (w_out1_hbm, w_out1),
                (gain2_hbm, gain2),
                (w_qkv2_hbm, w_qkv2),
                (w_out2_hbm, w_out2),
                (gain3_hbm, gain3),
                (w_up_hbm, w_up),
                (w_down_hbm, w_down),
            ]
        )
    ]
    for copy in weight_copies:
        copy.start()
    own_in = pltpu.make_async_copy(vol.at[:, me], got.at[:, me], local_sem.at[0])
    own_in.start()

    for copy in table_copies:
        copy.wait()
    lane = lax.broadcasted_iota(jnp.int32, (1, 128), 1)

    lane_bin = lax.broadcasted_iota(jnp.int32, (bins, 128), 1) // 8
    row_bin = lax.broadcasted_iota(jnp.int32, (bins, 128), 0)
    there = jnp.zeros((bins, 128), jnp.int32)
    here = jnp.zeros((bins, 128), jnp.int32)
    for c in range(bins):
        there = jnp.where(lane_bin == c, bin_phase[c], there)
        here = jnp.where(row_bin == c, bin_phase[c], here)
    gap = there - here
    gap = jnp.where(gap < 0, gap + bins, gap)
    same = (
        lax.broadcasted_iota(jnp.int32, (bins, 8, 128), 1)
        == lax.broadcasted_iota(jnp.int32, (bins, 8, 128), 2) % 8
    )
    for h in range(heads):
        level = jnp.zeros((bins, 128), F32)
        for k in range(bins):
            level = jnp.where(gap == k, phase_bias[h, k] * unscale, level)
        table = jnp.where(same, jnp.broadcast_to(level[:, None, :], (bins, 8, 128)), MASKED)
        phase_table[h] = table.reshape(128, 128)

    @pl.when(jnp.logical_not(not_first))
    def _():
        ext[0:reach] = jnp.zeros((reach, blocks, 8, 256), BF16)

    @pl.when(jnp.logical_not(not_last))
    def _():
        ext[reach + planes :] = jnp.zeros((reach, blocks, 8, 256), BF16)

    sides = not_first.astype(jnp.int32) + not_last.astype(jnp.int32)
    pl.semaphore_wait(barrier, bins - 1 + sides)

    middle = ((1, 2),)
    outer = ((0, 1), (3, 1))

    def gather(part, pieces):
        @pl.loop(1, bins)
        def _(i):
            peer = lax.rem(me + i, bins)
            for first, count in pieces:
                pltpu.make_async_remote_copy(
                    src_ref=vol.at[pl.ds(first, count), peer],
                    dst_ref=got.at[pl.ds(first, count), me],
                    send_sem=send_sem.at[part],
                    recv_sem=recv_sem.at[part],
                    device_id={"phase": peer},
                    device_id_type=MESH,
                ).start()

    gather(0, middle)
    row = lax.broadcasted_iota(jnp.int32, (128, 128), 0)
    column = lax.broadcasted_iota(jnp.int32, (128, 128), 1)
    step_x = column // 32 - row // 32
    step_y = column % 32 - row % 32
    window_table[4 * heads] = jnp.full((128, 128), MASKED, F32)

    @pl.loop(0, heads)
    def _(h):
        b = step_x - corner[1, h]
        c = step_y - corner[2, h]
        inside = (b >= 0) & (b < 4) & (c >= 0) & (c < 4)
        code = jnp.where(inside, 4 * b + c, 16)
        for a in range(4):
            table = jnp.full((128, 128), MASKED, F32)
            for j in range(16):
                table = jnp.where(code == j, window_bias[h, 16 * a + j] * unscale, table)
            window_table[4 * h + a] = table

    gather(1, outer)

    head_lanes = [(lane // 32) == i for i in range(4)]
    head_keep = [m.astype(F32).astype(BF16) for m in head_lanes]

    def attend(pieces):
        rows = 256
        stream = jnp.concatenate([got[f : f + n] for f, n in pieces], axis=0)
        stream = stream.astype(F32).reshape(rows, 256)
        triple = dot(normed(stream, gain1[...]), w_qkv1[...]).astype(BF16)
        mixed = []
        for p in range(2):
            tiles = []
            for t in range(2):
                q = triple[128 * p : 128 * p + 128, 128 * t : 128 * t + 128]
                k = triple[128 * p : 128 * p + 128, 256 + 128 * t : 384 + 128 * t]
                v = triple[128 * p : 128 * p + 128, 512 + 128 * t : 640 + 128 * t]
                both = jnp.concatenate([v, jnp.ones((128, 128), BF16)], axis=1)
                stacked = jnp.concatenate([q * keep for keep in head_keep], axis=0)
                z = dot_t(stacked, k) + phase_table[4 * t : 4 * t + 4].reshape(512, 128)
                peak = jnp.max(z, axis=1, keepdims=True)
                weight = jnp.exp2((z - peak) * rate).astype(BF16)
                summed = dot(weight, both)
                top = summed[:128, :128]
                low = summed[:128, 128:]
                for i in range(1, 4):
                    top = jnp.where(head_lanes[i], summed[128 * i : 128 * i + 128, :128], top)
                    low = jnp.where(head_lanes[i], summed[128 * i : 128 * i + 128, 128:], low)
                tiles.append((top / low).astype(BF16))
            mixed.append(jnp.concatenate(tiles, axis=1))
        residual = stream + dot(jnp.concatenate(mixed, axis=0), w_out1[...])
        residual = residual.astype(BF16).reshape(2, blocks, 8, 256)
        at = 0
        for f, n in pieces:
            sent[f : f + n] = residual[at : at + n]
            at += n

    even = lax.rem(slab, 2) == 0
    low, high = 0, reach + planes
    partner = jnp.where(even, slab + 1, slab - 1)
    partner_slot = jnp.where(even, low, high + 1)
    held_slot = jnp.where(even, high + 1, low)
    onward = jnp.where(even, slab + 2, slab - 2)
    sends_on = (onward >= 0) & (onward < slabs)
    taken_from = jnp.where(even, slab - 2, slab + 2)
    takes = (taken_from >= 0) & (taken_from < slabs)

    def to_owner(part, pieces):
        for first, count in pieces:
            pltpu.make_async_copy(
                sent.at[pl.ds(first, count), me],
                ext.at[pl.ds(reach + first, count), me],
                local_sem.at[1 + part],
            ).start()

        @pl.loop(1, bins)
        def _(i):
            peer = lax.rem(me + i, bins)
            for first, count in pieces:
                pltpu.make_async_remote_copy(
                    src_ref=sent.at[pl.ds(first, count), peer],
                    dst_ref=ext.at[pl.ds(reach + first, count), me],
                    send_sem=send_sem.at[2 + part],
                    recv_sem=recv_sem.at[2 + part],
                    device_id={"phase": peer},
                    device_id_type=MESH,
                ).start()

    def to_slab(first, count, slot, target, sem):
        @pl.loop(0, bins)
        def _(i):
            peer = lax.rem(me + i, bins)
            pltpu.make_async_remote_copy(
                src_ref=sent.at[pl.ds(first, count), peer],
                dst_ref=ext.at[pl.ds(slot, count), me],
                send_sem=send_sem.at[sem],
                recv_sem=recv_sem.at[sem],
                device_id={"phase": peer, "space": target},
                device_id_type=MESH,
            ).start()

    def arrived(ref, sem):
        pltpu.make_async_copy(ref, ref, sem).wait()

    two_blocks = got.at[pl.ds(0, 2), pl.ds(0, bins - 1)]

    def owned(part, pieces):
        for first, count in pieces:
            pltpu.make_async_copy(
                sent.at[pl.ds(first, count), me],
                ext.at[pl.ds(reach + first, count), me],
                local_sem.at[1 + part],
            ).wait()
        arrived(two_blocks, recv_sem.at[2 + part])

    own_in.wait()
    for copy in weight_copies[:3]:
        copy.wait()
    arrived(two_blocks, recv_sem.at[0])
    attend(middle)
    to_slab(1, 2, partner_slot, partner, 4)
    to_owner(0, middle)
    arrived(two_blocks, recv_sem.at[1])
    attend(outer)
    @pl.when(not_last)
    def _():
        to_slab(3, 1, low + reach - 1, slab + 1, 5)

    @pl.when(not_first)
    def _():
        to_slab(0, 1, high, slab - 1, 6)

    to_owner(1, outer)

    def forward():
        return pltpu.make_async_remote_copy(
            src_ref=ext.at[pl.ds(held_slot, 2)],
            dst_ref=ext.at[pl.ds(partner_slot, 2)],
            send_sem=send_sem.at[7],
            recv_sem=recv_sem.at[7],
            device_id={"space": onward},
            device_id_type=MESH,
        )

    arrived(ext.at[pl.ds(0, 2)], recv_sem.at[4])

    @pl.when(sends_on)
    def _():
        forward().start()

    for copy in weight_copies[3:5]:
        copy.wait()

    def project(plane, inner):
        stream = ext[plane].astype(F32).reshape(128, 256)
        if inner is None:
            pair = dot(normed(stream, gain2[...]), w_qkv2[:, 256:]).astype(BF16)
            keys[plane] = pair[:, :256]
            values[plane] = pair[:, 256:]
        else:
            triple = dot(normed(stream, gain2[...]), w_qkv2[...]).astype(BF16)
            queries[inner] = triple[:, :256]
            keys[plane] = triple[:, 256:512]
            values[plane] = triple[:, 512:]

    for i in range(2):
        project(held_slot + i, None)
    owned(0, middle)
    for g in (1, 2):
        project(reach + g, g)
    owned(1, outer)
    for g in (0, 3):
        project(reach + g, g)

    @pl.when(not_first)
    def _():
        arrived(ext.at[pl.ds(0, 1)], recv_sem.at[5])

    @pl.when(not_last)
    def _():
        arrived(ext.at[pl.ds(0, 1)], recv_sem.at[6])

    for slot in (low + reach - 1, high):
        project(slot, None)

    @pl.when(takes)
    def _():
        arrived(ext.at[pl.ds(0, 2)], recv_sem.at[7])

    for i in range(2):
        project(partner_slot + i, None)

    for copy in weight_copies[5:]:
        copy.wait()

    depth = planes * slabs

    def look(g):
        tiles = []
        for t in range(2):
            lanes = slice(128 * t, 128 * t + 128)
            q = queries[g, :, lanes]
            top = jnp.zeros((128, 128), F32)
            low = jnp.ones((128, 128), F32)
            for i in range(4):
                h = 4 * t + i
                low_z = g + corner[0, h]
                first = low_z + reach
                k = keys[pl.ds(first, 4), :, lanes].reshape(512, 128)
                v = values[pl.ds(first, 4), :, lanes].reshape(512, 128)
                parts = []
                for a in range(4):
                    z_key = slab * planes + low_z + a
                    outside = (z_key < 0) | (z_key >= depth)
                    parts.append(window_table[jnp.where(outside, 4 * heads, 4 * h + a)])
                z = dot_t(q * head_keep[i], k) + jnp.concatenate(parts, axis=1)
                peak = jnp.max(z, axis=1, keepdims=True)
                weight = jnp.exp2((z - peak) * rate).astype(BF16)
                both = jnp.concatenate([v, jnp.ones((512, 128), BF16)], axis=1)
                summed = dot(weight, both)
                top = jnp.where(head_lanes[i], summed[:, :128], top)
                low = jnp.where(head_lanes[i], summed[:, 128:], low)
            tiles.append((top / low).astype(BF16))
        attended[g] = jnp.concatenate(tiles, axis=1)

    for g in range(planes):
        look(g)
    half = planes // 2
    for part in range(2):
        here = half * part
        rows = 128 * half
        mixed = attended[here : here + half].reshape(rows, 256)
        residual = ext[reach + here : reach + here + half].astype(F32).reshape(rows, 256) + dot(mixed, w_out2[...])
        hidden = jax.nn.gelu(dot(normed(residual, gain3[...]), w_up[...]), approximate=True)
        final = residual + dot(hidden.astype(BF16), w_down[...])
        out[here : here + half] = final.reshape(half, 128, 256)

    for sem in range(4):
        arrived(two_blocks, send_sem.at[sem])
    arrived(ext.at[pl.ds(0, 2)], send_sem.at[4])

    @pl.when(not_last)
    def _():
        arrived(ext.at[pl.ds(0, 1)], send_sem.at[5])

    @pl.when(not_first)
    def _():
        arrived(ext.at[pl.ds(0, 1)], send_sem.at[6])

    @pl.when(sends_on)
    def _():
        forward().wait_send()


def solution(mesh):
    bins, slabs = mesh.shape["phase"], mesh.shape["space"]

    def local(
        volume,
        gain_first,
        phase_qkv,
        phase_out,
        bin_phase,
        phase_bias,
        gain_second,
        window_qkv,
        window_out,
        window_corner,
        window_bias,
        gain_third,
        mlp_up,
        mlp_down,
    ):
        _, planes, extent_x, extent_y, width = volume.shape
        tokens = extent_x * extent_y
        blocks = tokens // 8
        reach = planes - 1
        deep = planes + 2 * reach
        vmem = pl.BlockSpec(memory_space=pltpu.VMEM)
        hbm = pl.BlockSpec(memory_space=pl.ANY)
        weights = (phase_qkv, phase_out, window_qkv, window_out, mlp_up, mlp_down)
        result = pl.pallas_call(
            functools.partial(kernel, bins, slabs),
            out_shape=pltpu.VMEM((planes, tokens, width), F32),
            in_specs=[hbm] * 14,
            out_specs=vmem,
            scratch_shapes=[
                pltpu.SMEM(bin_phase.shape, jnp.int32),
                pltpu.SMEM(phase_bias.shape, F32),
                pltpu.SMEM(window_corner.shape[::-1], jnp.int32),
                pltpu.SMEM(window_bias.shape, F32),
            ]
            + [pltpu.VMEM((1, width), F32)] * 3
            + [pltpu.VMEM(w.shape, BF16) for w in weights]
            + [
                pltpu.VMEM((planes, blocks, 8, width), BF16),
                pltpu.VMEM((planes, blocks, 8, width), BF16),
                pltpu.VMEM((deep, blocks, 8, width), BF16),
                pltpu.VMEM((planes, tokens, width), BF16),
                pltpu.VMEM((deep, tokens, width), BF16),
                pltpu.VMEM((deep, tokens, width), BF16),
                pltpu.VMEM((planes, tokens, width), BF16),
                pltpu.VMEM((8, 128, 128), F32),
                pltpu.VMEM((33, 128, 128), F32),
                pltpu.SemaphoreType.DMA((4,)),
                pltpu.SemaphoreType.DMA((9,)),
                pltpu.SemaphoreType.DMA((3,)),
                pltpu.SemaphoreType.DMA((8,)),
                pltpu.SemaphoreType.DMA((8,)),
            ],
            compiler_params=pltpu.CompilerParams(collective_id=0, has_side_effects=True),
        )(
            bin_phase,
            phase_bias,
            window_corner.T,
            window_bias,
            gain_first.reshape(1, width),
            gain_second.reshape(1, width),
            gain_third.reshape(1, width),
            volume.reshape(planes, blocks, 8, width),
            *weights,
        )
        return result.astype(BF16).reshape(volume.shape)

    split = P("phase", "space", None, None, None)
    return jax.shard_map(
        local,
        mesh=mesh,
        in_specs=(split,) + (P(),) * 13,
        out_specs=split,
        check_vma=False,
    )
```

```python
import functools
import math

import jax
import jax.numpy as jnp
from jax import lax
from jax.experimental import pallas as pl
from jax.experimental.pallas import tpu as pltpu
from jax.sharding import PartitionSpec as P

MESH = pl.DeviceIdType.MESH
EPSILON = 1e-06
MASKED = -1e30
F32 = jnp.float32
BF16 = jnp.bfloat16


def normed(values, gain):
    mean_sq = jnp.mean(values * values, axis=-1, keepdims=True)
    return (values * lax.rsqrt(mean_sq + EPSILON) * gain).astype(BF16)


def dot(a, b):
    return jnp.dot(a, b, preferred_element_type=F32)


def dot_t(a, b):
    return lax.dot_general(a, b, (((1,), (1,)), ((), ())), preferred_element_type=F32)


def kernel(
    bins,
    slabs,
    bin_phase_hbm,
    phase_bias_hbm,
    corner_hbm,
    window_bias_hbm,
    gain1_hbm,
    gain2_hbm,
    gain3_hbm,
    vol,
    w_qkv1_hbm,
    w_out1_hbm,
    w_qkv2_hbm,
    w_out2_hbm,
    w_up_hbm,
    w_down_hbm,
    out,
    bin_phase,
    phase_bias,
    corner,
    window_bias,
    gain1,
    gain2,
    gain3,
    w_qkv1,
    w_out1,
    w_qkv2,
    w_out2,
    w_up,
    w_down,
    got,
    sent,
    ext,
    queries,
    keys,
    values,
    attended,
    phase_table,
    window_table,
    table_sem,
    weight_sem,
    local_sem,
    own_sem,
    send_sem,
    recv_sem,
):
    me = lax.axis_index("phase")
    slab = lax.axis_index("space")
    planes, blocks = vol.shape[0], vol.shape[1]
    heads = 8
    scale = 1.0 / math.sqrt(32)
    unscale = math.sqrt(32)
    rate = scale * math.log2(math.e)
    reach = planes - 1
    assert planes == 4
    not_first = slab > 0
    not_last = slab < slabs - 1

    barrier = pltpu.get_barrier_semaphore()

    @pl.loop(1, bins)
    def _(i):
        pl.semaphore_signal(
            barrier, inc=1, device_id={"phase": lax.rem(me + i, bins)}, device_id_type=MESH
        )

    @pl.when(not_first)
    def _():
        pl.semaphore_signal(barrier, inc=1, device_id={"space": slab - 1}, device_id_type=MESH)

    @pl.when(not_last)
    def _():
        pl.semaphore_signal(barrier, inc=1, device_id={"space": slab + 1}, device_id_type=MESH)

    table_copies = [
        pltpu.make_async_copy(source, target, table_sem.at[i])
        for i, (source, target) in enumerate(
            [
                (bin_phase_hbm, bin_phase),
                (phase_bias_hbm, phase_bias),
                (corner_hbm, corner),
                (window_bias_hbm, window_bias),
            ]
        )
    ]
    for copy in table_copies:
        copy.start()
    weight_copies = [
        pltpu.make_async_copy(source, target, weight_sem.at[i])
        for i, (source, target) in enumerate(
            [
                (gain1_hbm, gain1),
                (w_qkv1_hbm, w_qkv1),
                (w_out1_hbm, w_out1),
                (gain2_hbm, gain2),
                (w_qkv2_hbm, w_qkv2),
                (w_out2_hbm, w_out2),
                (gain3_hbm, gain3),
                (w_up_hbm, w_up),
                (w_down_hbm, w_down),
            ]
        )
    ]
    for copy in weight_copies:
        copy.start()
    own_in = pltpu.make_async_copy(vol.at[:, me], got.at[:, me], local_sem.at[0])
    own_in.start()

    for copy in table_copies:
        copy.wait()
    lane = lax.broadcasted_iota(jnp.int32, (1, 128), 1)

    lane_bin = lax.broadcasted_iota(jnp.int32, (bins, 128), 1) // 8
    row_bin = lax.broadcasted_iota(jnp.int32, (bins, 128), 0)
    there = jnp.zeros((bins, 128), jnp.int32)
    here = jnp.zeros((bins, 128), jnp.int32)
    for c in range(bins):
        there = jnp.where(lane_bin == c, bin_phase[c], there)
        here = jnp.where(row_bin == c, bin_phase[c], here)
    gap = there - here
    gap = jnp.where(gap < 0, gap + bins, gap)
    same = (
        lax.broadcasted_iota(jnp.int32, (bins, 8, 128), 1)
        == lax.broadcasted_iota(jnp.int32, (bins, 8, 128), 2) % 8
    )
    for h in range(heads):
        level = jnp.zeros((bins, 128), F32)
        for k in range(bins):
            level = jnp.where(gap == k, phase_bias[h, k] * unscale, level)
        table = jnp.where(same, jnp.broadcast_to(level[:, None, :], (bins, 8, 128)), MASKED)
        phase_table[h] = table.reshape(128, 128)

    @pl.when(jnp.logical_not(not_first))
    def _():
        ext[0:reach] = jnp.zeros((reach, blocks, 8, 256), BF16)

    @pl.when(jnp.logical_not(not_last))
    def _():
        ext[reach + planes :] = jnp.zeros((reach, blocks, 8, 256), BF16)

    sides = not_first.astype(jnp.int32) + not_last.astype(jnp.int32)
    pl.semaphore_wait(barrier, bins - 1 + sides)

    def gather(plane):
        @pl.loop(1, bins)
        def _(i):
            peer = lax.rem(me + i, bins)
            pltpu.make_async_remote_copy(
                src_ref=vol.at[plane, peer],
                dst_ref=got.at[plane, me],
                send_sem=send_sem.at[plane],
                recv_sem=recv_sem.at[plane],
                device_id={"phase": peer},
                device_id_type=MESH,
            ).start()

    gather(1)
    gather(2)
    row = lax.broadcasted_iota(jnp.int32, (128, 128), 0)
    column = lax.broadcasted_iota(jnp.int32, (128, 128), 1)
    step_x = column // 32 - row // 32
    step_y = column % 32 - row % 32
    window_table[4 * heads] = jnp.full((128, 128), MASKED, F32)

    @pl.loop(0, heads)
    def _(h):
        b = step_x - corner[1, h]
        c = step_y - corner[2, h]
        inside = (b >= 0) & (b < 4) & (c >= 0) & (c < 4)
        code = jnp.where(inside, 4 * b + c, 16)
        for a in range(4):
            table = jnp.full((128, 128), MASKED, F32)
            for j in range(16):
                table = jnp.where(code == j, window_bias[h, 16 * a + j] * unscale, table)
            window_table[4 * h + a] = table

    gather(0)
    gather(3)

    head_lanes = [(lane // 32) == i for i in range(4)]
    head_keep = [m.astype(F32).astype(BF16) for m in head_lanes]

    def attend(plane):
        stream = got[plane].astype(F32).reshape(128, 256)
        triple = dot(normed(stream, gain1[...]), w_qkv1[...]).astype(BF16)
        mixed = []
        for p in range(1):
            tiles = []
            for t in range(2):
                q = triple[128 * p : 128 * p + 128, 128 * t : 128 * t + 128]
                k = triple[128 * p : 128 * p + 128, 256 + 128 * t : 384 + 128 * t]
                v = triple[128 * p : 128 * p + 128, 512 + 128 * t : 640 + 128 * t]
                both = jnp.concatenate([v, jnp.ones((128, 128), BF16)], axis=1)
                stacked = jnp.concatenate([q * keep for keep in head_keep], axis=0)
                z = dot_t(stacked, k) + phase_table[4 * t : 4 * t + 4].reshape(512, 128)
                peak = jnp.max(z, axis=1, keepdims=True)
                weight = jnp.exp2((z - peak) * rate).astype(BF16)
                summed = dot(weight, both)
                top = summed[:128, :128]
                low = summed[:128, 128:]
                for i in range(1, 4):
                    top = jnp.where(head_lanes[i], summed[128 * i : 128 * i + 128, :128], top)
                    low = jnp.where(head_lanes[i], summed[128 * i : 128 * i + 128, 128:], low)
                tiles.append((top / low).astype(BF16))
            mixed.append(jnp.concatenate(tiles, axis=1))
        residual = stream + dot(jnp.concatenate(mixed, axis=0), w_out1[...])
        sent[plane] = residual.astype(BF16).reshape(blocks, 8, 256)

    even = lax.rem(slab, 2) == 0
    low, high = 0, reach + planes
    partner = jnp.where(even, slab + 1, slab - 1)
    partner_slot = jnp.where(even, low, high + 1)
    held_slot = jnp.where(even, high + 1, low)
    onward = jnp.where(even, slab + 2, slab - 2)
    sends_on = (onward >= 0) & (onward < slabs)
    taken_from = jnp.where(even, slab - 2, slab + 2)
    takes = (taken_from >= 0) & (taken_from < slabs)

    def to_owner(plane):
        pltpu.make_async_copy(
            sent.at[plane, me], ext.at[reach + plane, me], own_sem.at[plane]
        ).start()

        @pl.loop(1, bins)
        def _(i):
            peer = lax.rem(me + i, bins)
            pltpu.make_async_remote_copy(
                src_ref=sent.at[plane, peer],
                dst_ref=ext.at[reach + plane, me],
                send_sem=send_sem.at[4 + plane],
                recv_sem=recv_sem.at[4 + plane],
                device_id={"phase": peer},
                device_id_type=MESH,
            ).start()

    def to_slab(plane, slot, target, sem):
        @pl.loop(0, bins)
        def _(i):
            peer = lax.rem(me + i, bins)
            pltpu.make_async_remote_copy(
                src_ref=sent.at[plane, peer],
                dst_ref=ext.at[slot, me],
                send_sem=send_sem.at[sem],
                recv_sem=recv_sem.at[sem],
                device_id={"phase": peer, "space": target},
                device_id_type=MESH,
            ).start()

    def arrived(ref, sem):
        pltpu.make_async_copy(ref, ref, sem).wait()

    others = got.at[0, pl.ds(0, bins - 1)]

    def owned(plane):
        pltpu.make_async_copy(
            sent.at[plane, me], ext.at[reach + plane, me], own_sem.at[plane]
        ).wait()
        arrived(others, recv_sem.at[4 + plane])

    own_in.wait()
    for copy in weight_copies[:3]:
        copy.wait()
    for plane in (1, 2):
        arrived(others, recv_sem.at[plane])
        attend(plane)
        to_slab(plane, partner_slot + plane - 1, partner, 7 + plane)
        to_owner(plane)
    arrived(others, recv_sem.at[0])
    attend(0)
    @pl.when(not_first)
    def _():
        to_slab(0, high, slab - 1, 10)

    to_owner(0)
    arrived(others, recv_sem.at[3])
    attend(3)
    @pl.when(not_last)
    def _():
        to_slab(3, low + reach - 1, slab + 1, 11)

    to_owner(3)

    def forward(i):
        return pltpu.make_async_remote_copy(
            src_ref=ext.at[held_slot + i],
            dst_ref=ext.at[partner_slot + i],
            send_sem=send_sem.at[12 + i],
            recv_sem=recv_sem.at[12 + i],
            device_id={"space": onward},
            device_id_type=MESH,
        )

    for i in range(2):
        arrived(ext.at[0], recv_sem.at[8 + i])

        @pl.when(sends_on)
        def _():
            forward(i).start()

    for copy in weight_copies[3:5]:
        copy.wait()

    def project(plane, inner):
        stream = ext[plane].astype(F32).reshape(128, 256)
        if inner is None:
            pair = dot(normed(stream, gain2[...]), w_qkv2[:, 256:]).astype(BF16)
            keys[plane] = pair[:, :256]
            values[plane] = pair[:, 256:]
        else:
            triple = dot(normed(stream, gain2[...]), w_qkv2[...]).astype(BF16)
            queries[inner] = triple[:, :256]
            keys[plane] = triple[:, 256:512]
            values[plane] = triple[:, 512:]

    for i in range(2):
        project(held_slot + i, None)
    owned(1)
    owned(2)
    for g in (1, 2):
        project(reach + g, g)
    owned(0)
    owned(3)
    for g in (0, 3):
        project(reach + g, g)

    @pl.when(not_first)
    def _():
        arrived(ext.at[0], recv_sem.at[11])

    @pl.when(not_last)
    def _():
        arrived(ext.at[0], recv_sem.at[10])

    for slot in (low + reach - 1, high):
        project(slot, None)

    @pl.when(takes)
    def _():
        arrived(ext.at[0], recv_sem.at[12])
        arrived(ext.at[0], recv_sem.at[13])

    for i in range(2):
        project(partner_slot + i, None)

    for copy in weight_copies[5:]:
        copy.wait()

    depth = planes * slabs

    def look(g):
        tiles = []
        for t in range(2):
            lanes = slice(128 * t, 128 * t + 128)
            q = queries[g, :, lanes]
            top = jnp.zeros((128, 128), F32)
            low = jnp.ones((128, 128), F32)
            for i in range(4):
                h = 4 * t + i
                low_z = g + corner[0, h]
                first = low_z + reach
                k = keys[pl.ds(first, 4), :, lanes].reshape(512, 128)
                v = values[pl.ds(first, 4), :, lanes].reshape(512, 128)
                parts = []
                for a in range(4):
                    z_key = slab * planes + low_z + a
                    outside = (z_key < 0) | (z_key >= depth)
                    parts.append(window_table[jnp.where(outside, 4 * heads, 4 * h + a)])
                z = dot_t(q * head_keep[i], k) + jnp.concatenate(parts, axis=1)
                peak = jnp.max(z, axis=1, keepdims=True)
                weight = jnp.exp2((z - peak) * rate).astype(BF16)
                both = jnp.concatenate([v, jnp.ones((512, 128), BF16)], axis=1)
                summed = dot(weight, both)
                top = jnp.where(head_lanes[i], summed[:, :128], top)
                low = jnp.where(head_lanes[i], summed[:, 128:], low)
            tiles.append((top / low).astype(BF16))
        attended[g] = jnp.concatenate(tiles, axis=1)

    for g in range(planes):
        look(g)
    half = planes // 2
    for part in range(2):
        here = half * part
        rows = 128 * half
        mixed = attended[here : here + half].reshape(rows, 256)
        residual = ext[reach + here : reach + here + half].astype(F32).reshape(rows, 256) + dot(mixed, w_out2[...])
        rise = dot(normed(residual, gain3[...]), w_up[...])
        slope = math.sqrt(2.0 / math.pi)
        bend = jnp.tanh(rise * (slope + (0.044715 * slope) * (rise * rise)))
        level = 0.5 * rise
        hidden = level + level * bend
        final = residual + dot(hidden.astype(BF16), w_down[...])
        out[here : here + half] = final.reshape(half, 128, 256)

    for sem in range(8):
        arrived(others, send_sem.at[sem])
    for sem in (8, 9):
        arrived(ext.at[0], send_sem.at[sem])

    @pl.when(not_first)
    def _():
        arrived(ext.at[0], send_sem.at[10])

    @pl.when(not_last)
    def _():
        arrived(ext.at[0], send_sem.at[11])

    @pl.when(sends_on)
    def _():
        forward(0).wait_send()
        forward(1).wait_send()


def solution(mesh):
    bins, slabs = mesh.shape["phase"], mesh.shape["space"]

    def local(
        volume,
        gain_first,
        phase_qkv,
        phase_out,
        bin_phase,
        phase_bias,
        gain_second,
        window_qkv,
        window_out,
        window_corner,
        window_bias,
        gain_third,
        mlp_up,
        mlp_down,
    ):
        _, planes, extent_x, extent_y, width = volume.shape
        tokens = extent_x * extent_y
        blocks = tokens // 8
        reach = planes - 1
        deep = planes + 2 * reach
        vmem = pl.BlockSpec(memory_space=pltpu.VMEM)
        hbm = pl.BlockSpec(memory_space=pl.ANY)
        weights = (phase_qkv, phase_out, window_qkv, window_out, mlp_up, mlp_down)
        result = pl.pallas_call(
            functools.partial(kernel, bins, slabs),
            out_shape=pltpu.VMEM((planes, tokens, width), F32),
            in_specs=[hbm] * 14,
            out_specs=vmem,
            scratch_shapes=[
                pltpu.SMEM(bin_phase.shape, jnp.int32),
                pltpu.SMEM(phase_bias.shape, F32),
                pltpu.SMEM(window_corner.shape[::-1], jnp.int32),
                pltpu.SMEM(window_bias.shape, F32),
            ]
            + [pltpu.VMEM((1, width), F32)] * 3
            + [pltpu.VMEM(w.shape, BF16) for w in weights]
            + [
                pltpu.VMEM((planes, blocks, 8, width), BF16),
                pltpu.VMEM((planes, blocks, 8, width), BF16),
                pltpu.VMEM((deep, blocks, 8, width), BF16),
                pltpu.VMEM((planes, tokens, width), BF16),
                pltpu.VMEM((deep, tokens, width), BF16),
                pltpu.VMEM((deep, tokens, width), BF16),
                pltpu.VMEM((planes, tokens, width), BF16),
                pltpu.VMEM((8, 128, 128), F32),
                pltpu.VMEM((33, 128, 128), F32),
                pltpu.SemaphoreType.DMA((4,)),
                pltpu.SemaphoreType.DMA((9,)),
                pltpu.SemaphoreType.DMA((4,)),
                pltpu.SemaphoreType.DMA((4,)),
                pltpu.SemaphoreType.DMA((14,)),
                pltpu.SemaphoreType.DMA((14,)),
            ],
            compiler_params=pltpu.CompilerParams(collective_id=0, has_side_effects=True),
        )(
            bin_phase,
            phase_bias,
            window_corner.T,
            window_bias,
            gain_first.reshape(1, width),
            gain_second.reshape(1, width),
            gain_third.reshape(1, width),
            volume.reshape(planes, blocks, 8, width),
            *weights,
        )
        return result.astype(BF16).reshape(volume.shape)

    split = P("phase", "space", None, None, None)
    return jax.shard_map(
        local,
        mesh=mesh,
        in_specs=(split,) + (P(),) * 13,
        out_specs=split,
        check_vma=False,
    )
```

```python
import functools
import math

import jax
import jax.numpy as jnp
from jax import lax
from jax.experimental import pallas as pl
from jax.experimental.pallas import tpu as pltpu
from jax.sharding import PartitionSpec as P

MESH = pl.DeviceIdType.MESH
EPSILON = 1e-06
MASKED = -1e30
F32 = jnp.float32
BF16 = jnp.bfloat16


def normed(values, gain):
    mean_sq = jnp.mean(values * values, axis=-1, keepdims=True)
    return (values * lax.rsqrt(mean_sq + EPSILON) * gain).astype(BF16)


def dot(a, b):
    return jnp.dot(a, b, preferred_element_type=F32)


def dot_t(a, b):
    return lax.dot_general(a, b, (((1,), (1,)), ((), ())), preferred_element_type=F32)


def kernel(
    bins,
    slabs,
    bin_phase_hbm,
    phase_bias_hbm,
    corner_hbm,
    window_bias_hbm,
    gain1_hbm,
    gain2_hbm,
    gain3_hbm,
    vol,
    w_qkv1_hbm,
    w_out1_hbm,
    w_qkv2_hbm,
    w_out2_hbm,
    w_up_hbm,
    w_down_hbm,
    out,
    bin_phase,
    phase_bias,
    corner,
    window_bias,
    gain1,
    gain2,
    gain3,
    w_qkv1,
    w_out1,
    w_qkv2,
    w_out2,
    w_up,
    w_down,
    got,
    sent,
    ext,
    queries,
    keys,
    values,
    phase_table,
    window_table,
    tops,
    lows,
    highs,
    table_sem,
    weight_sem,
    local_sem,
    own_sem,
    send_sem,
    recv_sem,
):
    me = lax.axis_index("phase")
    slab = lax.axis_index("space")
    planes, blocks = vol.shape[0], vol.shape[1]
    heads = 8
    scale = 1.0 / math.sqrt(32)
    unscale = math.sqrt(32)
    rate = scale * math.log2(math.e)
    reach = planes - 1
    assert planes == 4
    not_first = slab > 0
    not_last = slab < slabs - 1

    barrier = pltpu.get_barrier_semaphore()

    @pl.loop(1, bins)
    def _(i):
        pl.semaphore_signal(
            barrier, inc=1, device_id={"phase": lax.rem(me + i, bins)}, device_id_type=MESH
        )

    @pl.when(not_first)
    def _():
        pl.semaphore_signal(barrier, inc=1, device_id={"space": slab - 1}, device_id_type=MESH)

    @pl.when(not_last)
    def _():
        pl.semaphore_signal(barrier, inc=1, device_id={"space": slab + 1}, device_id_type=MESH)

    table_copies = [
        pltpu.make_async_copy(source, target, table_sem.at[i])
        for i, (source, target) in enumerate(
            [
                (bin_phase_hbm, bin_phase),
                (phase_bias_hbm, phase_bias),
                (corner_hbm, corner),
                (window_bias_hbm, window_bias),
            ]
        )
    ]
    for copy in table_copies:
        copy.start()
    weight_copies = [
        pltpu.make_async_copy(source, target, weight_sem.at[i])
        for i, (source, target) in enumerate(
            [
                (gain1_hbm, gain1),
                (w_qkv1_hbm, w_qkv1),
                (w_out1_hbm, w_out1),
                (gain2_hbm, gain2),
                (w_qkv2_hbm, w_qkv2),
                (w_out2_hbm, w_out2),
                (gain3_hbm, gain3),
                (w_up_hbm, w_up),
                (w_down_hbm, w_down),
            ]
        )
    ]
    for copy in weight_copies:
        copy.start()
    own_in = pltpu.make_async_copy(vol.at[:, me], got.at[:, me], local_sem.at[0])
    own_in.start()

    for copy in table_copies:
        copy.wait()
    lane = lax.broadcasted_iota(jnp.int32, (1, 128), 1)

    lane_bin = lax.broadcasted_iota(jnp.int32, (bins, 128), 1) // 8
    row_bin = lax.broadcasted_iota(jnp.int32, (bins, 128), 0)
    there = jnp.zeros((bins, 128), jnp.int32)
    here = jnp.zeros((bins, 128), jnp.int32)
    for c in range(bins):
        there = jnp.where(lane_bin == c, bin_phase[c], there)
        here = jnp.where(row_bin == c, bin_phase[c], here)
    gap = there - here
    gap = jnp.where(gap < 0, gap + bins, gap)
    same = (
        lax.broadcasted_iota(jnp.int32, (bins, 8, 128), 1)
        == lax.broadcasted_iota(jnp.int32, (bins, 8, 128), 2) % 8
    )
    for h in range(heads):
        level = jnp.zeros((bins, 128), F32)
        for k in range(bins):
            level = jnp.where(gap == k, phase_bias[h, k] * unscale, level)
        table = jnp.where(same, jnp.broadcast_to(level[:, None, :], (bins, 8, 128)), MASKED)
        phase_table[h] = table.reshape(128, 128)

    @pl.when(jnp.logical_not(not_first))
    def _():
        ext[0:reach] = jnp.zeros((reach, blocks, 8, 256), BF16)

    @pl.when(jnp.logical_not(not_last))
    def _():
        ext[reach + planes :] = jnp.zeros((reach, blocks, 8, 256), BF16)

    sides = not_first.astype(jnp.int32) + not_last.astype(jnp.int32)
    pl.semaphore_wait(barrier, bins - 1 + sides)

    def gather(plane):
        @pl.loop(1, bins)
        def _(i):
            peer = lax.rem(me + i, bins)
            pltpu.make_async_remote_copy(
                src_ref=vol.at[plane, peer],
                dst_ref=got.at[plane, me],
                send_sem=send_sem.at[plane],
                recv_sem=recv_sem.at[plane],
                device_id={"phase": peer},
                device_id_type=MESH,
            ).start()

    gather(1)
    gather(2)
    row = lax.broadcasted_iota(jnp.int32, (32, 128), 0)
    column = lax.broadcasted_iota(jnp.int32, (32, 128), 1)
    key = lax.rem(column, 64)
    step_x = key // 16 - row // 8
    step_y = lax.rem(key, 16) - lax.rem(row, 8) - 4
    one_end = (lax.rem(row, 8) < 4) == (lax.rem(key, 16) < 8)
    masked = jnp.full((32, 128), MASKED, F32)

    @pl.loop(0, heads)
    def _(h):
        b = step_x - corner[1, h]
        c = step_y - corner[2, h]
        inside = (b >= 0) & (b < 4) & (c >= 0) & (c < 4)
        code = jnp.where(inside, 4 * b + c, 16)
        steps = []
        for a in range(4):
            table = masked
            for j in range(16):
                table = jnp.where(code == j, window_bias[h, 16 * a + j] * unscale, table)
            steps.append(table)
        for ends in range(2):
            sides = [jnp.where(one_end, table, MASKED) if ends else table for table in steps] + [masked]
            for left in range(5):
                for right in range(5):
                    window_table[2 * h + ends, 5 * left + right] = jnp.where(
                        column < 64, sides[left], sides[right]
                    )

    gather(0)
    gather(3)

    head_lanes = [(lane // 32) == i for i in range(4)]
    head_keep = [m.astype(F32).astype(BF16) for m in head_lanes]

    def attend(plane):
        stream = got[plane].astype(F32).reshape(128, 256)
        triple = dot(normed(stream, gain1[...]), w_qkv1[...]).astype(BF16)
        mixed = []
        for p in range(1):
            tiles = []
            for t in range(2):
                q = triple[128 * p : 128 * p + 128, 128 * t : 128 * t + 128]
                k = triple[128 * p : 128 * p + 128, 256 + 128 * t : 384 + 128 * t]
                v = triple[128 * p : 128 * p + 128, 512 + 128 * t : 640 + 128 * t]
                both = jnp.concatenate([v, jnp.ones((128, 128), BF16)], axis=1)
                stacked = jnp.concatenate([q * keep for keep in head_keep], axis=0)
                z = dot_t(stacked, k) + phase_table[4 * t : 4 * t + 4].reshape(512, 128)
                peak = jnp.max(z, axis=1, keepdims=True)
                weight = jnp.exp2((z - peak) * rate).astype(BF16)
                summed = dot(weight, both)
                top = summed[:128, :128]
                low = summed[:128, 128:]
                for i in range(1, 4):
                    top = jnp.where(head_lanes[i], summed[128 * i : 128 * i + 128, :128], top)
                    low = jnp.where(head_lanes[i], summed[128 * i : 128 * i + 128, 128:], low)
                tiles.append((top / low).astype(BF16))
            mixed.append(jnp.concatenate(tiles, axis=1))
        residual = stream + dot(jnp.concatenate(mixed, axis=0), w_out1[...])
        sent[plane] = residual.astype(BF16).reshape(blocks, 8, 256)

    even = lax.rem(slab, 2) == 0
    low, high = 0, reach + planes
    partner = jnp.where(even, slab + 1, slab - 1)
    partner_slot = jnp.where(even, low, high + 1)
    held_slot = jnp.where(even, high + 1, low)
    onward = jnp.where(even, slab + 2, slab - 2)
    sends_on = (onward >= 0) & (onward < slabs)
    taken_from = jnp.where(even, slab - 2, slab + 2)
    takes = (taken_from >= 0) & (taken_from < slabs)

    def to_owner(plane):
        pltpu.make_async_copy(
            sent.at[plane, me], ext.at[reach + plane, me], own_sem.at[plane]
        ).start()

        for i in range(1, bins):
            peer = lax.rem(me + i, bins)
            pltpu.make_async_remote_copy(
                src_ref=sent.at[plane, peer],
                dst_ref=ext.at[reach + plane, me],
                send_sem=send_sem.at[4 + plane],
                recv_sem=recv_sem.at[4 + plane],
                device_id={"phase": peer},
                device_id_type=MESH,
            ).start()

    def to_slab(plane, slot, target, sem):
        for i in range(bins):
            peer = lax.rem(me + i, bins)
            pltpu.make_async_remote_copy(
                src_ref=sent.at[plane, peer],
                dst_ref=ext.at[slot, me],
                send_sem=send_sem.at[sem],
                recv_sem=recv_sem.at[sem],
                device_id={"phase": peer, "space": target},
                device_id_type=MESH,
            ).start()

    def arrived(ref, sem):
        pltpu.make_async_copy(ref, ref, sem).wait()

    others = got.at[0, pl.ds(0, bins - 1)]

    def owned(plane):
        pltpu.make_async_copy(
            sent.at[plane, me], ext.at[reach + plane, me], own_sem.at[plane]
        ).wait()
        arrived(others, recv_sem.at[4 + plane])

    own_in.wait()
    for copy in weight_copies[:3]:
        copy.wait()
    arrived(others, recv_sem.at[1])
    attend(1)
    arrived(others, recv_sem.at[2])
    to_slab(1, partner_slot, partner, 8)
    to_owner(1)
    attend(2)
    arrived(others, recv_sem.at[0])
    to_slab(2, partner_slot + 1, partner, 9)
    to_owner(2)
    attend(0)
    arrived(others, recv_sem.at[3])
    to_owner(0)
    attend(3)
    to_owner(3)

    @pl.when(not_first)
    def _():
        to_slab(0, high, slab - 1, 10)

    @pl.when(not_last)
    def _():
        to_slab(3, low + reach - 1, slab + 1, 11)

    def forward(i):
        return pltpu.make_async_remote_copy(
            src_ref=ext.at[held_slot + i],
            dst_ref=ext.at[partner_slot + i],
            send_sem=send_sem.at[12 + i],
            recv_sem=recv_sem.at[12 + i],
            device_id={"space": onward},
            device_id_type=MESH,
        )

    for copy in weight_copies[3:5]:
        copy.wait()

    def banded(target, plane, rows):
        blocked = rows.reshape(4, 4, 8, 256)
        for b in range(4):
            near = blocked[:, b : b + 1]
            far = blocked[:, (b + 1) % 4 : (b + 1) % 4 + 1]
            target[plane, b] = jnp.concatenate([near, far], axis=1).reshape(64, 256).astype(BF16)

    def project(plane, inner):
        stream = ext[plane].astype(F32).reshape(128, 256)
        if inner is None:
            pair = dot(normed(stream, gain2[...]), w_qkv2[:, 256:])
        else:
            triple = dot(normed(stream, gain2[...]), w_qkv2[...])
            turned = [pltpu.roll(triple[32 * x : 32 * x + 32, :256], 28, 0) for x in range(4)]
            for b in range(4):
                queries[inner, 32 * b : 32 * b + 32] = jnp.concatenate(
                    [turned[x][8 * b : 8 * b + 8] for x in range(4)], axis=0
                ).astype(BF16)
            pair = triple[:, 256:]
        banded(keys, plane, pair[:, :256])
        banded(values, plane, pair[:, 256:])

    depth = planes * slabs

    def entries(query_planes, key_planes):
        found = []
        for h in range(heads):
            rows = []
            for g in query_planes:
                steps = []
                for k in key_planes:
                    a = k - g - corner[0, h]
                    z = slab * planes + k
                    usable = (a >= 0) & (a < 4) & (z >= 0) & (z < depth)
                    steps.append(jnp.where(usable, a, 4))
                rows.append([5 * steps[j] + steps[j + 1] for j in range(0, len(steps), 2)])
            found.append(rows)
        return found

    def look(query_planes, key_planes, merge):
        entry = entries(query_planes, key_planes)
        count = len(query_planes)
        size = 32 * count
        for t in range(2):
            lanes = slice(128 * t, 128 * t + 128)
            for b in range(4):
                q = jnp.concatenate([queries[g, 32 * b : 32 * b + 32, lanes] for g in query_planes], axis=0)
                stacked = jnp.concatenate([q * keep for keep in head_keep], axis=0)
                k = jnp.concatenate([keys[p + reach, b, :, lanes] for p in key_planes], axis=0)
                v = jnp.concatenate([values[p + reach, b, :, lanes] for p in key_planes], axis=0)
                both = jnp.concatenate([v, jnp.ones(v.shape, BF16)], axis=1)
                table = jnp.concatenate(
                    [
                        jnp.concatenate([window_table[2 * h + b // 3, e] for e in rows], axis=1)
                        for h in range(4 * t, 4 * t + 4)
                        for rows in entry[h]
                    ],
                    axis=0,
                )
                z = dot_t(stacked, k) + table
                peak = jnp.max(z, axis=1, keepdims=True)
                weight = jnp.exp2((z - peak) * rate).astype(BF16)
                summed = dot(weight, both)
                top = summed[:size, :128]
                low = summed[:size, 128:]
                high = jnp.broadcast_to(peak[:size], (size, 128))
                for i in range(1, 4):
                    part = slice(size * i, size * i + size)
                    top = jnp.where(head_lanes[i], summed[part, :128], top)
                    low = jnp.where(head_lanes[i], summed[part, 128:], low)
                    high = jnp.where(head_lanes[i], peak[part], high)
                top = top.reshape(count, 32, 128)
                low = low.reshape(count, 32, 128)
                high = high.reshape(count, 32, 128)
                at = (t, b, pl.ds(query_planes[0], count))
                if merge:
                    before = highs[at]
                    peak = jnp.maximum(before, high)
                    old = jnp.exp2((before - peak) * rate)
                    new = jnp.exp2((high - peak) * rate)
                    top = tops[at] * old + top * new
                    low = lows[at] * old + low * new
                    high = peak
                tops[at] = top
                lows[at] = low
                highs[at] = high

    for i in range(2):
        arrived(ext.at[0], recv_sem.at[8 + i])

        @pl.when(sends_on)
        def _():
            forward(i).start()

        owned(1 + i)
        project(held_slot + i, None)
        project(reach + 1 + i, 1 + i)
    owned(0)
    owned(3)
    for g in (0, 3):
        project(reach + g, g)

    look(range(planes), range(planes), False)

    @pl.when(not_first)
    def _():
        arrived(ext.at[0], recv_sem.at[11])

    @pl.when(not_last)
    def _():
        arrived(ext.at[0], recv_sem.at[10])

    for slot in (low + reach - 1, high):
        project(slot, None)

    ahead = jnp.where(even, 2, 0)
    behind = 2 - ahead
    look([ahead, ahead + 1], [held_slot - reach, held_slot - reach + 1, -1, planes], True)
    for copy in weight_copies[5:]:
        copy.wait()

    def finish(first):
        rows = []
        for j in range(2):
            tiles = []
            for t in range(2):
                share = [tops[t, b, first + j] / lows[t, b, first + j] for b in range(4)]
                turned = [
                    jnp.concatenate([share[b][8 * x : 8 * x + 8] for b in range(4)], axis=0) for x in range(4)
                ]
                tiles.append(jnp.concatenate([pltpu.roll(part, 4, 0) for part in turned], axis=0))
            rows.append(jnp.concatenate(tiles, axis=1))
        mixed = jnp.concatenate(rows, axis=0).astype(BF16)
        stream = ext[pl.ds(reach + first, 2)].astype(F32).reshape(256, 256)
        residual = stream + dot(mixed, w_out2[...])
        rise = dot(normed(residual, gain3[...]), w_up[...])
        slope = math.sqrt(2.0 / math.pi)
        bend = jnp.tanh(rise * (slope + (0.044715 * slope) * (rise * rise)))
        level = 0.5 * rise
        hidden = level + level * bend
        final = residual + dot(hidden.astype(BF16), w_down[...])
        out[pl.ds(first, 2)] = final.reshape(2, 128, 256)


    @pl.when(takes)
    def _():
        arrived(ext.at[0], recv_sem.at[12])
        arrived(ext.at[0], recv_sem.at[13])

    for i in range(2):
        project(partner_slot + i, None)

    look([behind, behind + 1], [partner_slot - reach, partner_slot - reach + 1, -1, planes], True)
    finish(0)
    finish(2)

    for sem in range(8):
        arrived(others, send_sem.at[sem])
    for sem in (8, 9):
        arrived(ext.at[0], send_sem.at[sem])

    @pl.when(not_first)
    def _():
        arrived(ext.at[0], send_sem.at[10])

    @pl.when(not_last)
    def _():
        arrived(ext.at[0], send_sem.at[11])

    @pl.when(sends_on)
    def _():
        forward(0).wait_send()
        forward(1).wait_send()


def solution(mesh):
    bins, slabs = mesh.shape["phase"], mesh.shape["space"]

    def local(
        volume,
        gain_first,
        phase_qkv,
        phase_out,
        bin_phase,
        phase_bias,
        gain_second,
        window_qkv,
        window_out,
        window_corner,
        window_bias,
        gain_third,
        mlp_up,
        mlp_down,
    ):
        _, planes, extent_x, extent_y, width = volume.shape
        tokens = extent_x * extent_y
        blocks = tokens // 8
        reach = planes - 1
        deep = planes + 2 * reach
        vmem = pl.BlockSpec(memory_space=pltpu.VMEM)
        hbm = pl.BlockSpec(memory_space=pl.ANY)
        weights = (phase_qkv, phase_out, window_qkv, window_out, mlp_up, mlp_down)
        result = pl.pallas_call(
            functools.partial(kernel, bins, slabs),
            out_shape=pltpu.VMEM((planes, tokens, width), F32),
            in_specs=[hbm] * 14,
            out_specs=vmem,
            scratch_shapes=[
                pltpu.SMEM(bin_phase.shape, jnp.int32),
                pltpu.SMEM(phase_bias.shape, F32),
                pltpu.SMEM(window_corner.shape[::-1], jnp.int32),
                pltpu.SMEM(window_bias.shape, F32),
            ]
            + [pltpu.VMEM((1, width), F32)] * 3
            + [pltpu.VMEM(w.shape, BF16) for w in weights]
            + [
                pltpu.VMEM((planes, blocks, 8, width), BF16),
                pltpu.VMEM((planes, blocks, 8, width), BF16),
                pltpu.VMEM((deep, blocks, 8, width), BF16),
                pltpu.VMEM((planes, tokens, width), BF16),
                pltpu.VMEM((deep, 4, 64, width), BF16),
                pltpu.VMEM((deep, 4, 64, width), BF16),
                pltpu.VMEM((8, 128, 128), F32),
                pltpu.VMEM((16, 25, 32, 128), F32),
                pltpu.VMEM((2, 4, planes, 32, 128), F32),
                pltpu.VMEM((2, 4, planes, 32, 128), F32),
                pltpu.VMEM((2, 4, planes, 32, 128), F32),
                pltpu.SemaphoreType.DMA((4,)),
                pltpu.SemaphoreType.DMA((9,)),
                pltpu.SemaphoreType.DMA((4,)),
                pltpu.SemaphoreType.DMA((4,)),
                pltpu.SemaphoreType.DMA((14,)),
                pltpu.SemaphoreType.DMA((14,)),
            ],
            compiler_params=pltpu.CompilerParams(collective_id=0, has_side_effects=True),
        )(
            bin_phase,
            phase_bias,
            window_corner.T,
            window_bias,
            gain_first.reshape(1, width),
            gain_second.reshape(1, width),
            gain_third.reshape(1, width),
            volume.reshape(planes, blocks, 8, width),
            *weights,
        )
        return result.astype(BF16).reshape(volume.shape)

    split = P("phase", "space", None, None, None)
    return jax.shard_map(
        local,
        mesh=mesh,
        in_specs=(split,) + (P(),) * 13,
        out_specs=split,
        check_vma=False,
    )
```

```python
import functools
import math

import jax
import jax.numpy as jnp
from jax import lax
from jax.experimental import pallas as pl
from jax.experimental.pallas import tpu as pltpu
from jax.sharding import PartitionSpec as P

MESH = pl.DeviceIdType.MESH
EPSILON = 1e-06
MASKED = -1e30
F32 = jnp.float32
BF16 = jnp.bfloat16


def normed(values, gain):
    mean_sq = jnp.mean(values * values, axis=-1, keepdims=True)
    return (values * lax.rsqrt(mean_sq + EPSILON) * gain).astype(BF16)


def dot(a, b):
    return jnp.dot(a, b, preferred_element_type=F32)


def dot_t(a, b):
    return lax.dot_general(a, b, (((1,), (1,)), ((), ())), preferred_element_type=F32)


def kernel(
    bins,
    slabs,
    bin_phase_hbm,
    phase_bias_hbm,
    corner_hbm,
    window_bias_hbm,
    gain1_hbm,
    gain2_hbm,
    gain3_hbm,
    vol,
    w_qkv1_hbm,
    w_out1_hbm,
    w_qkv2_hbm,
    w_out2_hbm,
    w_up_hbm,
    w_down_hbm,
    out,
    bin_phase,
    phase_bias,
    corner,
    window_bias,
    gain1,
    gain2,
    gain3,
    w_qkv1,
    w_out1,
    w_qkv2,
    w_out2,
    w_up,
    w_down,
    got,
    sent,
    ext,
    queries,
    keys,
    values,
    phase_table,
    window_table,
    tops,
    lows,
    highs,
    table_sem,
    weight_sem,
    local_sem,
    own_sem,
    send_sem,
    recv_sem,
):
    me = lax.axis_index("phase")
    slab = lax.axis_index("space")
    planes, blocks = vol.shape[0], vol.shape[1]
    heads = 8
    scale = 1.0 / math.sqrt(32)
    unscale = math.sqrt(32)
    rate = scale * math.log2(math.e)
    reach = planes - 1
    assert planes == 4
    not_first = slab > 0
    not_last = slab < slabs - 1

    barrier = pltpu.get_barrier_semaphore()
    assert bins == 16
    flips = [v * (1 - 2 * lax.rem(lax.div(me, v), 2)) for v in (1, 2, 4, 8)]
    peers = [
        me + sum(flips[j] for j in range(4) if m >> j & 1)
        for m in (12, 13, 4, 5, 10, 11, 14, 15, 8, 9, 2, 3, 6, 7, 1)
    ]
    slab_peers = [
        me + sum(flips[j] for j in range(4) if m >> j & 1)
        for m in (4, 5, 12, 13, 2, 3, 6, 7, 0, 1, 10, 11, 14, 15, 8, 9)
    ]

    for peer in peers:
        pl.semaphore_signal(barrier, inc=1, device_id={"phase": peer}, device_id_type=MESH)

    @pl.when(not_first)
    def _():
        pl.semaphore_signal(barrier, inc=1, device_id={"space": slab - 1}, device_id_type=MESH)

    @pl.when(not_last)
    def _():
        pl.semaphore_signal(barrier, inc=1, device_id={"space": slab + 1}, device_id_type=MESH)

    table_copies = [
        pltpu.make_async_copy(source, target, table_sem.at[i])
        for i, (source, target) in enumerate(
            [
                (bin_phase_hbm, bin_phase),
                (phase_bias_hbm, phase_bias),
                (corner_hbm, corner),
                (window_bias_hbm, window_bias),
            ]
        )
    ]
    for copy in table_copies:
        copy.start()
    weight_copies = [
        pltpu.make_async_copy(source, target, weight_sem.at[i])
        for i, (source, target) in enumerate(
            [
                (gain1_hbm, gain1),
                (w_qkv1_hbm, w_qkv1),
                (w_out1_hbm, w_out1),
                (gain2_hbm, gain2),
                (w_qkv2_hbm, w_qkv2),
                (w_out2_hbm, w_out2),
                (gain3_hbm, gain3),
                (w_up_hbm, w_up),
                (w_down_hbm, w_down),
            ]
        )
    ]
    for copy in weight_copies:
        copy.start()
    own_in = pltpu.make_async_copy(vol.at[:, me], got.at[:, me], local_sem.at[0])
    own_in.start()

    for copy in table_copies:
        copy.wait()
    lane = lax.broadcasted_iota(jnp.int32, (1, 128), 1)

    lane_bin = lax.broadcasted_iota(jnp.int32, (bins, 128), 1) // 8
    row_bin = lax.broadcasted_iota(jnp.int32, (bins, 128), 0)
    there = jnp.zeros((bins, 128), jnp.int32)
    here = jnp.zeros((bins, 128), jnp.int32)
    for c in range(bins):
        there = jnp.where(lane_bin == c, bin_phase[c], there)
        here = jnp.where(row_bin == c, bin_phase[c], here)
    gap = there - here
    gap = jnp.where(gap < 0, gap + bins, gap)
    same = (
        lax.broadcasted_iota(jnp.int32, (bins, 8, 128), 1)
        == lax.broadcasted_iota(jnp.int32, (bins, 8, 128), 2) % 8
    )
    for h in range(heads):
        level = jnp.zeros((bins, 128), F32)
        for k in range(bins):
            level = jnp.where(gap == k, phase_bias[h, k] * unscale, level)
        table = jnp.where(same, jnp.broadcast_to(level[:, None, :], (bins, 8, 128)), MASKED)
        phase_table[h] = table.reshape(128, 128)

    @pl.when(jnp.logical_not(not_first))
    def _():
        ext[0:reach] = jnp.zeros((reach, blocks, 8, 256), BF16)

    @pl.when(jnp.logical_not(not_last))
    def _():
        ext[reach + planes :] = jnp.zeros((reach, blocks, 8, 256), BF16)

    sides = not_first.astype(jnp.int32) + not_last.astype(jnp.int32)
    pl.semaphore_wait(barrier, bins - 1 + sides)

    def gather(plane):
        for peer in peers:
            pltpu.make_async_remote_copy(
                src_ref=vol.at[plane, peer],
                dst_ref=got.at[plane, me],
                send_sem=send_sem.at[plane],
                recv_sem=recv_sem.at[plane],
                device_id={"phase": peer},
                device_id_type=MESH,
            ).start()

    gather(1)
    gather(2)
    row = lax.broadcasted_iota(jnp.int32, (32, 128), 0)
    column = lax.broadcasted_iota(jnp.int32, (32, 128), 1)
    key = lax.rem(column, 64)
    step_x = key // 16 - row // 8
    step_y = lax.rem(key, 16) - lax.rem(row, 8) - 4
    one_end = (lax.rem(row, 8) < 4) == (lax.rem(key, 16) < 8)
    masked = jnp.full((32, 128), MASKED, F32)

    @pl.loop(0, heads)
    def _(h):
        b = step_x - corner[1, h]
        c = step_y - corner[2, h]
        inside = (b >= 0) & (b < 4) & (c >= 0) & (c < 4)
        code = jnp.where(inside, 4 * b + c, 16)
        steps = []
        for a in range(4):
            table = masked
            for j in range(16):
                table = jnp.where(code == j, window_bias[h, 16 * a + j] * unscale, table)
            steps.append(table)
        for ends in range(2):
            sides = [jnp.where(one_end, table, MASKED) if ends else table for table in steps] + [masked]
            for left in range(5):
                for right in range(5):
                    window_table[2 * h + ends, 5 * left + right] = jnp.where(
                        column < 64, sides[left], sides[right]
                    )

    gather(0)
    gather(3)

    head_lanes = [(lane // 32) == i for i in range(4)]
    head_keep = [m.astype(F32).astype(BF16) for m in head_lanes]

    def attend(plane):
        stream = got[plane].astype(F32).reshape(128, 256)
        triple = dot(normed(stream, gain1[...]), w_qkv1[...]).astype(BF16)
        mixed = []
        for p in range(1):
            tiles = []
            for t in range(2):
                q = triple[128 * p : 128 * p + 128, 128 * t : 128 * t + 128]
                k = triple[128 * p : 128 * p + 128, 256 + 128 * t : 384 + 128 * t]
                v = triple[128 * p : 128 * p + 128, 512 + 128 * t : 640 + 128 * t]
                both = jnp.concatenate([v, jnp.ones((128, 128), BF16)], axis=1)
                stacked = jnp.concatenate([q * keep for keep in head_keep], axis=0)
                z = dot_t(stacked, k) + phase_table[4 * t : 4 * t + 4].reshape(512, 128)
                peak = jnp.max(z, axis=1, keepdims=True)
                weight = jnp.exp2((z - peak) * rate).astype(BF16)
                summed = dot(weight, both)
                top = summed[:128, :128]
                low = summed[:128, 128:]
                for i in range(1, 4):
                    top = jnp.where(head_lanes[i], summed[128 * i : 128 * i + 128, :128], top)
                    low = jnp.where(head_lanes[i], summed[128 * i : 128 * i + 128, 128:], low)
                tiles.append((top / low).astype(BF16))
            mixed.append(jnp.concatenate(tiles, axis=1))
        residual = stream + dot(jnp.concatenate(mixed, axis=0), w_out1[...])
        sent[plane] = residual.astype(BF16).reshape(blocks, 8, 256)

    even = lax.rem(slab, 2) == 0
    low, high = 0, reach + planes
    partner = jnp.where(even, slab + 1, slab - 1)
    partner_slot = jnp.where(even, low, high + 1)
    held_slot = jnp.where(even, high + 1, low)
    onward = jnp.where(even, slab + 2, slab - 2)
    sends_on = (onward >= 0) & (onward < slabs)
    taken_from = jnp.where(even, slab - 2, slab + 2)
    takes = (taken_from >= 0) & (taken_from < slabs)

    def to_owner(plane):
        pltpu.make_async_copy(
            sent.at[plane, me], ext.at[reach + plane, me], own_sem.at[plane]
        ).start()

        for peer in peers:
            pltpu.make_async_remote_copy(
                src_ref=sent.at[plane, peer],
                dst_ref=ext.at[reach + plane, me],
                send_sem=send_sem.at[4 + plane],
                recv_sem=recv_sem.at[4 + plane],
                device_id={"phase": peer},
                device_id_type=MESH,
            ).start()

    def to_slab(plane, slot, target, sem):
        for peer in slab_peers:
            pltpu.make_async_remote_copy(
                src_ref=sent.at[plane, peer],
                dst_ref=ext.at[slot, me],
                send_sem=send_sem.at[sem],
                recv_sem=recv_sem.at[sem],
                device_id={"phase": peer, "space": target},
                device_id_type=MESH,
            ).start()

    def arrived(ref, sem):
        pltpu.make_async_copy(ref, ref, sem).wait()

    others = got.at[0, pl.ds(0, bins - 1)]

    def owned(plane):
        pltpu.make_async_copy(
            sent.at[plane, me], ext.at[reach + plane, me], own_sem.at[plane]
        ).wait()
        arrived(others, recv_sem.at[4 + plane])

    own_in.wait()
    for copy in weight_copies[:3]:
        copy.wait()
    arrived(others, recv_sem.at[1])
    attend(1)
    arrived(others, recv_sem.at[2])
    to_slab(1, partner_slot, partner, 8)
    to_owner(1)
    attend(2)
    arrived(others, recv_sem.at[0])
    to_slab(2, partner_slot + 1, partner, 9)
    to_owner(2)
    attend(0)
    arrived(others, recv_sem.at[3])
    to_owner(0)
    attend(3)
    to_owner(3)

    @pl.when(not_first)
    def _():
        to_slab(0, high, slab - 1, 10)

    @pl.when(not_last)
    def _():
        to_slab(3, low + reach - 1, slab + 1, 11)

    def forward(i):
        return pltpu.make_async_remote_copy(
            src_ref=ext.at[held_slot + i],
            dst_ref=ext.at[partner_slot + i],
            send_sem=send_sem.at[12 + i],
            recv_sem=recv_sem.at[12 + i],
            device_id={"space": onward},
            device_id_type=MESH,
        )

    for copy in weight_copies[3:5]:
        copy.wait()

    def banded(target, plane, rows):
        blocked = rows.reshape(4, 4, 8, 256)
        for b in range(4):
            near = blocked[:, b : b + 1]
            far = blocked[:, (b + 1) % 4 : (b + 1) % 4 + 1]
            target[plane, b] = jnp.concatenate([near, far], axis=1).reshape(64, 256).astype(BF16)

    def project(plane, inner):
        stream = ext[plane].astype(F32).reshape(128, 256)
        if inner is None:
            pair = dot(normed(stream, gain2[...]), w_qkv2[:, 256:])
        else:
            triple = dot(normed(stream, gain2[...]), w_qkv2[...])
            turned = [pltpu.roll(triple[32 * x : 32 * x + 32, :256], 28, 0) for x in range(4)]
            for b in range(4):
                queries[inner, 32 * b : 32 * b + 32] = jnp.concatenate(
                    [turned[x][8 * b : 8 * b + 8] for x in range(4)], axis=0
                ).astype(BF16)
            pair = triple[:, 256:]
        banded(keys, plane, pair[:, :256])
        banded(values, plane, pair[:, 256:])

    depth = planes * slabs

    def entries(query_planes, key_planes):
        found = []
        for h in range(heads):
            rows = []
            for g in query_planes:
                steps = []
                for k in key_planes:
                    a = k - g - corner[0, h]
                    z = slab * planes + k
                    usable = (a >= 0) & (a < 4) & (z >= 0) & (z < depth)
                    steps.append(jnp.where(usable, a, 4))
                rows.append([5 * steps[j] + steps[j + 1] for j in range(0, len(steps), 2)])
            found.append(rows)
        return found

    def look(query_planes, key_planes, merge):
        entry = entries(query_planes, key_planes)
        count = len(query_planes)
        size = 32 * count
        for t in range(2):
            lanes = slice(128 * t, 128 * t + 128)
            for b in range(4):
                q = jnp.concatenate([queries[g, 32 * b : 32 * b + 32, lanes] for g in query_planes], axis=0)
                stacked = jnp.concatenate([q * keep for keep in head_keep], axis=0)
                k = jnp.concatenate([keys[p + reach, b, :, lanes] for p in key_planes], axis=0)
                v = jnp.concatenate([values[p + reach, b, :, lanes] for p in key_planes], axis=0)
                both = jnp.concatenate([v, jnp.ones(v.shape, BF16)], axis=1)
                table = jnp.concatenate(
                    [
                        jnp.concatenate([window_table[2 * h + b // 3, e] for e in rows], axis=1)
                        for h in range(4 * t, 4 * t + 4)
                        for rows in entry[h]
                    ],
                    axis=0,
                )
                z = dot_t(stacked, k) + table
                peak = jnp.max(z, axis=1, keepdims=True)
                weight = jnp.exp2((z - peak) * rate).astype(BF16)
                summed = dot(weight, both)
                top = summed[:size, :128]
                low = summed[:size, 128:]
                high = jnp.broadcast_to(peak[:size], (size, 128))
                for i in range(1, 4):
                    part = slice(size * i, size * i + size)
                    top = jnp.where(head_lanes[i], summed[part, :128], top)
                    low = jnp.where(head_lanes[i], summed[part, 128:], low)
                    high = jnp.where(head_lanes[i], peak[part], high)
                top = top.reshape(count, 32, 128)
                low = low.reshape(count, 32, 128)
                high = high.reshape(count, 32, 128)
                at = (t, b, pl.ds(query_planes[0], count))
                if merge:
                    before = highs[at]
                    peak = jnp.maximum(before, high)
                    old = jnp.exp2((before - peak) * rate)
                    new = jnp.exp2((high - peak) * rate)
                    top = tops[at] * old + top * new
                    low = lows[at] * old + low * new
                    high = peak
                tops[at] = top
                lows[at] = low
                highs[at] = high

    for i in range(2):
        arrived(ext.at[0], recv_sem.at[8 + i])

        @pl.when(sends_on)
        def _():
            forward(i).start()

        owned(1 + i)
        project(held_slot + i, None)
        project(reach + 1 + i, 1 + i)
    owned(0)
    owned(3)
    for g in (0, 3):
        project(reach + g, g)

    look(range(planes), range(planes), False)

    @pl.when(not_first)
    def _():
        arrived(ext.at[0], recv_sem.at[11])

    @pl.when(not_last)
    def _():
        arrived(ext.at[0], recv_sem.at[10])

    for slot in (low + reach - 1, high):
        project(slot, None)

    ahead = jnp.where(even, 2, 0)
    behind = 2 - ahead
    look([ahead, ahead + 1], [held_slot - reach, held_slot - reach + 1, -1, planes], True)
    for copy in weight_copies[5:]:
        copy.wait()

    def finish(first):
        rows = []
        for j in range(2):
            tiles = []
            for t in range(2):
                share = [tops[t, b, first + j] / lows[t, b, first + j] for b in range(4)]
                turned = [
                    jnp.concatenate([share[b][8 * x : 8 * x + 8] for b in range(4)], axis=0) for x in range(4)
                ]
                tiles.append(jnp.concatenate([pltpu.roll(part, 4, 0) for part in turned], axis=0))
            rows.append(jnp.concatenate(tiles, axis=1))
        mixed = jnp.concatenate(rows, axis=0).astype(BF16)
        stream = ext[pl.ds(reach + first, 2)].astype(F32).reshape(256, 256)
        residual = stream + dot(mixed, w_out2[...])
        rise = dot(normed(residual, gain3[...]), w_up[...])
        slope = math.sqrt(2.0 / math.pi)
        bend = jnp.tanh(rise * (slope + (0.044715 * slope) * (rise * rise)))
        level = 0.5 * rise
        hidden = level + level * bend
        final = residual + dot(hidden.astype(BF16), w_down[...])
        out[pl.ds(first, 2)] = final.reshape(2, 128, 256)


    @pl.when(takes)
    def _():
        arrived(ext.at[0], recv_sem.at[12])
        arrived(ext.at[0], recv_sem.at[13])

    for i in range(2):
        project(partner_slot + i, None)

    look([behind, behind + 1], [partner_slot - reach, partner_slot - reach + 1, -1, planes], True)
    finish(0)
    finish(2)

    for sem in range(8):
        arrived(others, send_sem.at[sem])
    for sem in (8, 9):
        arrived(ext.at[0], send_sem.at[sem])

    @pl.when(not_first)
    def _():
        arrived(ext.at[0], send_sem.at[10])

    @pl.when(not_last)
    def _():
        arrived(ext.at[0], send_sem.at[11])

    @pl.when(sends_on)
    def _():
        forward(0).wait_send()
        forward(1).wait_send()


def solution(mesh):
    bins, slabs = mesh.shape["phase"], mesh.shape["space"]

    def local(
        volume,
        gain_first,
        phase_qkv,
        phase_out,
        bin_phase,
        phase_bias,
        gain_second,
        window_qkv,
        window_out,
        window_corner,
        window_bias,
        gain_third,
        mlp_up,
        mlp_down,
    ):
        _, planes, extent_x, extent_y, width = volume.shape
        tokens = extent_x * extent_y
        blocks = tokens // 8
        reach = planes - 1
        deep = planes + 2 * reach
        vmem = pl.BlockSpec(memory_space=pltpu.VMEM)
        hbm = pl.BlockSpec(memory_space=pl.ANY)
        weights = (phase_qkv, phase_out, window_qkv, window_out, mlp_up, mlp_down)
        result = pl.pallas_call(
            functools.partial(kernel, bins, slabs),
            out_shape=pltpu.VMEM((planes, tokens, width), F32),
            in_specs=[hbm] * 14,
            out_specs=vmem,
            scratch_shapes=[
                pltpu.SMEM(bin_phase.shape, jnp.int32),
                pltpu.SMEM(phase_bias.shape, F32),
                pltpu.SMEM(window_corner.shape[::-1], jnp.int32),
                pltpu.SMEM(window_bias.shape, F32),
            ]
            + [pltpu.VMEM((1, width), F32)] * 3
            + [pltpu.VMEM(w.shape, BF16) for w in weights]
            + [
                pltpu.VMEM((planes, blocks, 8, width), BF16),
                pltpu.VMEM((planes, blocks, 8, width), BF16),
                pltpu.VMEM((deep, blocks, 8, width), BF16),
                pltpu.VMEM((planes, tokens, width), BF16),
                pltpu.VMEM((deep, 4, 64, width), BF16),
                pltpu.VMEM((deep, 4, 64, width), BF16),
                pltpu.VMEM((8, 128, 128), F32),
                pltpu.VMEM((16, 25, 32, 128), F32),
                pltpu.VMEM((2, 4, planes, 32, 128), F32),
                pltpu.VMEM((2, 4, planes, 32, 128), F32),
                pltpu.VMEM((2, 4, planes, 32, 128), F32),
                pltpu.SemaphoreType.DMA((4,)),
                pltpu.SemaphoreType.DMA((9,)),
                pltpu.SemaphoreType.DMA((4,)),
                pltpu.SemaphoreType.DMA((4,)),
                pltpu.SemaphoreType.DMA((14,)),
                pltpu.SemaphoreType.DMA((14,)),
            ],
            compiler_params=pltpu.CompilerParams(collective_id=0, has_side_effects=True),
        )(
            bin_phase,
            phase_bias,
            window_corner.T,
            window_bias,
            gain_first.reshape(1, width),
            gain_second.reshape(1, width),
            gain_third.reshape(1, width),
            volume.reshape(planes, blocks, 8, width),
            *weights,
        )
        return result.astype(BF16).reshape(volume.shape)

    split = P("phase", "space", None, None, None)
    return jax.shard_map(
        local,
        mesh=mesh,
        in_specs=(split,) + (P(),) * 13,
        out_specs=split,
        check_vma=False,
    )
```

```python
import functools
import math

import jax
import jax.numpy as jnp
from jax import lax
from jax.experimental import pallas as pl
from jax.experimental.pallas import tpu as pltpu
from jax.sharding import PartitionSpec as P

MESH = pl.DeviceIdType.MESH
EPSILON = 1e-06
MASKED = -1e30
F32 = jnp.float32
BF16 = jnp.bfloat16


def normed(values, gain):
    mean_sq = jnp.mean(values * values, axis=-1, keepdims=True)
    return (values * lax.rsqrt(mean_sq + EPSILON) * gain).astype(BF16)


def dot(a, b):
    return jnp.dot(a, b, preferred_element_type=F32)


def dot_t(a, b):
    return lax.dot_general(a, b, (((1,), (1,)), ((), ())), preferred_element_type=F32)


def kernel(
    bins,
    slabs,
    bin_phase_hbm,
    phase_bias_hbm,
    corner_hbm,
    window_bias_hbm,
    gain1_hbm,
    gain2_hbm,
    gain3_hbm,
    vol,
    w_qkv1_hbm,
    w_out1_hbm,
    w_qkv2_hbm,
    w_out2_hbm,
    w_up_hbm,
    w_down_hbm,
    out,
    bin_phase,
    phase_bias,
    corner,
    window_bias,
    gain1,
    gain2,
    gain3,
    w_qkv1,
    w_out1,
    w_qkv2,
    w_out2,
    w_up,
    w_down,
    got,
    sent,
    ext,
    queries,
    keys,
    values,
    phase_table,
    window_table,
    tops,
    lows,
    highs,
    table_sem,
    weight_sem,
    local_sem,
    own_sem,
    send_sem,
    recv_sem,
):
    me = lax.axis_index("phase")
    slab = lax.axis_index("space")
    planes, blocks = vol.shape[0], vol.shape[1]
    heads = 8
    scale = 1.0 / math.sqrt(32)
    unscale = math.sqrt(32)
    rate = scale * math.log2(math.e)
    reach = planes - 1
    assert planes == 4
    not_first = slab > 0
    not_last = slab < slabs - 1

    barrier = pltpu.get_barrier_semaphore()
    assert bins == 16
    flips = [v * (1 - 2 * lax.rem(lax.div(me, v), 2)) for v in (1, 2, 4, 8)]
    peers = [
        me + sum(flips[j] for j in range(4) if m >> j & 1)
        for m in (12, 13, 4, 5, 10, 11, 14, 15, 8, 9, 2, 3, 6, 7, 1)
    ]
    slab_peers = [
        me + sum(flips[j] for j in range(4) if m >> j & 1)
        for m in (4, 5, 12, 13, 2, 3, 6, 7, 0, 1, 10, 11, 14, 15, 8, 9)
    ]

    for peer in peers:
        pl.semaphore_signal(barrier, inc=1, device_id={"phase": peer}, device_id_type=MESH)

    @pl.when(not_first)
    def _():
        pl.semaphore_signal(barrier, inc=1, device_id={"space": slab - 1}, device_id_type=MESH)

    @pl.when(not_last)
    def _():
        pl.semaphore_signal(barrier, inc=1, device_id={"space": slab + 1}, device_id_type=MESH)

    table_copies = [
        pltpu.make_async_copy(source, target, table_sem.at[i])
        for i, (source, target) in enumerate(
            [
                (bin_phase_hbm, bin_phase),
                (phase_bias_hbm, phase_bias),
                (corner_hbm, corner),
                (window_bias_hbm, window_bias),
            ]
        )
    ]
    for copy in table_copies:
        copy.start()
    weight_copies = [
        pltpu.make_async_copy(source, target, weight_sem.at[i])
        for i, (source, target) in enumerate(
            [
                (gain1_hbm, gain1),
                (w_qkv1_hbm, w_qkv1),
                (w_out1_hbm, w_out1),
                (gain2_hbm, gain2),
                (w_qkv2_hbm, w_qkv2),
                (w_out2_hbm, w_out2),
                (gain3_hbm, gain3),
                (w_up_hbm, w_up),
                (w_down_hbm, w_down),
            ]
        )
    ]
    for copy in weight_copies:
        copy.start()
    own_in = pltpu.make_async_copy(vol.at[:, me], got.at[:, me], local_sem.at[0])
    own_in.start()

    for copy in table_copies:
        copy.wait()
    lane = lax.broadcasted_iota(jnp.int32, (1, 128), 1)

    lane_bin = lax.broadcasted_iota(jnp.int32, (bins, 128), 1) // 8
    row_bin = lax.broadcasted_iota(jnp.int32, (bins, 128), 0)
    there = jnp.zeros((bins, 128), jnp.int32)
    here = jnp.zeros((bins, 128), jnp.int32)
    for c in range(bins):
        there = jnp.where(lane_bin == c, bin_phase[c], there)
        here = jnp.where(row_bin == c, bin_phase[c], here)
    gap = there - here
    gap = jnp.where(gap < 0, gap + bins, gap)
    same = (
        lax.broadcasted_iota(jnp.int32, (bins, 8, 128), 1)
        == lax.broadcasted_iota(jnp.int32, (bins, 8, 128), 2) % 8
    )
    for h in range(heads):
        level = jnp.zeros((bins, 128), F32)
        for k in range(bins):
            level = jnp.where(gap == k, phase_bias[h, k] * unscale, level)
        table = jnp.where(same, jnp.broadcast_to(level[:, None, :], (bins, 8, 128)), MASKED)
        phase_table[h] = table.reshape(128, 128)

    @pl.when(jnp.logical_not(not_first))
    def _():
        ext[0:reach] = jnp.zeros((reach, blocks, 8, 256), BF16)

    @pl.when(jnp.logical_not(not_last))
    def _():
        ext[reach + planes :] = jnp.zeros((reach, blocks, 8, 256), BF16)

    sides = not_first.astype(jnp.int32) + not_last.astype(jnp.int32)
    pl.semaphore_wait(barrier, bins - 1 + sides)

    def gather(plane):
        for peer in peers:
            pltpu.make_async_remote_copy(
                src_ref=vol.at[plane, peer],
                dst_ref=got.at[plane, me],
                send_sem=send_sem.at[plane],
                recv_sem=recv_sem.at[plane],
                device_id={"phase": peer},
                device_id_type=MESH,
            ).start()

    gather(1)
    gather(2)
    row = lax.broadcasted_iota(jnp.int32, (32, 128), 0)
    column = lax.broadcasted_iota(jnp.int32, (32, 128), 1)
    key = lax.rem(column, 64)
    step_x = key // 16 - row // 8
    step_y = lax.rem(key, 16) - lax.rem(row, 8) - 4
    one_end = (lax.rem(row, 8) < 4) == (lax.rem(key, 16) < 8)
    masked = jnp.full((32, 128), MASKED, F32)

    @pl.loop(0, heads)
    def _(h):
        b = step_x - corner[1, h]
        c = step_y - corner[2, h]
        inside = (b >= 0) & (b < 4) & (c >= 0) & (c < 4)
        code = jnp.where(inside, 4 * b + c, 16)
        steps = []
        for a in range(4):
            table = masked
            for j in range(16):
                table = jnp.where(code == j, window_bias[h, 16 * a + j] * unscale, table)
            steps.append(table)
        for ends in range(2):
            sides = [jnp.where(one_end, table, MASKED) if ends else table for table in steps] + [masked]
            for left in range(5):
                for right in range(5):
                    window_table[2 * h + ends, 5 * left + right] = jnp.where(
                        column < 64, sides[left], sides[right]
                    )

    gather(0)
    gather(3)

    head_lanes = [(lane // 32) == i for i in range(4)]
    head_keep = [m.astype(F32).astype(BF16) for m in head_lanes]

    def attend(plane):
        stream = got[plane].astype(F32).reshape(128, 256)
        triple = dot(normed(stream, gain1[...]), w_qkv1[...]).astype(BF16)
        mixed = []
        for p in range(1):
            tiles = []
            for t in range(2):
                q = triple[128 * p : 128 * p + 128, 128 * t : 128 * t + 128]
                k = triple[128 * p : 128 * p + 128, 256 + 128 * t : 384 + 128 * t]
                v = triple[128 * p : 128 * p + 128, 512 + 128 * t : 640 + 128 * t]
                both = jnp.concatenate([v, jnp.ones((128, 128), BF16)], axis=1)
                stacked = jnp.concatenate([q * keep for keep in head_keep], axis=0)
                z = dot_t(stacked, k) + phase_table[4 * t : 4 * t + 4].reshape(512, 128)
                peak = jnp.max(z, axis=1, keepdims=True)
                weight = jnp.exp2((z - peak) * rate).astype(BF16)
                summed = dot(weight, both)
                top = summed[:128, :128]
                low = summed[:128, 128:]
                for i in range(1, 4):
                    top = jnp.where(head_lanes[i], summed[128 * i : 128 * i + 128, :128], top)
                    low = jnp.where(head_lanes[i], summed[128 * i : 128 * i + 128, 128:], low)
                tiles.append((top / low).astype(BF16))
            mixed.append(jnp.concatenate(tiles, axis=1))
        residual = stream + dot(jnp.concatenate(mixed, axis=0), w_out1[...])
        sent[plane] = residual.astype(BF16).reshape(blocks, 8, 256)

    even = lax.rem(slab, 2) == 0
    low, high = 0, reach + planes
    partner = jnp.where(even, slab + 1, slab - 1)
    partner_slot = jnp.where(even, low, high + 1)
    held_slot = jnp.where(even, high + 1, low)
    onward = jnp.where(even, slab + 2, slab - 2)
    sends_on = (onward >= 0) & (onward < slabs)
    taken_from = jnp.where(even, slab - 2, slab + 2)
    takes = (taken_from >= 0) & (taken_from < slabs)

    def to_owner(plane):
        pltpu.make_async_copy(
            sent.at[plane, me], ext.at[reach + plane, me], own_sem.at[plane]
        ).start()

        for peer in peers:
            pltpu.make_async_remote_copy(
                src_ref=sent.at[plane, peer],
                dst_ref=ext.at[reach + plane, me],
                send_sem=send_sem.at[4 + plane],
                recv_sem=recv_sem.at[4 + plane],
                device_id={"phase": peer},
                device_id_type=MESH,
            ).start()

    def to_slab(plane, slot, target, sem):
        for peer in slab_peers:
            pltpu.make_async_remote_copy(
                src_ref=sent.at[plane, peer],
                dst_ref=ext.at[slot, me],
                send_sem=send_sem.at[sem],
                recv_sem=recv_sem.at[sem],
                device_id={"phase": peer, "space": target},
                device_id_type=MESH,
            ).start()

    def arrived(ref, sem):
        pltpu.make_async_copy(ref, ref, sem).wait()

    others = got.at[0, pl.ds(0, bins - 1)]

    def owned(plane):
        pltpu.make_async_copy(
            sent.at[plane, me], ext.at[reach + plane, me], own_sem.at[plane]
        ).wait()
        arrived(others, recv_sem.at[4 + plane])

    own_in.wait()
    for copy in weight_copies[:3]:
        copy.wait()
    arrived(others, recv_sem.at[1])
    attend(1)
    arrived(others, recv_sem.at[2])
    to_slab(1, partner_slot, partner, 8)
    to_owner(1)
    attend(2)
    arrived(others, recv_sem.at[0])
    to_slab(2, partner_slot + 1, partner, 9)
    to_owner(2)
    attend(0)
    arrived(others, recv_sem.at[3])
    to_owner(0)
    attend(3)
    to_owner(3)

    @pl.when(not_first)
    def _():
        to_slab(0, high, slab - 1, 10)

    @pl.when(not_last)
    def _():
        to_slab(3, low + reach - 1, slab + 1, 11)

    def forward(i):
        return pltpu.make_async_remote_copy(
            src_ref=ext.at[held_slot + i],
            dst_ref=ext.at[partner_slot + i],
            send_sem=send_sem.at[12 + i],
            recv_sem=recv_sem.at[12 + i],
            device_id={"space": onward},
            device_id_type=MESH,
        )

    for copy in weight_copies[3:5]:
        copy.wait()

    def banded(target, plane, rows):
        blocked = rows.reshape(4, 4, 8, 256)
        for b in range(4):
            near = blocked[:, b : b + 1]
            far = blocked[:, (b + 1) % 4 : (b + 1) % 4 + 1]
            target[plane, b] = jnp.concatenate([near, far], axis=1).reshape(64, 256).astype(BF16)

    def project(plane, inner):
        stream = ext[plane].astype(F32).reshape(128, 256)
        if inner is None:
            pair = dot(normed(stream, gain2[...]), w_qkv2[:, 256:])
        else:
            triple = dot(normed(stream, gain2[...]), w_qkv2[...])
            turned = [pltpu.roll(triple[32 * x : 32 * x + 32, :256], 28, 0) for x in range(4)]
            for b in range(4):
                queries[inner, 32 * b : 32 * b + 32] = jnp.concatenate(
                    [turned[x][8 * b : 8 * b + 8] for x in range(4)], axis=0
                ).astype(BF16)
            pair = triple[:, 256:]
        banded(keys, plane, pair[:, :256])
        banded(values, plane, pair[:, 256:])

    depth = planes * slabs

    def entries(query_planes, key_planes):
        found = []
        for h in range(heads):
            rows = []
            for g in query_planes:
                steps = []
                for k in key_planes:
                    a = k - g - corner[0, h]
                    z = slab * planes + k
                    usable = (a >= 0) & (a < 4) & (z >= 0) & (z < depth)
                    steps.append(jnp.where(usable, a, 4))
                rows.append([5 * steps[j] + steps[j + 1] for j in range(0, len(steps), 2)])
            found.append(rows)
        return found

    def look(query_planes, key_planes, merge):
        entry = entries(query_planes, key_planes)
        count = len(query_planes)
        size = 32 * count
        for t in range(2):
            lanes = slice(128 * t, 128 * t + 128)
            for b in range(4):
                q = jnp.concatenate([queries[g, 32 * b : 32 * b + 32, lanes] for g in query_planes], axis=0)
                stacked = jnp.concatenate([q * keep for keep in head_keep], axis=0)
                k = jnp.concatenate([keys[p + reach, b, :, lanes] for p in key_planes], axis=0)
                v = jnp.concatenate([values[p + reach, b, :, lanes] for p in key_planes], axis=0)
                both = jnp.concatenate([v, jnp.ones(v.shape, BF16)], axis=1)
                table = jnp.concatenate(
                    [
                        jnp.concatenate([window_table[2 * h + b // 3, e] for e in rows], axis=1)
                        for h in range(4 * t, 4 * t + 4)
                        for rows in entry[h]
                    ],
                    axis=0,
                )
                z = dot_t(stacked, k) + table
                peak = jnp.max(z, axis=1, keepdims=True)
                weight = jnp.exp2((z - peak) * rate).astype(BF16)
                summed = dot(weight, both)
                top = summed[:size, :128]
                low = summed[:size, 128:]
                high = jnp.broadcast_to(peak[:size], (size, 128))
                for i in range(1, 4):
                    part = slice(size * i, size * i + size)
                    top = jnp.where(head_lanes[i], summed[part, :128], top)
                    low = jnp.where(head_lanes[i], summed[part, 128:], low)
                    high = jnp.where(head_lanes[i], peak[part], high)
                top = top.reshape(count, 32, 128)
                low = low.reshape(count, 32, 128)
                high = high.reshape(count, 32, 128)
                at = (t, b, pl.ds(query_planes[0], count))
                if merge:
                    before = highs[at]
                    peak = jnp.maximum(before, high)
                    old = jnp.exp2((before - peak) * rate)
                    new = jnp.exp2((high - peak) * rate)
                    top = tops[at] * old + top * new
                    low = lows[at] * old + low * new
                    high = peak
                tops[at] = top
                lows[at] = low
                highs[at] = high

    for i in range(2):
        arrived(ext.at[0], recv_sem.at[8 + i])

        @pl.when(sends_on)
        def _():
            forward(i).start()

        owned(1 + i)
        project(held_slot + i, None)
        project(reach + 1 + i, 1 + i)
    owned(0)
    owned(3)
    for g in (0, 3):
        project(reach + g, g)

    look(range(planes), range(planes), False)

    @pl.when(not_first)
    def _():
        arrived(ext.at[0], recv_sem.at[11])

    @pl.when(not_last)
    def _():
        arrived(ext.at[0], recv_sem.at[10])

    @pl.when(takes)
    def _():
        arrived(ext.at[0], recv_sem.at[12])
        arrived(ext.at[0], recv_sem.at[13])

    for slot in (low + reach - 1, high):
        project(slot, None)
    for i in range(2):
        project(partner_slot + i, None)

    for copy in weight_copies[5:]:
        copy.wait()
    ahead = jnp.where(even, 2, 0)
    behind = 2 - ahead
    look([ahead, ahead + 1], [held_slot - reach, held_slot - reach + 1, -1, planes], True)
    def finish(first):
        rows = []
        for j in range(2):
            tiles = []
            for t in range(2):
                share = [tops[t, b, first + j] / lows[t, b, first + j] for b in range(4)]
                turned = [
                    jnp.concatenate([share[b][8 * x : 8 * x + 8] for b in range(4)], axis=0) for x in range(4)
                ]
                tiles.append(jnp.concatenate([pltpu.roll(part, 4, 0) for part in turned], axis=0))
            rows.append(jnp.concatenate(tiles, axis=1))
        mixed = jnp.concatenate(rows, axis=0).astype(BF16)
        stream = ext[pl.ds(reach + first, 2)].astype(F32).reshape(256, 256)
        residual = stream + dot(mixed, w_out2[...])
        rise = dot(normed(residual, gain3[...]), w_up[...])
        slope = math.sqrt(2.0 / math.pi)
        bend = jnp.tanh(rise * (slope + (0.044715 * slope) * (rise * rise)))
        level = 0.5 * rise
        hidden = level + level * bend
        final = residual + dot(hidden.astype(BF16), w_down[...])
        out[pl.ds(first, 2)] = final.reshape(2, 128, 256)


    look([behind, behind + 1], [partner_slot - reach, partner_slot - reach + 1, -1, planes], True)
    finish(0)
    finish(2)

    for sem in range(8):
        arrived(others, send_sem.at[sem])
    for sem in (8, 9):
        arrived(ext.at[0], send_sem.at[sem])

    @pl.when(not_first)
    def _():
        arrived(ext.at[0], send_sem.at[10])

    @pl.when(not_last)
    def _():
        arrived(ext.at[0], send_sem.at[11])

    @pl.when(sends_on)
    def _():
        forward(0).wait_send()
        forward(1).wait_send()


def solution(mesh):
    bins, slabs = mesh.shape["phase"], mesh.shape["space"]

    def local(
        volume,
        gain_first,
        phase_qkv,
        phase_out,
        bin_phase,
        phase_bias,
        gain_second,
        window_qkv,
        window_out,
        window_corner,
        window_bias,
        gain_third,
        mlp_up,
        mlp_down,
    ):
        _, planes, extent_x, extent_y, width = volume.shape
        tokens = extent_x * extent_y
        blocks = tokens // 8
        reach = planes - 1
        deep = planes + 2 * reach
        vmem = pl.BlockSpec(memory_space=pltpu.VMEM)
        hbm = pl.BlockSpec(memory_space=pl.ANY)
        weights = (phase_qkv, phase_out, window_qkv, window_out, mlp_up, mlp_down)
        result = pl.pallas_call(
            functools.partial(kernel, bins, slabs),
            out_shape=pltpu.VMEM((planes, tokens, width), F32),
            in_specs=[hbm] * 14,
            out_specs=vmem,
            scratch_shapes=[
                pltpu.SMEM(bin_phase.shape, jnp.int32),
                pltpu.SMEM(phase_bias.shape, F32),
                pltpu.SMEM(window_corner.shape[::-1], jnp.int32),
                pltpu.SMEM(window_bias.shape, F32),
            ]
            + [pltpu.VMEM((1, width), F32)] * 3
            + [pltpu.VMEM(w.shape, BF16) for w in weights]
            + [
                pltpu.VMEM((planes, blocks, 8, width), BF16),
                pltpu.VMEM((planes, blocks, 8, width), BF16),
                pltpu.VMEM((deep, blocks, 8, width), BF16),
                pltpu.VMEM((planes, tokens, width), BF16),
                pltpu.VMEM((deep, 4, 64, width), BF16),
                pltpu.VMEM((deep, 4, 64, width), BF16),
                pltpu.VMEM((8, 128, 128), F32),
                pltpu.VMEM((16, 25, 32, 128), F32),
                pltpu.VMEM((2, 4, planes, 32, 128), F32),
                pltpu.VMEM((2, 4, planes, 32, 128), F32),
                pltpu.VMEM((2, 4, planes, 32, 128), F32),
                pltpu.SemaphoreType.DMA((4,)),
                pltpu.SemaphoreType.DMA((9,)),
                pltpu.SemaphoreType.DMA((4,)),
                pltpu.SemaphoreType.DMA((4,)),
                pltpu.SemaphoreType.DMA((14,)),
                pltpu.SemaphoreType.DMA((14,)),
            ],
            compiler_params=pltpu.CompilerParams(collective_id=0, has_side_effects=True),
        )(
            bin_phase,
            phase_bias,
            window_corner.T,
            window_bias,
            gain_first.reshape(1, width),
            gain_second.reshape(1, width),
            gain_third.reshape(1, width),
            volume.reshape(planes, blocks, 8, width),
            *weights,
        )
        return result.astype(BF16).reshape(volume.shape)

    split = P("phase", "space", None, None, None)
    return jax.shard_map(
        local,
        mesh=mesh,
        in_specs=(split,) + (P(),) * 13,
        out_specs=split,
        check_vma=False,
    )
```

```python
import functools
import math

import jax
import jax.numpy as jnp
from jax import lax
from jax.experimental import pallas as pl
from jax.experimental.pallas import tpu as pltpu
from jax.sharding import PartitionSpec as P

MESH = pl.DeviceIdType.MESH
EPSILON = 1e-06
MASKED = -1e30
F32 = jnp.float32
BF16 = jnp.bfloat16


def normed(values, gain):
    mean_sq = jnp.mean(values * values, axis=-1, keepdims=True)
    return (values * lax.rsqrt(mean_sq + EPSILON) * gain).astype(BF16)


def dot(a, b):
    return jnp.dot(a, b, preferred_element_type=F32)


def dot_t(a, b):
    return lax.dot_general(a, b, (((1,), (1,)), ((), ())), preferred_element_type=F32)


def kernel(
    bins,
    slabs,
    bin_phase_hbm,
    phase_bias_hbm,
    corner_hbm,
    window_bias_hbm,
    gain1_hbm,
    gain2_hbm,
    gain3_hbm,
    vol,
    w_qkv1_hbm,
    w_out1_hbm,
    w_qkv2_hbm,
    w_out2_hbm,
    w_up_hbm,
    w_down_hbm,
    out,
    bin_phase,
    phase_bias,
    corner,
    window_bias,
    gain1,
    gain2,
    gain3,
    w_qkv1,
    w_out1,
    w_qkv2,
    w_out2,
    w_up,
    w_down,
    got,
    sent,
    ext,
    queries,
    keys,
    values,
    phase_table,
    window_table,
    tops,
    lows,
    highs,
    table_sem,
    weight_sem,
    local_sem,
    own_sem,
    send_sem,
    recv_sem,
):
    me = lax.axis_index("phase")
    slab = lax.axis_index("space")
    planes, blocks = vol.shape[0], vol.shape[1]
    heads = 8
    scale = 1.0 / math.sqrt(32)
    unscale = math.sqrt(32)
    rate = scale * math.log2(math.e)
    reach = planes - 1
    assert planes == 4
    not_first = slab > 0
    not_last = slab < slabs - 1

    barrier = pltpu.get_barrier_semaphore()
    assert bins == 16
    flips = [v * (1 - 2 * lax.rem(lax.div(me, v), 2)) for v in (1, 2, 4, 8)]
    peers = [
        me + sum(flips[j] for j in range(4) if m >> j & 1)
        for m in (12, 13, 4, 5, 10, 11, 14, 15, 8, 9, 2, 3, 6, 7, 1)
    ]
    slab_peers = [
        me + sum(flips[j] for j in range(4) if m >> j & 1)
        for m in (4, 5, 12, 13, 2, 3, 6, 7, 0, 1, 10, 11, 14, 15, 8, 9)
    ]

    for peer in peers:
        pl.semaphore_signal(barrier, inc=1, device_id={"phase": peer}, device_id_type=MESH)

    @pl.when(not_first)
    def _():
        pl.semaphore_signal(barrier, inc=1, device_id={"space": slab - 1}, device_id_type=MESH)

    @pl.when(not_last)
    def _():
        pl.semaphore_signal(barrier, inc=1, device_id={"space": slab + 1}, device_id_type=MESH)

    table_copies = [
        pltpu.make_async_copy(source, target, table_sem.at[i])
        for i, (source, target) in enumerate(
            [
                (bin_phase_hbm, bin_phase),
                (phase_bias_hbm, phase_bias),
                (corner_hbm, corner),
                (window_bias_hbm, window_bias),
            ]
        )
    ]
    for copy in table_copies:
        copy.start()
    weight_copies = [
        pltpu.make_async_copy(source, target, weight_sem.at[i])
        for i, (source, target) in enumerate(
            [
                (gain1_hbm, gain1),
                (w_qkv1_hbm, w_qkv1),
                (w_out1_hbm, w_out1),
                (gain2_hbm, gain2),
                (w_qkv2_hbm, w_qkv2),
                (w_out2_hbm, w_out2),
                (gain3_hbm, gain3),
                (w_up_hbm, w_up),
                (w_down_hbm, w_down),
            ]
        )
    ]
    for copy in weight_copies:
        copy.start()
    own_in = pltpu.make_async_copy(vol.at[:, me], got.at[:, me], local_sem.at[0])
    own_in.start()

    for copy in table_copies:
        copy.wait()
    lane = lax.broadcasted_iota(jnp.int32, (1, 128), 1)

    lane_bin = lax.broadcasted_iota(jnp.int32, (bins, 128), 1) // 8
    row_bin = lax.broadcasted_iota(jnp.int32, (bins, 128), 0)
    there = jnp.zeros((bins, 128), jnp.int32)
    here = jnp.zeros((bins, 128), jnp.int32)
    for c in range(bins):
        there = jnp.where(lane_bin == c, bin_phase[c], there)
        here = jnp.where(row_bin == c, bin_phase[c], here)
    gap = there - here
    gap = jnp.where(gap < 0, gap + bins, gap)
    same = (
        lax.broadcasted_iota(jnp.int32, (bins, 8, 128), 1)
        == lax.broadcasted_iota(jnp.int32, (bins, 8, 128), 2) % 8
    )
    for h in range(heads):
        level = jnp.zeros((bins, 128), F32)
        for k in range(bins):
            level = jnp.where(gap == k, phase_bias[h, k] * unscale, level)
        table = jnp.where(same, jnp.broadcast_to(level[:, None, :], (bins, 8, 128)), MASKED)
        phase_table[h] = table.reshape(128, 128)

    @pl.when(jnp.logical_not(not_first))
    def _():
        ext[0:reach] = jnp.zeros((reach, blocks, 8, 256), BF16)

    @pl.when(jnp.logical_not(not_last))
    def _():
        ext[reach + planes :] = jnp.zeros((reach, blocks, 8, 256), BF16)

    sides = not_first.astype(jnp.int32) + not_last.astype(jnp.int32)
    pl.semaphore_wait(barrier, bins - 1 + sides)

    def gather(plane):
        for peer in peers:
            pltpu.make_async_remote_copy(
                src_ref=vol.at[plane, peer],
                dst_ref=got.at[plane, me],
                send_sem=send_sem.at[plane],
                recv_sem=recv_sem.at[plane],
                device_id={"phase": peer},
                device_id_type=MESH,
            ).start()

    gather(1)
    gather(2)
    row = lax.broadcasted_iota(jnp.int32, (32, 128), 0)
    column = lax.broadcasted_iota(jnp.int32, (32, 128), 1)
    key = lax.rem(column, 64)
    step_x = key // 16 - row // 8
    step_y = lax.rem(key, 16) - lax.rem(row, 8) - 4
    one_end = (lax.rem(row, 8) < 4) == (lax.rem(key, 16) < 8)
    masked = jnp.full((32, 128), MASKED, F32)

    @pl.loop(0, heads)
    def _(h):
        b = step_x - corner[1, h]
        c = step_y - corner[2, h]
        inside = (b >= 0) & (b < 4) & (c >= 0) & (c < 4)
        code = jnp.where(inside, 4 * b + c, 16)
        steps = []
        for a in range(4):
            table = masked
            for j in range(16):
                table = jnp.where(code == j, window_bias[h, 16 * a + j] * unscale, table)
            steps.append(table)
        for ends in range(2):
            sides = [jnp.where(one_end, table, MASKED) if ends else table for table in steps] + [masked]
            for left in range(5):
                for right in range(5):
                    window_table[2 * h + ends, 5 * left + right] = jnp.where(
                        column < 64, sides[left], sides[right]
                    )

    gather(0)
    gather(3)

    head_lanes = [(lane // 32) == i for i in range(4)]
    head_keep = [m.astype(F32).astype(BF16) for m in head_lanes]

    def attend(plane):
        stream = got[plane].astype(F32).reshape(128, 256)
        triple = dot(normed(stream, gain1[...]), w_qkv1[...]).astype(BF16)
        mixed = []
        for p in range(1):
            tiles = []
            for t in range(2):
                q = triple[128 * p : 128 * p + 128, 128 * t : 128 * t + 128]
                k = triple[128 * p : 128 * p + 128, 256 + 128 * t : 384 + 128 * t]
                v = triple[128 * p : 128 * p + 128, 512 + 128 * t : 640 + 128 * t]
                both = jnp.concatenate([v, jnp.ones((128, 128), BF16)], axis=1)
                stacked = jnp.concatenate([q * keep for keep in head_keep], axis=0)
                z = dot_t(stacked, k) + phase_table[4 * t : 4 * t + 4].reshape(512, 128)
                peak = jnp.max(z, axis=1, keepdims=True)
                weight = jnp.exp2((z - peak) * rate).astype(BF16)
                summed = dot(weight, both)
                top = summed[:128, :128]
                low = summed[:128, 128:]
                for i in range(1, 4):
                    top = jnp.where(head_lanes[i], summed[128 * i : 128 * i + 128, :128], top)
                    low = jnp.where(head_lanes[i], summed[128 * i : 128 * i + 128, 128:], low)
                tiles.append((top / low).astype(BF16))
            mixed.append(jnp.concatenate(tiles, axis=1))
        residual = stream + dot(jnp.concatenate(mixed, axis=0), w_out1[...])
        sent[plane] = residual.astype(BF16).reshape(blocks, 8, 256)

    even = lax.rem(slab, 2) == 0
    low, high = 0, reach + planes
    partner = jnp.where(even, slab + 1, slab - 1)
    partner_slot = jnp.where(even, low, high + 1)
    held_slot = jnp.where(even, high + 1, low)
    onward = jnp.where(even, slab + 2, slab - 2)
    sends_on = (onward >= 0) & (onward < slabs)
    taken_from = jnp.where(even, slab - 2, slab + 2)
    takes = (taken_from >= 0) & (taken_from < slabs)

    def to_owner(plane):
        pltpu.make_async_copy(
            sent.at[plane, me], ext.at[reach + plane, me], own_sem.at[plane]
        ).start()

        for peer in peers:
            pltpu.make_async_remote_copy(
                src_ref=sent.at[plane, peer],
                dst_ref=ext.at[reach + plane, me],
                send_sem=send_sem.at[4 + plane],
                recv_sem=recv_sem.at[4 + plane],
                device_id={"phase": peer},
                device_id_type=MESH,
            ).start()

    def to_slab(plane, slot, target, sem):
        for peer in slab_peers:
            pltpu.make_async_remote_copy(
                src_ref=sent.at[plane, peer],
                dst_ref=ext.at[slot, me],
                send_sem=send_sem.at[sem],
                recv_sem=recv_sem.at[sem],
                device_id={"phase": peer, "space": target},
                device_id_type=MESH,
            ).start()

    def arrived(ref, sem):
        pltpu.make_async_copy(ref, ref, sem).wait()

    others = got.at[0, pl.ds(0, bins - 1)]

    def owned(plane):
        pltpu.make_async_copy(
            sent.at[plane, me], ext.at[reach + plane, me], own_sem.at[plane]
        ).wait()
        arrived(others, recv_sem.at[4 + plane])

    own_in.wait()
    for copy in weight_copies[:3]:
        copy.wait()
    arrived(others, recv_sem.at[1])
    attend(1)
    arrived(others, recv_sem.at[2])
    to_slab(1, partner_slot, partner, 8)
    to_owner(1)
    attend(2)
    arrived(others, recv_sem.at[0])
    to_slab(2, partner_slot + 1, partner, 9)
    to_owner(2)
    attend(0)
    arrived(others, recv_sem.at[3])
    to_owner(0)
    attend(3)
    to_owner(3)

    @pl.when(not_first)
    def _():
        to_slab(0, high, slab - 1, 10)

    @pl.when(not_last)
    def _():
        to_slab(3, low + reach - 1, slab + 1, 11)

    def forward(i):
        return pltpu.make_async_remote_copy(
            src_ref=ext.at[held_slot + i],
            dst_ref=ext.at[partner_slot + i],
            send_sem=send_sem.at[12 + i],
            recv_sem=recv_sem.at[12 + i],
            device_id={"space": onward},
            device_id_type=MESH,
        )

    for copy in weight_copies[3:5]:
        copy.wait()

    def banded(target, plane, rows):
        blocked = rows.reshape(4, 4, 8, 256)
        for b in range(4):
            near = blocked[:, b : b + 1]
            far = blocked[:, (b + 1) % 4 : (b + 1) % 4 + 1]
            target[plane, b] = jnp.concatenate([near, far], axis=1).reshape(64, 256).astype(BF16)

    def project(plane, inner):
        stream = ext[plane].astype(F32).reshape(128, 256)
        if inner is None:
            pair = dot(normed(stream, gain2[...]), w_qkv2[:, 256:])
        else:
            triple = dot(normed(stream, gain2[...]), w_qkv2[...])
            turned = [pltpu.roll(triple[32 * x : 32 * x + 32, :256], 28, 0) for x in range(4)]
            for b in range(4):
                queries[inner, 32 * b : 32 * b + 32] = jnp.concatenate(
                    [turned[x][8 * b : 8 * b + 8] for x in range(4)], axis=0
                ).astype(BF16)
            pair = triple[:, 256:]
        banded(keys, plane, pair[:, :256])
        banded(values, plane, pair[:, 256:])

    depth = planes * slabs

    def entries(query_planes, key_planes):
        found = []
        for h in range(heads):
            rows = []
            for g in query_planes:
                steps = []
                for k in key_planes:
                    a = k - g - corner[0, h]
                    z = slab * planes + k
                    usable = (a >= 0) & (a < 4) & (z >= 0) & (z < depth)
                    steps.append(jnp.where(usable, a, 4))
                rows.append([5 * steps[j] + steps[j + 1] for j in range(0, len(steps), 2)])
            found.append(rows)
        return found

    def look(query_planes, key_planes, merge):
        entry = entries(query_planes, key_planes)
        count = len(query_planes)
        size = 32 * count
        for t in range(2):
            lanes = slice(128 * t, 128 * t + 128)
            for b in range(4):
                q = jnp.concatenate([queries[g, 32 * b : 32 * b + 32, lanes] for g in query_planes], axis=0)
                stacked = jnp.concatenate([q * keep for keep in head_keep], axis=0)
                k = jnp.concatenate([keys[p + reach, b, :, lanes] for p in key_planes], axis=0)
                v = jnp.concatenate([values[p + reach, b, :, lanes] for p in key_planes], axis=0)
                both = jnp.concatenate([v, jnp.ones(v.shape, BF16)], axis=1)
                table = jnp.concatenate(
                    [
                        jnp.concatenate([window_table[2 * h + b // 3, e] for e in rows], axis=1)
                        for h in range(4 * t, 4 * t + 4)
                        for rows in entry[h]
                    ],
                    axis=0,
                )
                z = dot_t(stacked, k) + table
                peak = jnp.max(z, axis=1, keepdims=True)
                weight = jnp.exp2((z - peak) * rate).astype(BF16)
                summed = dot(weight, both)
                top = summed[:size, :128]
                low = summed[:size, 128:]
                high = jnp.broadcast_to(peak[:size], (size, 128))
                for i in range(1, 4):
                    part = slice(size * i, size * i + size)
                    top = jnp.where(head_lanes[i], summed[part, :128], top)
                    low = jnp.where(head_lanes[i], summed[part, 128:], low)
                    high = jnp.where(head_lanes[i], peak[part], high)
                top = top.reshape(count, 32, 128)
                low = low.reshape(count, 32, 128)
                high = high.reshape(count, 32, 128)
                at = (t, b, pl.ds(query_planes[0], count))
                if merge:
                    before = highs[at]
                    peak = jnp.maximum(before, high)
                    old = jnp.exp2((before - peak) * rate)
                    new = jnp.exp2((high - peak) * rate)
                    top = tops[at] * old + top * new
                    low = lows[at] * old + low * new
                    high = peak
                tops[at] = top
                lows[at] = low
                highs[at] = high

    for i in range(2):
        arrived(ext.at[0], recv_sem.at[8 + i])

        @pl.when(sends_on)
        def _():
            forward(i).start()

        owned(1 + i)
        project(held_slot + i, None)
        project(reach + 1 + i, 1 + i)
    owned(0)
    owned(3)
    for g in (0, 3):
        project(reach + g, g)

    look(range(planes), range(planes), False)

    @pl.when(not_first)
    def _():
        arrived(ext.at[0], recv_sem.at[11])

    @pl.when(not_last)
    def _():
        arrived(ext.at[0], recv_sem.at[10])

    @pl.when(takes)
    def _():
        arrived(ext.at[0], recv_sem.at[12])
        arrived(ext.at[0], recv_sem.at[13])

    for slot in (low + reach - 1, high):
        project(slot, None)
    for i in range(2):
        project(partner_slot + i, None)

    for copy in weight_copies[5:]:
        copy.wait()
    ahead = jnp.where(even, 2, 0)
    behind = 2 - ahead
    look([ahead, ahead + 1], [held_slot - reach, held_slot - reach + 1, -1, planes], True)
    def finish(first):
        rows = []
        for j in range(2):
            tiles = []
            for t in range(2):
                share = [tops[t, b, first + j] / lows[t, b, first + j] for b in range(4)]
                turned = [
                    jnp.concatenate([share[b][8 * x : 8 * x + 8] for b in range(4)], axis=0) for x in range(4)
                ]
                tiles.append(jnp.concatenate([pltpu.roll(part, 4, 0) for part in turned], axis=0))
            rows.append(jnp.concatenate(tiles, axis=1))
        mixed = jnp.concatenate(rows, axis=0).astype(BF16)
        stream = ext[pl.ds(reach + first, 2)].astype(F32).reshape(256, 256)
        residual = stream + dot(mixed, w_out2[...])
        rise = dot(normed(residual, gain3[...]), w_up[...])
        slope = math.sqrt(2.0 / math.pi)
        bend = jnp.tanh(rise * (slope + (0.044715 * slope) * (rise * rise)))
        level = 0.5 * rise
        hidden = level + level * bend
        final = residual + dot(hidden.astype(BF16), w_down[...])
        out[pl.ds(first, 2)] = final.astype(BF16).reshape(2, 128, 256)


    look([behind, behind + 1], [partner_slot - reach, partner_slot - reach + 1, -1, planes], True)
    finish(0)
    finish(2)

    for sem in range(8):
        arrived(others, send_sem.at[sem])
    for sem in (8, 9):
        arrived(ext.at[0], send_sem.at[sem])

    @pl.when(not_first)
    def _():
        arrived(ext.at[0], send_sem.at[10])

    @pl.when(not_last)
    def _():
        arrived(ext.at[0], send_sem.at[11])

    @pl.when(sends_on)
    def _():
        forward(0).wait_send()
        forward(1).wait_send()


def solution(mesh):
    bins, slabs = mesh.shape["phase"], mesh.shape["space"]

    def local(
        volume,
        gain_first,
        phase_qkv,
        phase_out,
        bin_phase,
        phase_bias,
        gain_second,
        window_qkv,
        window_out,
        window_corner,
        window_bias,
        gain_third,
        mlp_up,
        mlp_down,
    ):
        _, planes, extent_x, extent_y, width = volume.shape
        tokens = extent_x * extent_y
        blocks = tokens // 8
        reach = planes - 1
        deep = planes + 2 * reach
        vmem = pl.BlockSpec(memory_space=pltpu.VMEM)
        hbm = pl.BlockSpec(memory_space=pl.ANY)
        weights = (phase_qkv, phase_out, window_qkv, window_out, mlp_up, mlp_down)
        result = pl.pallas_call(
            functools.partial(kernel, bins, slabs),
            out_shape=pltpu.VMEM((planes, tokens, width), BF16),
            in_specs=[hbm] * 14,
            out_specs=vmem,
            scratch_shapes=[
                pltpu.SMEM(bin_phase.shape, jnp.int32),
                pltpu.SMEM(phase_bias.shape, F32),
                pltpu.SMEM(window_corner.shape[::-1], jnp.int32),
                pltpu.SMEM(window_bias.shape, F32),
            ]
            + [pltpu.VMEM((1, width), F32)] * 3
            + [pltpu.VMEM(w.shape, BF16) for w in weights]
            + [
                pltpu.VMEM((planes, blocks, 8, width), BF16),
                pltpu.VMEM((planes, blocks, 8, width), BF16),
                pltpu.VMEM((deep, blocks, 8, width), BF16),
                pltpu.VMEM((planes, tokens, width), BF16),
                pltpu.VMEM((deep, 4, 64, width), BF16),
                pltpu.VMEM((deep, 4, 64, width), BF16),
                pltpu.VMEM((8, 128, 128), F32),
                pltpu.VMEM((16, 25, 32, 128), F32),
                pltpu.VMEM((2, 4, planes, 32, 128), F32),
                pltpu.VMEM((2, 4, planes, 32, 128), F32),
                pltpu.VMEM((2, 4, planes, 32, 128), F32),
                pltpu.SemaphoreType.DMA((4,)),
                pltpu.SemaphoreType.DMA((9,)),
                pltpu.SemaphoreType.DMA((4,)),
                pltpu.SemaphoreType.DMA((4,)),
                pltpu.SemaphoreType.DMA((14,)),
                pltpu.SemaphoreType.DMA((14,)),
            ],
            compiler_params=pltpu.CompilerParams(collective_id=0, has_side_effects=True),
        )(
            bin_phase,
            phase_bias,
            window_corner.T,
            window_bias,
            gain_first.reshape(1, width),
            gain_second.reshape(1, width),
            gain_third.reshape(1, width),
            volume.reshape(planes, blocks, 8, width),
            *weights,
        )
        return result.reshape(volume.shape)

    split = P("phase", "space", None, None, None)
    return jax.shard_map(
        local,
        mesh=mesh,
        in_specs=(split,) + (P(),) * 13,
        out_specs=split,
        check_vma=False,
    )
```
